32 devices in a mesh: flow: 8 (over y, x, core), grad: 4 (over z).
Axes of the slice: x: 2, y: 2, z: 4, core: 2. Of those that a mesh axis runs over, the one named last changes fastest.
Arguments:
- positions: float32 [3, 4, 2048], P(None, 'grad', 'flow'), may hold values from 0 to 1
- features: float32 [4, 128, 2048], P('grad', None, 'flow'), may hold values from -6 to 6
- neighbours: int32 [4, 32, 2048], P('grad', None, 'flow'), may hold values from 0 to 1279, as said below
- face_blocks: int32 [4, 4, 16], P('grad', None, 'flow'), may hold values from 0 to 1
- shear_cells: int32 [1], replicated, may hold values from 0 to 7
- split_block: int32 [1], replicated, may hold values from 0 to 2
- radial_in: float32 [8, 64], replicated, may hold values from -2 to 2
- radial_out: float32 [64, 128], replicated, may hold values from -0.75 to 0.75
- mixing: float32 [3, 128, 128], replicated, may hold values from -0.3125 to 0.3125
- readout: float32 [128], replicated, may hold values from -0.5 to 0.5
Outputs:
- atom_energy: float32 [4, 2048], P('grad', 'flow')
- forces: float32 [3, 4, 2048], P(None, 'grad', 'flow')
The draws below stay inside these ranges and needn't reach their ends.
Inputs may be any that keep to these rules, and one draw needn't show every extreme that they name: `neighbours`: each atom's 32 entries index its cell's extended list: the 256 own atoms, then 2 * 128 ghost atoms from each of the flow-lower, flow-upper, grad-lower and grad-upper sides, in that order. An atom never lists itself; entries may repeat. `face_blocks`: row k of a cell lists blocks of its own atoms that it shares: face 0 with the flow-upper cell, 1 with the flow-lower, 2 with the grad-upper, 3 with the grad-lower. Entries may repeat.
All inputs are finite; a program needn't handle non-finite values.
Results may differ from the reference program's by a relative error of at most 0.0003.
Values sent between devices are 32-bit elements; how exact they have to be, the bound alone decides.
No kernel may reach another device: no remote copies, remote signals or barrier semaphores. Data moves between devices by JAX's collectives and lax.ppermute only.
A program may use at most 64 MiB of HBM per device.

```python
import jax
import jax.numpy as jnp
from jax import lax

CH = 128
RHID = 64
NRAD = 8
NEIGH = 32
BLOCK = 128
GHOST_BLK = 2
ATOMS_DEV = 256
ATOMS = 2048
EXTENDED = 1280
N_FLOW = 8
N_GRAD = 4


def draw_neighbours(key, part):
    picks = jax.random.randint(key, (N_GRAD, NEIGH, ATOMS), 0, EXTENDED - 1)
    owned = jnp.arange(ATOMS, dtype=jnp.int32) % ATOMS_DEV
    return jnp.where(picks >= owned[None, None, :], picks + 1, picks).astype(jnp.int32)


def touch_ends(values, key, smallest, high):
    extent = values.shape
    place = [jax.random.randint(jax.random.fold_in(key, axis), (), 0, extent[axis]) for axis in range(len(extent))]
    values = values.at[tuple(place)].set(smallest)
    longest = extent.index(max(extent))
    place[longest] = (place[longest] + 1) % extent[longest]
    return values.at[tuple(place)].set(high)


def block_levels(own_key, shape, cuts, low, high):
    def one(position, blocks):
        steps = jax.random.uniform(jax.random.fold_in(jax.random.fold_in(own_key, 6), position), (blocks,), jnp.float32, low / len(cuts), high / len(cuts))
        return jnp.repeat(jnp.exp(steps), shape[position] // blocks).reshape((-1,) + (1,) * (len(shape) - position - 1))

    gain = one(*cuts[0])
    for cut in cuts[1:]:
        gain = gain * one(*cut)
    return gain


def centred(rng, shape, spread, most, cuts=(), kind=jnp.bfloat16):
    drawn = jax.random.normal(rng, shape, jnp.float32) * spread
    if len(cuts) > 0:
        drawn = block_levels(rng, shape, cuts, -0.22, 0.18) * drawn
    return jnp.clip(drawn, min=-most, max=most).astype(kind)


def setup_inputs(seed: int = 0) -> dict:
    streams_of = jax.random.split(jax.random.key(seed), 11)
    positions = jnp.clip(1.0 * jax.random.uniform(streams_of[0], (3, N_GRAD, ATOMS), jnp.float32) ** block_levels(streams_of[0], (3, N_GRAD, ATOMS), ((1, 4), (2, 8)), -0.2, 0.2), 0.0, 1.0)
    features = centred(streams_of[1], (N_GRAD, CH, ATOMS), 1.0, 6.0, ((0, 4), (2, 8)), jnp.float32)
    neighbours = draw_neighbours(jax.random.fold_in(streams_of[10], 71), 0)
    face_blocks = touch_ends(jax.random.randint(streams_of[3], (N_GRAD, 4, N_FLOW * GHOST_BLK), 0, ATOMS_DEV // BLOCK), jax.random.fold_in(streams_of[3], 1), 0, (ATOMS_DEV // BLOCK) - 1).astype(jnp.int32)
    shear_cells = jax.random.randint(streams_of[4], (1,), 0, N_FLOW).astype(jnp.int32)
    split_block = jax.random.randint(streams_of[5], (1,), 0, GHOST_BLK + 1).astype(jnp.int32)
    radial_in = centred(streams_of[6], (NRAD, RHID), NRAD ** -0.5, 2.0, (), jnp.float32)
    radial_out = centred(streams_of[7], (RHID, CH), RHID ** -0.5, 0.75, (), jnp.float32)
    mixing = centred(streams_of[8], (3, CH, CH), (3 * CH) ** -0.5, 0.3125, (), jnp.float32)
    readout = centred(streams_of[9], (CH,), CH ** -0.5, 0.5, (), jnp.float32)
    return {"positions": positions, "features": features, "neighbours": neighbours, "face_blocks": face_blocks, "shear_cells": shear_cells, "split_block": split_block, "radial_in": radial_in, "radial_out": radial_out, "mixing": mixing, "readout": readout}


highest = lax.Precision.HIGHEST
root_three = 3.0 ** 0.5
root_five = 5.0 ** 0.5
root_fifteen = 15.0 ** 0.5

def harmonics(separation):
    xcoord = separation[0]
    ycoord = separation[1]
    zcoord = separation[2]
    square = xcoord * xcoord + ycoord * ycoord + zcoord * zcoord
    values = [jnp.ones_like(xcoord), root_three * xcoord, root_three * ycoord, root_three * zcoord, root_fifteen * xcoord * ycoord, root_fifteen * ycoord * zcoord, 0.5 * root_five * (3.0 * zcoord * zcoord - square), root_fifteen * xcoord * zcoord, 0.5 * root_fifteen * (xcoord * xcoord - ycoord * ycoord)]
    return (jnp.stack(values), square)

def contribution(centre, group_pos, group_idx, features_all, radial_in, radial_out):
    separation = group_pos - centre[:, None, :]
    harmonic, square = harmonics(separation)
    number = radial_in.shape[0]
    centres = jnp.arange(number, dtype=jnp.int32).astype(jnp.float32) * (6.0 / (number - 1))
    gaussians = jnp.exp(-0.5 * jnp.square((square[None] - centres[:, None, None]) / 0.75))
    hidden = jax.nn.silu(jnp.einsum('rh,rgb->hgb', radial_in, gaussians, precision=highest))
    radial = jnp.einsum('hc,hgb->cgb', radial_out, hidden, precision=highest)
    weighted = radial * jnp.take(features_all, group_idx, axis=1)
    return jnp.einsum('cgb,mgb->mcb', weighted, harmonic, precision=highest)

def readout_energy(moments, mixing, readout):
    squared = moments * moments
    invariants = jnp.stack([squared[0], squared[1] + squared[2] + squared[3], lax.optimization_barrier(jnp.sum(squared[4:], axis=0))])
    mixed = jnp.einsum('lcd,lcb->db', mixing, invariants, precision=highest)
    return jnp.einsum('d,db->b', readout, jax.nn.silu(mixed), precision=highest)

def block_pass(centre, others, chosen, features_all, radial_in, radial_out, mixing, readout):
    neigh_count = chosen.shape[0]
    width = chosen.shape[1]
    grouping = 8
    rounds = neigh_count // grouping
    other_groups = others.reshape(3, rounds, grouping, width).transpose(1, 0, 2, 3)
    chosen_groups = chosen.reshape(rounds, grouping, width)
    factor = neigh_count ** (-0.5)

    def forward(running, pieces):
        return (running + contribution(centre, pieces[0], pieces[1], features_all, radial_in, radial_out), None)
    starting = jnp.zeros((9, features_all.shape[0], width), jnp.float32)
    summed, _ = lax.scan(forward, starting, (other_groups, chosen_groups))
    moments = summed * factor

    def head(moments_value):
        return readout_energy(moments_value, mixing, readout)
    energy, pullback = jax.vjp(head, moments)
    cotangent, = pullback(jnp.ones_like(energy))
    cotangent = cotangent * factor

    def backward(grad_centre, pieces):
        group_idx = pieces[1]

        def local(centre_value, group_value):
            return contribution(centre_value, group_value, group_idx, features_all, radial_in, radial_out)
        _, pullback_group = jax.vjp(local, centre, pieces[0])
        centre_grad, group_grad = pullback_group(cotangent)
        return (grad_centre + centre_grad, group_grad)
    grad_centre, grad_groups = lax.scan(backward, jnp.zeros_like(centre), (other_groups, chosen_groups))
    grad_others = grad_groups.transpose(1, 0, 2, 3).reshape(3, neigh_count, width)
    return (energy, grad_centre, grad_others)

def device_pass(ext_pos, features_all, neigh, radial_in, radial_out, mixing, readout, block):
    atom_count = neigh.shape[1]
    number = atom_count // block

    def step(gradient, step_index):
        anchor = step_index * block
        chosen = lax.dynamic_slice_in_dim(neigh, anchor, block, 1)
        centre = lax.dynamic_slice_in_dim(ext_pos, anchor, block, 1)
        others = jnp.take(ext_pos, chosen, axis=1)
        energy, grad_centre, grad_others = block_pass(centre, others, chosen, features_all, radial_in, radial_out, mixing, readout)
        gradient = gradient.at[:, chosen].add(grad_others)
        current = lax.dynamic_slice_in_dim(gradient, anchor, block, 1)
        gradient = lax.dynamic_update_slice_in_dim(gradient, current + grad_centre, anchor, 1)
        return (gradient, energy)
    gradient, energies = lax.scan(step, jnp.zeros(ext_pos.shape, jnp.float32), jnp.arange(number, dtype=jnp.int32))
    return (energies.reshape(-1), gradient)

def extended_atoms(face_blocks, row, columns, face, slots):
    listed = face_blocks[row, face][columns * GHOST_BLK + slots]
    firsts = (row * N_FLOW + columns) * ATOMS_DEV + listed * BLOCK
    return (firsts[:, None] + jnp.arange(BLOCK, dtype=jnp.int32)[None, :]).reshape(-1)

def reference(positions, features, neighbours, face_blocks, shear_cells, split_block, radial_in, radial_out, mixing, readout):
    flat_pos = positions.reshape(3, -1)
    flat_feat = jnp.transpose(features, (1, 0, 2)).reshape(features.shape[1], -1)
    offset = shear_cells[0]
    split = split_block[0]
    fraction = split.astype(jnp.float32) / GHOST_BLK
    slots = jnp.arange(GHOST_BLK, dtype=jnp.int32)
    ghost_rows = GHOST_BLK * BLOCK

    def device_step(forces, device):
        row = device // N_FLOW
        column = device % N_FLOW
        same = jnp.zeros_like(slots) + column
        owned = (row * N_FLOW + column) * ATOMS_DEV + jnp.arange(ATOMS_DEV, dtype=jnp.int32)
        left = extended_atoms(face_blocks, row, (same - 1) % N_FLOW, 0, slots)
        right = extended_atoms(face_blocks, row, (same + 1) % N_FLOW, 1, slots)
        low_wrap = row == 0
        low_early = slots < split
        low_cols = jnp.where(low_wrap, jnp.where(low_early, same - offset - 1, same - offset), same) % N_FLOW
        low_slots = jnp.where(low_wrap, jnp.where(low_early, slots + GHOST_BLK - split, slots - split), slots)
        low_shift = jnp.where(low_wrap, jnp.where(low_early, fraction - 1.0, fraction), 0.0)
        lower = extended_atoms(face_blocks, (row - 1) % N_GRAD, low_cols, 2, low_slots)
        high_wrap = row == N_GRAD - 1
        high_early = slots < GHOST_BLK - split
        high_cols = jnp.where(high_wrap, jnp.where(high_early, same + offset, same + offset + 1), same) % N_FLOW
        high_slots = jnp.where(high_wrap, jnp.where(high_early, slots + split, slots + split - GHOST_BLK), slots)
        high_shift = jnp.where(high_wrap, jnp.where(high_early, -fraction, 1.0 - fraction), 0.0)
        upper = extended_atoms(face_blocks, (row + 1) % N_GRAD, high_cols, 3, high_slots)
        indices = jnp.concatenate([owned, left, right, lower, upper])
        blank = jnp.zeros((ghost_rows,), jnp.float32)
        xshift = jnp.concatenate([jnp.zeros((ATOMS_DEV,), jnp.float32), blank - 1.0, blank + 1.0, jnp.repeat(low_shift, BLOCK), jnp.repeat(high_shift, BLOCK)])
        yshift = jnp.concatenate([jnp.zeros((ATOMS_DEV,), jnp.float32), blank, blank, blank - 1.0, blank + 1.0])
        shifts = jnp.stack([xshift, yshift, jnp.zeros_like(xshift)])
        ext_pos = flat_pos[:, indices] + shifts
        features_all = flat_feat[:, indices]
        neigh = lax.dynamic_slice_in_dim(neighbours[row], column * ATOMS_DEV, ATOMS_DEV, 1)
        energies, gradient = device_pass(ext_pos, features_all, neigh, radial_in, radial_out, mixing, readout, BLOCK)
        forces = forces.at[:, indices].add(-gradient)
        return (forces, energies)
    forces, energies = lax.scan(device_step, jnp.zeros(flat_pos.shape, jnp.float32), jnp.arange(N_GRAD * N_FLOW, dtype=jnp.int32))
    return (energies.reshape(N_GRAD, N_FLOW * ATOMS_DEV), forces.reshape(3, N_GRAD, N_FLOW * ATOMS_DEV))
```

```python
import functools

import jax
import jax.numpy as jnp
from jax import lax
from jax.experimental import pallas as pl
from jax.experimental.pallas import tpu as pltpu
from jax.sharding import PartitionSpec as P

LANES = 128
GROUPS = 8
highest = lax.Precision.HIGHEST
root_three = 3.0**0.5
root_five = 5.0**0.5
root_fifteen = 15.0**0.5
f32 = jnp.float32
bf16 = jnp.bfloat16


def halves(value):
    upper = value.astype(bf16).astype(f32)
    return upper, value - upper


def nt(left, right, precision=None):
    return lax.dot_general(left, right, (((1,), (1,)), ((), ())), precision=precision, preferred_element_type=f32)


def core_kernel(groups, neighbours, number, rows, ghost, split_ref, row_ref, idx_ref, own_pos, own_feat,
                win_ref, wout_ref, mix_ref, read_ref, left_ref, right_ref, *refs):
    slot_refs, refs = refs[: 2 * ghost], refs[2 * ghost :]
    energy_ref, own_ref, ghost_ref = refs[:3]
    xyz_scr, d_scr, w_scr, dw_scr, mom_scr, g_scr, acc_scr, cen_scr = refs[3:]
    split = split_ref[0]
    row = row_ref[0]
    atoms = own_pos.shape[1]
    channels = own_feat.shape[0]
    hidden = win_ref.shape[1]
    tile = groups * neighbours
    tiles = atoms // groups
    own_chunks = atoms // LANES
    faces = 4
    chunks = own_chunks + faces * ghost
    factor = neighbours ** (-0.5)
    ghosts = [left_ref.at[j] for j in range(ghost)] + [right_ref.at[j] for j in range(ghost)] + list(slot_refs)

    def pos_chunk(c, axis):
        if c < own_chunks:
            return own_pos[axis : axis + 1, c * LANES : (c + 1) * LANES]
        k, j = divmod(c - own_chunks, ghost)
        line = ghosts[c - own_chunks][channels + axis : channels + axis + 1, :]
        fraction = split.astype(f32) / ghost
        if axis == 0:
            if k < 2:
                line = line + (2.0 * k - 1.0)
            elif k == 2:
                line = line + jnp.where(row == 0, jnp.where(j < split, fraction - 1.0, fraction), 0.0)
            else:
                line = line + jnp.where(
                    row == rows - 1, jnp.where(j < ghost - split, -fraction, 1.0 - fraction), 0.0
                )
        elif axis == 1 and k >= 2:
            line = line + (2.0 * k - 5.0)
        return line

    def feat_chunk(c):
        if c < own_chunks:
            return own_feat[:, c * LANES : (c + 1) * LANES]
        return ghosts[c - own_chunks][0:channels, :]

    blocks = tile // LANES
    for lb in range(blocks):
        lanes = slice(lb * LANES, (lb + 1) * LANES)
        idx = idx_ref[:, lanes]
        low = jnp.bitwise_and(idx, LANES - 1)
        chunk = jnp.right_shift(idx, LANES.bit_length() - 1)
        lines = lax.broadcasted_iota(jnp.int32, idx.shape, 0)
        cols = lax.broadcasted_iota(jnp.int32, idx.shape, 1) + lb * LANES
        centre = lines * groups + cols // neighbours
        clow = jnp.bitwise_and(centre, LANES - 1)
        cchunk = jnp.right_shift(centre, LANES.bit_length() - 1)
        for axis in range(3):
            other = None
            mine = None
            for c in range(chunks):
                src = jnp.broadcast_to(pos_chunk(c, axis), idx.shape)
                got = jnp.take_along_axis(src, low, axis=1)
                other = got if other is None else jnp.where(chunk == c, got, other)
                if c < own_chunks:
                    got = jnp.take_along_axis(src, clow, axis=1)
                    mine = got if mine is None else jnp.where(cchunk == c, got, mine)
            xyz_scr[axis, :, lanes] = other - mine

    d_scr[...] = jnp.zeros(d_scr.shape, f32)
    d_scr[0:number, 0:hidden] = win_ref[...]
    d_scr[number : 2 * number, hidden : 2 * hidden] = win_ref[...]
    dhi, dlo = halves(d_scr[...])
    first = jnp.transpose(jnp.concatenate([dhi, dhi, dlo, dlo], axis=0)).astype(bf16)
    ohi, olo = halves(wout_ref[...])
    second = jnp.transpose(jnp.concatenate([ohi, ohi, olo, olo], axis=0)).astype(bf16)

    row_iota = lax.broadcasted_iota(jnp.int32, (groups, tile), 0)
    lane_iota = lax.broadcasted_iota(jnp.int32, (groups, tile), 1)
    mine_mask = row_iota == lane_iota // neighbours
    centres = row_iota.astype(f32) * (6.0 / (number - 1))

    def spread(axis, t):
        return jnp.broadcast_to(xyz_scr[axis, pl.ds(t, 1), :], (groups, tile))

    def harmonics(x, y, z):
        square = x * x + y * y + z * z
        values = [
            jnp.ones_like(x),
            root_three * x,
            root_three * y,
            root_three * z,
            root_fifteen * x * y,
            root_fifteen * y * z,
            0.5 * root_five * (3.0 * z * z - square),
            root_fifteen * x * z,
            0.5 * root_fifteen * (x * x - y * y),
        ]
        return values, square

    def forward(t, carry):
        x, y, z = spread(0, t), spread(1, t), spread(2, t)
        values, square = harmonics(x, y, z)
        away = square - centres
        scaled = away / 0.75
        gauss = jnp.exp(-0.5 * (scaled * scaled))
        slope = gauss * (away * (-1.0 / 0.5625))
        bhi, blo = halves(jnp.concatenate([gauss, slope], axis=0))
        basis = jnp.concatenate([bhi, blo, bhi, blo], axis=0).astype(bf16)
        both = jnp.dot(first, basis, preferred_element_type=f32)
        h, dh = both[0:hidden], both[hidden : 2 * hidden]
        sig = 0.5 * jnp.tanh(0.5 * h) + 0.5
        act = h * sig
        dact = dh * (sig + act * (1.0 - sig))
        ahi, alo = halves(act)
        acts = jnp.concatenate([ahi, alo, ahi, alo], axis=0).astype(bf16)
        chi, clo = halves(dact)
        dacts = jnp.concatenate([chi, clo, chi, clo], axis=0).astype(bf16)
        radial = jnp.dot(second, acts, preferred_element_type=f32)
        dradial = jnp.dot(second, dacts, preferred_element_type=f32)
        idx_row = idx_ref[pl.ds(t, 1), :]
        for lb in range(blocks):
            lanes = slice(lb * LANES, (lb + 1) * LANES)
            idx = jnp.broadcast_to(idx_row[:, lanes], (channels, LANES))
            low = jnp.bitwise_and(idx, LANES - 1)
            chunk = jnp.right_shift(idx, LANES.bit_length() - 1)
            feat = None
            for c in range(chunks):
                got = jnp.take_along_axis(feat_chunk(c), low, axis=1)
                feat = got if feat is None else jnp.where(chunk == c, got, feat)
            whi, wlo = halves(radial[:, lanes] * feat)
            w_scr[t, 0:channels, lanes] = whi.astype(bf16)
            w_scr[t, channels : 2 * channels, lanes] = wlo.astype(bf16)
            whi, wlo = halves(dradial[:, lanes] * feat)
            dw_scr[t, 0:channels, lanes] = whi.astype(bf16)
            dw_scr[t, channels : 2 * channels, lanes] = wlo.astype(bf16)
        his, los = [], []
        for value in values:
            hi, lo = halves(jnp.where(mine_mask, value, 0.0))
            his.append(hi)
            los.append(lo)
        ys = jnp.concatenate(his + los, axis=0).astype(bf16)
        out = nt(ys, w_scr[t])
        n = len(values) * groups
        total = (out[0:n, 0:channels] + out[0:n, channels:]) + out[n : 2 * n, 0:channels]
        base = pl.multiple_of(t * groups, groups)
        for m in range(len(values)):
            mom_scr[m, pl.ds(base, groups), :] = total[m * groups : (m + 1) * groups] * factor
        return carry

    lax.fori_loop(0, tiles, forward, 0)

    degree = [0, 1, 1, 1, 2, 2, 2, 2, 2]
    count = len(degree)
    invariants = []
    for l in range(3):
        total = None
        for m in range(count):
            if degree[m] == l:
                sq = mom_scr[m] * mom_scr[m]
                total = sq if total is None else total + sq
        invariants.append(total)
    mixed = None
    for l in range(3):
        part = jnp.dot(invariants[l], mix_ref[l], precision=highest, preferred_element_type=f32)
        mixed = part if mixed is None else mixed + part
    sig = 0.5 * jnp.tanh(0.5 * mixed) + 0.5
    act = mixed * sig
    reads = read_ref[...]
    energy_ref[...] = nt(jnp.broadcast_to(reads, (8, channels)), act, highest)[0:1]
    dmixed = reads * (sig + act * (1.0 - sig))
    for l in range(3):
        dinv = nt(dmixed, mix_ref[l], highest) * (2.0 * factor)
        for m in range(count):
            if degree[m] == l:
                hi, lo = halves(dinv * mom_scr[m])
                g_scr[:, m * groups : (m + 1) * groups, :] = hi.reshape(tiles, groups, channels)
                g_scr[:, (count + m) * groups : (count + m + 1) * groups, :] = lo.reshape(tiles, groups, channels)

    acc_scr[...] = jnp.zeros(acc_scr.shape, f32)
    padded = acc_scr.shape[0] // 6
    chunk_iota = lax.broadcasted_iota(jnp.int32, (padded, tile), 0)
    lane_rows = lax.broadcasted_iota(jnp.int32, (LANES, tile), 0)
    n = count * groups

    def backward(t, carry):
        x, y, z = spread(0, t), spread(1, t), spread(2, t)
        values, _ = harmonics(x, y, z)
        g = g_scr[t]
        gl = jnp.concatenate(
            [g.astype(bf16), jnp.concatenate([g[0:n], jnp.zeros((n, channels), f32)], axis=0).astype(bf16)], axis=1
        )
        a = jnp.dot(gl, w_scr[t], preferred_element_type=f32)
        b = jnp.dot(gl, dw_scr[t], preferred_element_type=f32)
        A = [a[m * groups : (m + 1) * groups] + a[n + m * groups : n + (m + 1) * groups] for m in range(count)]
        rad = None
        for m in range(count):
            B = b[m * groups : (m + 1) * groups] + b[n + m * groups : n + (m + 1) * groups]
            rad = B if m == 0 else rad + values[m] * B
        rad = 2.0 * rad
        dx = root_three * A[1] + root_fifteen * (y * A[4] + z * A[7] + x * A[8]) - root_five * (x * A[6]) + x * rad
        dy = root_three * A[2] + root_fifteen * (x * A[4] + z * A[5] - y * A[8]) - root_five * (y * A[6]) + y * rad
        dz = root_three * A[3] + root_fifteen * (y * A[5] + x * A[7]) + (2.0 * root_five) * (z * A[6]) + z * rad
        comps = [jnp.where(mine_mask, v, 0.0) for v in (dx, dy, dz)]
        base = pl.multiple_of(t * groups, groups)
        lane = lax.broadcasted_iota(jnp.int32, (groups, LANES), 1)
        cen = jnp.zeros((groups, LANES), f32)
        for i, v in enumerate(comps):
            cen = jnp.where(lane == i, jnp.sum(v, axis=1, keepdims=True), cen)
        cen_scr[pl.ds(base, groups), :] = cen
        idx = idx_ref[pl.ds(t, 1), :]
        low = jnp.bitwise_and(idx, LANES - 1)
        chunk = jnp.right_shift(idx, LANES.bit_length() - 1)
        hit = jnp.broadcast_to(chunk, (padded, tile)) == chunk_iota
        his, los = [], []
        for v in comps:
            row = jnp.sum(v, axis=0, keepdims=True)
            hi, lo = halves(jnp.where(hit, jnp.broadcast_to(row, (padded, tile)), 0.0))
            his.append(hi)
            los.append(lo)
        left = jnp.concatenate(his + los, axis=0).astype(bf16)
        right = jnp.where(jnp.broadcast_to(low, (LANES, tile)) == lane_rows, 1.0, 0.0).astype(bf16)
        acc_scr[...] += nt(left, right)
        return carry

    lax.fori_loop(0, tiles, backward, 0)

    half = 3 * padded
    cen = jnp.concatenate(
        [jnp.transpose(cen_scr[c * LANES : (c + 1) * LANES, :])[0:8] for c in range(own_chunks)], axis=1
    )
    for axis in range(3):
        lo = axis * padded
        rows = acc_scr[lo : lo + padded] + acc_scr[half + lo : half + lo + padded]
        for c in range(own_chunks):
            own_ref[axis : axis + 1, c * LANES : (c + 1) * LANES] = (
                rows[c : c + 1] - cen[axis : axis + 1, c * LANES : (c + 1) * LANES]
            )
        for k in range(faces):
            for j in range(ghost):
                c = own_chunks + k * ghost + j
                ghost_ref[k, j, axis : axis + 1, :] = rows[c : c + 1]


def core(split, row, idx, own_pos, own_feat, win, wout, mixing, readout, left, right, slots, rows):
    atoms = own_pos.shape[1]
    channels = own_feat.shape[0]
    tiles, tile = idx.shape
    groups = GROUPS
    neighbours = tile // groups
    ghost = left.shape[0]
    faces = 4
    number, hidden = win.shape
    chunks = atoms // LANES + faces * ghost
    padded = -(-chunks // 16) * 16
    vm = pl.BlockSpec(memory_space=pltpu.VMEM)
    sm = pl.BlockSpec(memory_space=pltpu.SMEM)
    return pl.pallas_call(
        functools.partial(core_kernel, groups, neighbours, number, rows, ghost),
        out_shape=(
            jax.ShapeDtypeStruct((1, atoms), f32),
            jax.ShapeDtypeStruct((3, atoms), f32),
            jax.ShapeDtypeStruct((faces, ghost, 3, LANES), f32),
        ),
        in_specs=[sm, sm] + [vm] * (9 + 2 * ghost),
        out_specs=(vm, vm, vm),
        scratch_shapes=[
            pltpu.VMEM((3, tiles, tile), f32),
            pltpu.VMEM((2 * number, 2 * hidden), f32),
            pltpu.VMEM((tiles, 2 * channels, tile), bf16),
            pltpu.VMEM((tiles, 2 * channels, tile), bf16),
            pltpu.VMEM((9, atoms, channels), f32),
            pltpu.VMEM((tiles, 18 * groups, channels), f32),
            pltpu.VMEM((6 * padded, LANES), f32),
            pltpu.VMEM((atoms, LANES), f32),
        ],
        compiler_params=pltpu.CompilerParams(vmem_limit_bytes=32 << 20),
        name="core",
    )(split, row, idx, own_pos, own_feat, win, wout, mixing, readout, left, right, *slots)


def source_slot(slot, ghost, crossing, split, sign):
    rolled = lax.rem(slot + sign * split + ghost, ghost)
    return jnp.where(crossing, rolled, slot)


def pack_kernel(rows, split_ref, row_ref, faces_ref, pos_ref, feat_ref, left_ref, right_ref, *slot_refs):
    ghost = faces_ref.shape[1]
    channels = feat_ref.shape[0]
    split = split_ref[0]
    row = row_ref[0]

    def put(dest, block):
        lanes = pl.ds(pl.multiple_of(block * LANES, LANES), LANES)
        dest[0:channels, :] = feat_ref[:, lanes]
        dest[channels : channels + 3, :] = pos_ref[:, lanes]
        dest[channels + 3 :, :] = jnp.zeros((dest.shape[0] - channels - 3, LANES), f32)

    for j in range(ghost):
        put(left_ref.at[j], faces_ref[0, j])
        put(right_ref.at[j], faces_ref[1, j])
        put(slot_refs[j], faces_ref[2, source_slot(j, ghost, row == rows - 1, split, -1)])
        put(slot_refs[ghost + j], faces_ref[3, source_slot(j, ghost, row == 0, split, 1)])


def pack(split, row, faces, pos, feat, rows):
    ghost = faces.shape[1]
    depth = feat.shape[0] + 8
    vm = pl.BlockSpec(memory_space=pltpu.VMEM)
    sm = pl.BlockSpec(memory_space=pltpu.SMEM)
    face = jax.ShapeDtypeStruct((ghost, depth, LANES), f32)
    slot = jax.ShapeDtypeStruct((depth, LANES), f32)
    outs = pl.pallas_call(
        functools.partial(pack_kernel, rows),
        out_shape=(face, face) + (slot,) * (2 * ghost),
        in_specs=[sm, sm, sm, vm, vm],
        out_specs=(vm,) * (2 + 2 * ghost),
        name="pack",
    )(split, row, faces, pos, feat)
    return outs[0], outs[1], outs[2:]


def row_permutation(rows, cols, upward, shift):
    pairs = []
    for g in range(rows):
        for c in range(cols):
            if upward:
                target = (g + 1, c) if g < rows - 1 else (0, (c + shift) % cols)
            else:
                target = (g - 1, c) if g > 0 else (rows - 1, (c - shift) % cols)
            pairs.append((c * rows + g, target[1] * rows + target[0]))
    return pairs


def slot_permutations(rows, cols, ghost, shift, split):
    perms = [row_permutation(rows, cols, True, shift + (1 if j < split else 0)) for j in range(ghost)]
    perms += [row_permutation(rows, cols, False, shift + (1 if j >= ghost - split else 0)) for j in range(ghost)]
    return perms


def crossing(slots, branch, rows, cols, ghost, back):
    def case(number):
        shift, split = divmod(number, ghost)
        perms = slot_permutations(rows, cols, ghost, shift, split)

        def route(values):
            outs = []
            for value, perm in zip(values, perms):
                pairs = [(b, a) for a, b in perm] if back else perm
                outs.append(lax.ppermute(value, ("flow", "grad"), pairs))
            return tuple(outs)

        return route

    return lax.switch(branch, [case(number) for number in range(cols * ghost)], tuple(slots))


def ring(value, by):
    peers = lax.axis_size("flow")
    return lax.ppermute(value, "flow", [(i, (i + by) % peers) for i in range(peers)])


def body(
    positions,
    features,
    neighbours,
    face_blocks,
    shear_cells,
    split_block,
    radial_in,
    radial_out,
    mixing,
    readout,
):
    own_pos = positions[:, 0, :]
    own_feat = features[0]
    faces = face_blocks[0]
    entries, atoms = neighbours.shape[1:]
    ghost = faces.shape[1]
    rows = lax.axis_size("grad")
    cols = lax.axis_size("flow")
    row = lax.axis_index("grad")
    row_array = row.astype(jnp.int32).reshape(1)
    split = split_block[0]
    whole = split // ghost
    branch = lax.rem(shear_cells[0] + whole, cols) * ghost + (split - whole * ghost)
    tile = GROUPS * entries
    idx = jnp.transpose(neighbours[0]).reshape(atoms // GROUPS, tile)

    left, right, slots = pack(split_block, row_array, faces, own_pos, own_feat, rows)
    left = ring(left, 1)
    right = ring(right, -1)
    slots = crossing(slots, branch, rows, cols, ghost, False)
    energy, own, ghosts = core(
        split_block, row_array, idx, own_pos, own_feat, radial_in, radial_out, mixing,
        readout.reshape(1, -1), left, right, slots, rows,
    )
    back_left = ring(ghosts[0], -1)
    back_right = ring(ghosts[1], 1)
    back = [ghosts[2, j] for j in range(ghost)] + [ghosts[3, j] for j in range(ghost)]
    back = crossing(back, branch, rows, cols, ghost, True)
    returned = [(faces[0, j], back_left[j]) for j in range(ghost)]
    returned += [(faces[1, j], back_right[j]) for j in range(ghost)]
    for j in range(ghost):
        returned.append((faces[2, source_slot(j, ghost, row == rows - 1, split, -1)], back[j]))
    for j in range(ghost):
        returned.append((faces[3, source_slot(j, ghost, row == 0, split, 1)], back[ghost + j]))
    blocks = []
    for number in range(atoms // LANES):
        total = own[:, number * LANES : (number + 1) * LANES]
        for block, value in returned:
            total = total + jnp.where(block == number, value, 0.0)
        blocks.append(-total)
    forces = jnp.concatenate(blocks, axis=1)
    return (energy, forces.reshape(3, 1, atoms))


def solution(mesh):
    in_specs = (
        P(None, "grad", "flow"),
        P("grad", None, "flow"),
        P("grad", None, "flow"),
        P("grad", None, "flow"),
        P(),
        P(),
        P(),
        P(),
        P(),
        P(),
    )
    out_specs = (P("grad", "flow"), P(None, "grad", "flow"))
    return jax.shard_map(body, mesh=mesh, in_specs=in_specs, out_specs=out_specs, check_vma=False)
```

```python
import functools

import jax
import jax.numpy as jnp
from jax import lax
from jax.experimental import pallas as pl
from jax.experimental.pallas import tpu as pltpu
from jax.sharding import PartitionSpec as P

LANES = 128
GROUPS = 8
highest = lax.Precision.HIGHEST
root_three = 3.0**0.5
root_five = 5.0**0.5
root_fifteen = 15.0**0.5
f32 = jnp.float32
bf16 = jnp.bfloat16


def halves(value):
    upper = value.astype(bf16).astype(f32)
    return upper, value - upper


def nt(left, right, precision=None):
    return lax.dot_general(left, right, (((1,), (1,)), ((), ())), precision=precision, preferred_element_type=f32)


def core_kernel(groups, rows, split_ref, row_ref, idx_ref, own_pos, own_feat, win_ref, wout_ref, mix_ref, read_ref,
                left_ref, right_ref, lower_ref, upper_ref,
                energy_ref, own_ref, back_left, back_right, back_lower, back_upper,
                xyz_scr, d_scr, f_scr, w_scr, dw_scr, mom_scr, g_scr, acc_scr, cen_scr):
    split = split_ref[0]
    row = row_ref[0]
    atoms = own_pos.shape[2]
    channels = own_feat.shape[1]
    number, hidden = win_ref.shape
    ghost = left_ref.shape[0]
    tiles, tile = idx_ref.shape
    neighbours = tile // groups
    own_chunks = atoms // LANES
    sides = (left_ref, right_ref, lower_ref, upper_ref)
    chunks = own_chunks + len(sides) * ghost
    factor = neighbours ** (-0.5)

    def pos_chunk(c, axis):
        if c < own_chunks:
            return own_pos[axis, :, c * LANES : (c + 1) * LANES]
        k, j = divmod(c - own_chunks, ghost)
        line = sides[k][j, channels + axis : channels + axis + 1, :]
        fraction = split.astype(f32) / ghost
        if axis == 0:
            if k < 2:
                line = line + (2.0 * k - 1.0)
            elif k == 2:
                line = line + jnp.where(row == 0, jnp.where(j < split, fraction - 1.0, fraction), 0.0)
            else:
                line = line + jnp.where(
                    row == rows - 1, jnp.where(j < ghost - split, -fraction, 1.0 - fraction), 0.0
                )
        elif axis == 1 and k >= 2:
            line = line + (2.0 * k - 5.0)
        return line

    blocks = tile // LANES
    for lb in range(blocks):
        lanes = slice(lb * LANES, (lb + 1) * LANES)
        idx = idx_ref[:, lanes]
        low = jnp.bitwise_and(idx, LANES - 1)
        chunk = jnp.right_shift(idx, LANES.bit_length() - 1)
        lines = lax.broadcasted_iota(jnp.int32, idx.shape, 0)
        cols = lax.broadcasted_iota(jnp.int32, idx.shape, 1) + lb * LANES
        centre = lines * groups + cols // neighbours
        clow = jnp.bitwise_and(centre, LANES - 1)
        cchunk = jnp.right_shift(centre, LANES.bit_length() - 1)
        for axis in range(3):
            other = None
            mine = None
            for c in range(chunks):
                src = jnp.broadcast_to(pos_chunk(c, axis), idx.shape)
                got = jnp.take_along_axis(src, low, axis=1)
                other = got if other is None else jnp.where(chunk == c, got, other)
                if c < own_chunks:
                    got = jnp.take_along_axis(src, clow, axis=1)
                    mine = got if mine is None else jnp.where(cchunk == c, got, mine)
            xyz_scr[axis, :, lanes] = other - mine

    d_scr[...] = jnp.zeros(d_scr.shape, f32)
    d_scr[0:number, 0:hidden] = win_ref[...]
    d_scr[number : 2 * number, hidden : 2 * hidden] = win_ref[...]
    dhi, dlo = halves(d_scr[...])
    first = jnp.transpose(jnp.concatenate([dhi, dhi, dlo, dlo], axis=0)).astype(bf16)
    ohi, olo = halves(wout_ref[...])
    second = jnp.transpose(jnp.concatenate([ohi, ohi, olo, olo], axis=0)).astype(bf16)

    for c in range(chunks):
        lanes = slice(c * LANES, (c + 1) * LANES)
        if c < own_chunks:
            feat = own_feat[0, :, lanes]
        else:
            k, j = divmod(c - own_chunks, ghost)
            feat = sides[k][j, 0:channels, :]
        hi, lo = halves(feat)
        f_scr[0:channels, lanes] = hi.astype(bf16)
        f_scr[channels : 2 * channels, lanes] = lo.astype(bf16)

    row_iota = lax.broadcasted_iota(jnp.int32, (groups, tile), 0)
    lane_iota = lax.broadcasted_iota(jnp.int32, (groups, tile), 1)
    mine_mask = row_iota == lane_iota // neighbours
    centres = row_iota.astype(f32) * (6.0 / (number - 1))

    entry_iota = lax.broadcasted_iota(jnp.int16, (chunks * LANES, tile), 0)

    def spread(axis, t):
        return jnp.broadcast_to(xyz_scr[axis, pl.ds(t, 1), :], (groups, tile))

    def harmonics(x, y, z):
        square = x * x + y * y + z * z
        values = [
            jnp.ones_like(x),
            root_three * x,
            root_three * y,
            root_three * z,
            root_fifteen * x * y,
            root_fifteen * y * z,
            0.5 * root_five * (3.0 * z * z - square),
            root_fifteen * x * z,
            0.5 * root_fifteen * (x * x - y * y),
        ]
        return values, square

    def forward(t, carry):
        x, y, z = spread(0, t), spread(1, t), spread(2, t)
        values, square = harmonics(x, y, z)
        away = square - centres
        scaled = away / 0.75
        gauss = jnp.exp(-0.5 * (scaled * scaled))
        slope = gauss * (away * (-1.0 / 0.5625))
        bhi, blo = halves(jnp.concatenate([gauss, slope], axis=0))
        basis = jnp.concatenate([bhi, blo, bhi, blo], axis=0).astype(bf16)
        both = jnp.dot(first, basis, preferred_element_type=f32)
        h, dh = both[0:hidden], both[hidden : 2 * hidden]
        sig = 0.5 * jnp.tanh(0.5 * h) + 0.5
        act = h * sig
        dact = dh * (sig + act * (1.0 - sig))
        ahi, alo = halves(act)
        acts = jnp.concatenate([ahi, alo, ahi, alo], axis=0).astype(bf16)
        chi, clo = halves(dact)
        dacts = jnp.concatenate([chi, clo, chi, clo], axis=0).astype(bf16)
        radial = jnp.dot(second, acts, preferred_element_type=f32)
        dradial = jnp.dot(second, dacts, preferred_element_type=f32)
        listed = jnp.broadcast_to(idx_ref[pl.ds(t, 1), :], (16, tile)).astype(jnp.int16)
        listed = jnp.concatenate([listed] * (chunks * LANES // 16), axis=0)
        picks = jnp.where(listed == entry_iota, jnp.ones((), bf16), jnp.zeros((), bf16))
        parts = jnp.dot(f_scr[...], picks, preferred_element_type=f32)
        feat = parts[0:channels] + parts[channels:]
        whi, wlo = halves(radial * feat)
        w_scr[t, 0:channels, :] = whi.astype(bf16)
        w_scr[t, channels : 2 * channels, :] = wlo.astype(bf16)
        whi, wlo = halves(dradial * feat)
        dw_scr[t, 0:channels, :] = whi.astype(bf16)
        dw_scr[t, channels : 2 * channels, :] = wlo.astype(bf16)
        his, los = [], []
        for value in values:
            hi, lo = halves(jnp.where(mine_mask, value, 0.0))
            his.append(hi)
            los.append(lo)
        ys = jnp.concatenate(his + los, axis=0).astype(bf16)
        out = nt(ys, w_scr[t])
        n = len(values) * groups
        total = (out[0:n, 0:channels] + out[0:n, channels:]) + out[n : 2 * n, 0:channels]
        base = pl.multiple_of(t * groups, groups)
        for m in range(len(values)):
            mom_scr[m, pl.ds(base, groups), :] = total[m * groups : (m + 1) * groups] * factor
        return carry

    lax.fori_loop(0, tiles, forward, 0)

    degree = [0, 1, 1, 1, 2, 2, 2, 2, 2]
    count = len(degree)
    invariants = []
    for l in range(3):
        total = None
        for m in range(count):
            if degree[m] == l:
                sq = mom_scr[m] * mom_scr[m]
                total = sq if total is None else total + sq
        invariants.append(total)
    mixed = None
    for l in range(3):
        part = jnp.dot(invariants[l], mix_ref[l], precision=highest, preferred_element_type=f32)
        mixed = part if mixed is None else mixed + part
    sig = 0.5 * jnp.tanh(0.5 * mixed) + 0.5
    act = mixed * sig
    reads = read_ref[...]
    energy_ref[...] = nt(jnp.broadcast_to(reads, (8, channels)), act, highest)[0:1]
    dmixed = reads * (sig + act * (1.0 - sig))
    for l in range(3):
        dinv = nt(dmixed, mix_ref[l], highest) * (2.0 * factor)
        for m in range(count):
            if degree[m] == l:
                hi, lo = halves(dinv * mom_scr[m])
                g_scr[:, m * groups : (m + 1) * groups, :] = hi.reshape(tiles, groups, channels)
                g_scr[:, (count + m) * groups : (count + m + 1) * groups, :] = lo.reshape(tiles, groups, channels)

    acc_scr[...] = jnp.zeros(acc_scr.shape, f32)
    padded = acc_scr.shape[0] // 6
    chunk_iota = lax.broadcasted_iota(jnp.int32, (padded, tile), 0)
    lane_rows = lax.broadcasted_iota(jnp.int32, (LANES, tile), 0)
    n = count * groups

    def backward(t, carry):
        x, y, z = spread(0, t), spread(1, t), spread(2, t)
        values, _ = harmonics(x, y, z)
        g = g_scr[t]
        gl = jnp.concatenate(
            [g.astype(bf16), jnp.concatenate([g[0:n], jnp.zeros((n, channels), f32)], axis=0).astype(bf16)], axis=1
        )
        a = jnp.dot(gl, w_scr[t], preferred_element_type=f32)
        b = jnp.dot(gl, dw_scr[t], preferred_element_type=f32)
        A = [a[m * groups : (m + 1) * groups] + a[n + m * groups : n + (m + 1) * groups] for m in range(count)]
        rad = None
        for m in range(count):
            B = b[m * groups : (m + 1) * groups] + b[n + m * groups : n + (m + 1) * groups]
            rad = B if m == 0 else rad + values[m] * B
        rad = 2.0 * rad
        dx = root_three * A[1] + root_fifteen * (y * A[4] + z * A[7] + x * A[8]) - root_five * (x * A[6]) + x * rad
        dy = root_three * A[2] + root_fifteen * (x * A[4] + z * A[5] - y * A[8]) - root_five * (y * A[6]) + y * rad
        dz = root_three * A[3] + root_fifteen * (y * A[5] + x * A[7]) + (2.0 * root_five) * (z * A[6]) + z * rad
        comps = [jnp.where(mine_mask, v, 0.0) for v in (dx, dy, dz)]
        base = pl.multiple_of(t * groups, groups)
        lane = lax.broadcasted_iota(jnp.int32, (groups, LANES), 1)
        cen = jnp.zeros((groups, LANES), f32)
        for i, v in enumerate(comps):
            cen = jnp.where(lane == i, jnp.sum(v, axis=1, keepdims=True), cen)
        cen_scr[pl.ds(base, groups), :] = cen
        idx = idx_ref[pl.ds(t, 1), :]
        low = jnp.bitwise_and(idx, LANES - 1)
        chunk = jnp.right_shift(idx, LANES.bit_length() - 1)
        hit = jnp.broadcast_to(chunk, (padded, tile)) == chunk_iota
        his, los = [], []
        for v in comps:
            row = jnp.sum(v, axis=0, keepdims=True)
            hi, lo = halves(jnp.where(hit, jnp.broadcast_to(row, (padded, tile)), 0.0))
            his.append(hi)
            los.append(lo)
        left = jnp.concatenate(his + los, axis=0).astype(bf16)
        right = jnp.where(jnp.broadcast_to(low, (LANES, tile)) == lane_rows, 1.0, 0.0).astype(bf16)
        acc_scr[...] += nt(left, right)
        return carry

    lax.fori_loop(0, tiles, backward, 0)

    half = 3 * padded
    cen = jnp.concatenate(
        [jnp.transpose(cen_scr[c * LANES : (c + 1) * LANES, :])[0:8] for c in range(own_chunks)], axis=1
    )
    for axis in range(3):
        lo = axis * padded
        sums = acc_scr[lo : lo + padded] + acc_scr[half + lo : half + lo + padded]
        for c in range(own_chunks):
            own_ref[axis : axis + 1, c * LANES : (c + 1) * LANES] = (
                sums[c : c + 1] - cen[axis : axis + 1, c * LANES : (c + 1) * LANES]
            )
        for k, back in enumerate((back_left, back_right, back_lower, back_upper)):
            for j in range(ghost):
                c = own_chunks + k * ghost + j
                back[j, axis : axis + 1, :] = sums[c : c + 1]


def core(split, row, idx, own_pos, own_feat, win, wout, mixing, readout, sides, rows):
    atoms = own_pos.shape[2]
    channels = own_feat.shape[1]
    tiles, tile = idx.shape
    ghost = sides[0].shape[0]
    number, hidden = win.shape
    extent = atoms + len(sides) * ghost * LANES
    padded = -(-extent // (LANES * 16)) * 16
    vm = pl.BlockSpec(memory_space=pltpu.VMEM)
    sm = pl.BlockSpec(memory_space=pltpu.SMEM)
    back = jax.ShapeDtypeStruct((ghost, 3, LANES), f32)
    return pl.pallas_call(
        functools.partial(core_kernel, GROUPS, rows),
        out_shape=(
            jax.ShapeDtypeStruct((1, atoms), f32),
            jax.ShapeDtypeStruct((3, atoms), f32),
        ) + (back,) * len(sides),
        in_specs=[sm, sm] + [vm] * (7 + len(sides)),
        out_specs=(vm,) * (2 + len(sides)),
        scratch_shapes=[
            pltpu.VMEM((3, tiles, tile), f32),
            pltpu.VMEM((2 * number, 2 * hidden), f32),
            pltpu.VMEM((2 * channels, extent), bf16),
            pltpu.VMEM((tiles, 2 * channels, tile), bf16),
            pltpu.VMEM((tiles, 2 * channels, tile), bf16),
            pltpu.VMEM((9, atoms, channels), f32),
            pltpu.VMEM((tiles, 18 * GROUPS, channels), f32),
            pltpu.VMEM((6 * padded, LANES), f32),
            pltpu.VMEM((atoms, LANES), f32),
        ],
        compiler_params=pltpu.CompilerParams(vmem_limit_bytes=32 << 20),
        name="core",
    )(split, row, idx, own_pos, own_feat, win, wout, mixing, readout, *sides)


def source_slot(slot, ghost, crossing, split, sign):
    rolled = lax.rem(slot + sign * split + ghost, ghost)
    return jnp.where(crossing, rolled, slot)


def shared_blocks(faces_ref, rows, split, row):
    ghost = faces_ref.shape[0]
    listed = [[faces_ref[j, k] for j in range(ghost)] for k in range(2)]
    listed.append([faces_ref[source_slot(j, ghost, row == rows - 1, split, -1), 2] for j in range(ghost)])
    listed.append([faces_ref[source_slot(j, ghost, row == 0, split, 1), 3] for j in range(ghost)])
    return listed


def pack_kernel(rows, split_ref, row_ref, faces_ref, pos_ref, feat_ref, *out_refs):
    channels = feat_ref.shape[1]
    listed = shared_blocks(faces_ref, rows, split_ref[0], row_ref[0])
    for out, blocks in zip(out_refs, listed):
        for j, block in enumerate(blocks):
            lanes = pl.ds(pl.multiple_of(block * LANES, LANES), LANES)
            out[j, 0:channels, :] = feat_ref[0, :, lanes]
            for axis in range(3):
                out[j, channels + axis : channels + axis + 1, :] = pos_ref[axis, :, lanes]
            out[j, channels + 3 :, :] = jnp.zeros((out.shape[1] - channels - 3, LANES), f32)


def pack(split, row, faces, pos, feat, rows):
    ghost, sides = faces.shape
    vm = pl.BlockSpec(memory_space=pltpu.VMEM)
    sm = pl.BlockSpec(memory_space=pltpu.SMEM)
    side = jax.ShapeDtypeStruct((ghost, feat.shape[1] + 8, LANES), f32)
    return pl.pallas_call(
        functools.partial(pack_kernel, rows),
        out_shape=(side,) * sides,
        in_specs=[sm, sm, sm, vm, vm],
        out_specs=(vm,) * sides,
        name="pack",
    )(split, row, faces, pos, feat)


def finish_kernel(rows, split_ref, row_ref, faces_ref, own_ref, *refs):
    forces_ref = refs[-1]
    listed = shared_blocks(faces_ref, rows, split_ref[0], row_ref[0])
    for number in range(own_ref.shape[1] // LANES):
        lanes = slice(number * LANES, (number + 1) * LANES)
        total = own_ref[:, lanes]
        for back, blocks in zip(refs[:-1], listed):
            for j, block in enumerate(blocks):
                total = total + jnp.where(block == number, back[j], 0.0)
        for axis in range(3):
            forces_ref[axis, :, lanes] = -total[axis : axis + 1]


def finish(split, row, faces, own, backs, rows):
    vm = pl.BlockSpec(memory_space=pltpu.VMEM)
    sm = pl.BlockSpec(memory_space=pltpu.SMEM)
    return pl.pallas_call(
        functools.partial(finish_kernel, rows),
        out_shape=jax.ShapeDtypeStruct((3, 1, own.shape[1]), f32),
        in_specs=[sm, sm, sm] + [vm] * (1 + len(backs)),
        out_specs=vm,
        name="finish",
    )(split, row, faces, own, *backs)


def row_permutation(rows, cols, upward, shift):
    pairs = []
    for g in range(rows):
        for c in range(cols):
            if upward:
                target = (g + 1, c) if g < rows - 1 else (0, (c + shift) % cols)
            else:
                target = (g - 1, c) if g > 0 else (rows - 1, (c - shift) % cols)
            pairs.append((c * rows + g, target[1] * rows + target[0]))
    return pairs


def ring_permutation(rows, cols, by):
    return [(c * rows + g, (c + by) % cols * rows + g) for c in range(cols) for g in range(rows)]


def exchange(sides, branch, rows, cols, back):
    ghost = sides[0].shape[0]

    def send(value, perm):
        pairs = [(b, a) for a, b in perm] if back else perm
        return lax.ppermute(value, ("flow", "grad"), pairs)

    def sheared(value, upward, shift, nearer):
        if nearer in (0, ghost):
            return send(value, row_permutation(rows, cols, upward, shift + (1 if nearer == 0 else 0)))
        first, rest = value[:nearer], value[nearer:]
        early, late = (shift + 1, shift) if upward else (shift, shift + 1)
        return jnp.concatenate(
            [
                send(first, row_permutation(rows, cols, upward, early)),
                send(rest, row_permutation(rows, cols, upward, late)),
            ],
            axis=0,
        )

    def case(number):
        shift, split = divmod(number, ghost)

        def route(values):
            left, right, lower, upper = values
            if split == 0:
                lower = send(lower, row_permutation(rows, cols, True, shift))
                upper = send(upper, row_permutation(rows, cols, False, shift))
            else:
                lower = sheared(lower, True, shift, split)
                upper = sheared(upper, False, shift, ghost - split)
            left = send(left, ring_permutation(rows, cols, 1))
            right = send(right, ring_permutation(rows, cols, -1))
            return (left, right, lower, upper)

        return route

    return lax.switch(branch, [case(number) for number in range(cols * ghost)], tuple(sides))


def body(
    positions,
    features,
    neighbours,
    face_blocks,
    shear_cells,
    split_block,
    radial_in,
    radial_out,
    mixing,
    readout,
):
    faces = jnp.transpose(face_blocks[0])
    entries, atoms = neighbours.shape[1:]
    ghost = faces.shape[0]
    rows = lax.axis_size("grad")
    cols = lax.axis_size("flow")
    row = lax.axis_index("grad").astype(jnp.int32).reshape(1)
    branch = shear_cells[0] * ghost + split_block[0]
    branch = jnp.where(branch == cols * ghost, 0, branch)
    idx = jnp.transpose(neighbours[0]).reshape(atoms // GROUPS, GROUPS * entries)

    sides = pack(split_block, row, faces, positions, features, rows)
    sides = exchange(sides, branch, rows, cols, False)
    energy, own, *backs = core(
        split_block, row, idx, positions, features, radial_in, radial_out, mixing, readout.reshape(1, -1), sides, rows
    )
    backs = exchange(backs, branch, rows, cols, True)
    forces = finish(split_block, row, faces, own, backs, rows)
    return (energy, forces)


def solution(mesh):
    in_specs = (
        P(None, "grad", "flow"),
        P("grad", None, "flow"),
        P("grad", None, "flow"),
        P("grad", None, "flow"),
        P(),
        P(),
        P(),
        P(),
        P(),
        P(),
    )
    out_specs = (P("grad", "flow"), P(None, "grad", "flow"))
    return jax.shard_map(body, mesh=mesh, in_specs=in_specs, out_specs=out_specs, check_vma=False)
```

```python
import functools

import jax
import jax.numpy as jnp
from jax import lax
from jax.experimental import pallas as pl
from jax.experimental.pallas import tpu as pltpu
from jax.sharding import PartitionSpec as P

LANES = 128
GROUPS = 8
AHEAD = 8
BEHIND = 8
highest = lax.Precision.HIGHEST
root_three = 3.0**0.5
root_five = 5.0**0.5
root_fifteen = 15.0**0.5
f32 = jnp.float32
bf16 = jnp.bfloat16


def halves(value):
    upper = value.astype(bf16).astype(f32)
    return upper, value - upper


def nt(left, right, precision=None):
    return lax.dot_general(left, right, (((1,), (1,)), ((), ())), precision=precision, preferred_element_type=f32)


def core_kernel(groups, rows, split_ref, row_ref, idx_ref, own_pos, own_feat, win_ref, wout_ref, mix_ref, read_ref,
                left_ref, right_ref, lower_ref, upper_ref,
                energy_ref, own_ref, back_left, back_right, back_lower, back_upper,
                xyz_scr, d_scr, f_scr, w_scr, dw_scr, mom_scr, g_scr, acc_scr, cen_scr):
    split = split_ref[0]
    row = row_ref[0]
    atoms = own_pos.shape[2]
    channels = own_feat.shape[1]
    number, hidden = win_ref.shape
    ghost = left_ref.shape[0]
    tiles, tile = idx_ref.shape
    neighbours = tile // groups
    own_chunks = atoms // LANES
    sides = (left_ref, right_ref, lower_ref, upper_ref)
    chunks = own_chunks + len(sides) * ghost
    factor = neighbours ** (-0.5)

    def pos_chunk(c, axis):
        if c < own_chunks:
            return own_pos[axis, :, c * LANES : (c + 1) * LANES]
        k, j = divmod(c - own_chunks, ghost)
        line = sides[k][j, channels + axis : channels + axis + 1, :]
        fraction = split.astype(f32) / ghost
        if axis == 0:
            if k < 2:
                line = line + (2.0 * k - 1.0)
            elif k == 2:
                line = line + jnp.where(row == 0, jnp.where(j < split, fraction - 1.0, fraction), 0.0)
            else:
                line = line + jnp.where(
                    row == rows - 1, jnp.where(j < ghost - split, -fraction, 1.0 - fraction), 0.0
                )
        elif axis == 1 and k >= 2:
            line = line + (2.0 * k - 5.0)
        return line

    blocks = tile // LANES
    for lb in range(blocks):
        lanes = slice(lb * LANES, (lb + 1) * LANES)
        idx = idx_ref[:, lanes]
        low = jnp.bitwise_and(idx, LANES - 1)
        chunk = jnp.right_shift(idx, LANES.bit_length() - 1)
        lines = lax.broadcasted_iota(jnp.int32, idx.shape, 0)
        cols = lax.broadcasted_iota(jnp.int32, idx.shape, 1) + lb * LANES
        centre = lines * groups + cols // neighbours
        clow = jnp.bitwise_and(centre, LANES - 1)
        cchunk = jnp.right_shift(centre, LANES.bit_length() - 1)
        for axis in range(3):
            other = None
            mine = None
            for c in range(chunks):
                src = jnp.broadcast_to(pos_chunk(c, axis), idx.shape)
                got = jnp.take_along_axis(src, low, axis=1)
                other = got if other is None else jnp.where(chunk == c, got, other)
                if c < own_chunks:
                    got = jnp.take_along_axis(src, clow, axis=1)
                    mine = got if mine is None else jnp.where(cchunk == c, got, mine)
            xyz_scr[axis, :, lanes] = other - mine

    d_scr[...] = jnp.zeros(d_scr.shape, f32)
    d_scr[0:number, 0:hidden] = win_ref[...]
    d_scr[number : 2 * number, hidden : 2 * hidden] = win_ref[...]
    dhi, dlo = halves(d_scr[...])
    first = jnp.transpose(jnp.concatenate([dhi, dhi, dlo, dlo], axis=0)).astype(bf16)
    ohi, olo = halves(wout_ref[...])
    second = jnp.transpose(jnp.concatenate([ohi, ohi, olo, olo], axis=0)).astype(bf16)

    for c in range(chunks):
        lanes = slice(c * LANES, (c + 1) * LANES)
        if c < own_chunks:
            feat = own_feat[0, :, lanes]
        else:
            k, j = divmod(c - own_chunks, ghost)
            feat = sides[k][j, 0:channels, :]
        hi, lo = halves(feat)
        f_scr[0:channels, lanes] = hi.astype(bf16)
        f_scr[channels : 2 * channels, lanes] = lo.astype(bf16)

    row_iota = lax.broadcasted_iota(jnp.int32, (groups, tile), 0)
    lane_iota = lax.broadcasted_iota(jnp.int32, (groups, tile), 1)
    mine_mask = row_iota == lane_iota // neighbours
    centres = lax.broadcasted_iota(jnp.int32, (number, tile), 0).astype(f32) * (6.0 / (number - 1))
    entry_iota = lax.broadcasted_iota(jnp.int16, (chunks * LANES, tile), 0)

    def spread(axis, t, lines=groups):
        return jnp.broadcast_to(xyz_scr[axis, pl.ds(t, 1), :], (lines, tile))

    def harmonics(x, y, z):
        square = x * x + y * y + z * z
        return [
            jnp.ones_like(x),
            root_three * x,
            root_three * y,
            root_three * z,
            root_fifteen * x * y,
            root_fifteen * y * z,
            0.5 * root_five * (3.0 * z * z - square),
            root_fifteen * x * z,
            0.5 * root_fifteen * (x * x - y * y),
        ]

    def stacked(value):
        hi, lo = halves(value)
        return jnp.concatenate([hi, lo, hi, lo], axis=0).astype(bf16)

    def forward(step, carry):
        numbers = [step * AHEAD + u for u in range(AHEAD)]
        bases = []
        for t in numbers:
            x, y, z = (spread(axis, t, number) for axis in range(3))
            away = x * x + y * y + z * z - centres
            scaled = away / 0.75
            gauss = jnp.exp(-0.5 * (scaled * scaled))
            slope = gauss * (away * (-1.0 / 0.5625))
            bases.append(stacked(jnp.concatenate([gauss, slope], axis=0)))
        boths = [jnp.dot(first, basis, preferred_element_type=f32) for basis in bases]
        gathered = []
        for t in numbers:
            listed = jnp.broadcast_to(idx_ref[pl.ds(t, 1), :], (16, tile)).astype(jnp.int16)
            listed = jnp.concatenate([listed] * (chunks * LANES // 16), axis=0)
            picks = jnp.where(listed == entry_iota, jnp.ones((), bf16), jnp.zeros((), bf16))
            gathered.append(jnp.dot(f_scr[...], picks, preferred_element_type=f32))
        acts, dacts = [], []
        for both in boths:
            h, dh = both[0:hidden], both[hidden : 2 * hidden]
            sig = 0.5 * jnp.tanh(0.5 * h) + 0.5
            act = h * sig
            acts.append(stacked(act))
            dacts.append(stacked(dh * (sig + act * (1.0 - sig))))
        radials = [jnp.dot(second, act, preferred_element_type=f32) for act in acts]
        dradials = [jnp.dot(second, dact, preferred_element_type=f32) for dact in dacts]
        feats = [part[0:channels] + part[channels:] for part in gathered]
        blocks_of = []
        for t in numbers:
            his, los = [], []
            for value in harmonics(*(spread(axis, t) for axis in range(3))):
                hi, lo = halves(jnp.where(mine_mask, value, 0.0))
                his.append(hi)
                los.append(lo)
            blocks_of.append(jnp.concatenate(his + los, axis=0).astype(bf16))
        weights = []
        for t, radial, feat in zip(numbers, radials, feats):
            whi, wlo = halves(radial * feat)
            weight = jnp.concatenate([whi, wlo], axis=0).astype(bf16)
            w_scr[t] = weight
            weights.append(weight)
        for t, dradial, feat in zip(numbers, dradials, feats):
            whi, wlo = halves(dradial * feat)
            dw_scr[t] = jnp.concatenate([whi, wlo], axis=0).astype(bf16)
        n = 9 * groups
        for t, ys, weight in zip(numbers, blocks_of, weights):
            out = nt(ys, weight)
            total = (out[0:n, 0:channels] + out[0:n, channels:]) + out[n : 2 * n, 0:channels]
            base = pl.multiple_of(t * groups, groups)
            for m in range(9):
                mom_scr[m, pl.ds(base, groups), :] = total[m * groups : (m + 1) * groups] * factor
        return carry

    lax.fori_loop(0, tiles // AHEAD, forward, 0)

    degree = [0, 1, 1, 1, 2, 2, 2, 2, 2]
    count = len(degree)
    invariants = []
    for l in range(3):
        total = None
        for m in range(count):
            if degree[m] == l:
                sq = mom_scr[m] * mom_scr[m]
                total = sq if total is None else total + sq
        invariants.append(total)
    mixed = None
    for l in range(3):
        part = jnp.dot(invariants[l], mix_ref[l], precision=highest, preferred_element_type=f32)
        mixed = part if mixed is None else mixed + part
    sig = 0.5 * jnp.tanh(0.5 * mixed) + 0.5
    act = mixed * sig
    reads = read_ref[...]
    energy_ref[...] = nt(jnp.broadcast_to(reads, (8, channels)), act, highest)[0:1]
    dmixed = reads * (sig + act * (1.0 - sig))
    for l in range(3):
        dinv = nt(dmixed, mix_ref[l], highest) * (2.0 * factor)
        for m in range(count):
            if degree[m] == l:
                hi, lo = halves(dinv * mom_scr[m])
                g_scr[:, m * groups : (m + 1) * groups, :] = hi.reshape(tiles, groups, channels)
                g_scr[:, (count + m) * groups : (count + m + 1) * groups, :] = lo.reshape(tiles, groups, channels)

    acc_scr[...] = jnp.zeros(acc_scr.shape, f32)
    padded = acc_scr.shape[0] // 6
    chunk_iota = lax.broadcasted_iota(jnp.int32, (padded, tile), 0)
    lane_rows = lax.broadcasted_iota(jnp.int32, (LANES, tile), 0)
    n = count * groups

    def backward(step, carry):
        numbers = [step * BEHIND + u for u in range(BEHIND)]
        outs = []
        for t in numbers:
            g = g_scr[t]
            gl = jnp.concatenate(
                [g.astype(bf16), jnp.concatenate([g[0:n], jnp.zeros((n, channels), f32)], axis=0).astype(bf16)],
                axis=1,
            )
            outs.append(
                (
                    jnp.dot(gl, w_scr[t], preferred_element_type=f32),
                    jnp.dot(gl, dw_scr[t], preferred_element_type=f32),
                )
            )
        rights = []
        for t in numbers:
            low = jnp.bitwise_and(idx_ref[pl.ds(t, 1), :], LANES - 1)
            rights.append(jnp.where(jnp.broadcast_to(low, (LANES, tile)) == lane_rows, 1.0, 0.0).astype(bf16))
        lefts = []
        for t, (a, b) in zip(numbers, outs):
            x, y, z = spread(0, t), spread(1, t), spread(2, t)
            values = harmonics(x, y, z)
            A = [a[m * groups : (m + 1) * groups] + a[n + m * groups : n + (m + 1) * groups] for m in range(count)]
            rad = None
            for m in range(count):
                B = b[m * groups : (m + 1) * groups] + b[n + m * groups : n + (m + 1) * groups]
                rad = B if m == 0 else rad + values[m] * B
            rad = 2.0 * rad
            dx = root_three * A[1] + root_fifteen * (y * A[4] + z * A[7] + x * A[8]) - root_five * (x * A[6]) + x * rad
            dy = root_three * A[2] + root_fifteen * (x * A[4] + z * A[5] - y * A[8]) - root_five * (y * A[6]) + y * rad
            dz = root_three * A[3] + root_fifteen * (y * A[5] + x * A[7]) + (2.0 * root_five) * (z * A[6]) + z * rad
            comps = [jnp.where(mine_mask, v, 0.0) for v in (dx, dy, dz)]
            base = pl.multiple_of(t * groups, groups)
            lane = lax.broadcasted_iota(jnp.int32, (groups, LANES), 1)
            cen = jnp.zeros((groups, LANES), f32)
            for i, v in enumerate(comps):
                cen = jnp.where(lane == i, jnp.sum(v, axis=1, keepdims=True), cen)
            cen_scr[pl.ds(base, groups), :] = cen
            chunk = jnp.right_shift(idx_ref[pl.ds(t, 1), :], LANES.bit_length() - 1)
            hit = jnp.broadcast_to(chunk, (padded, tile)) == chunk_iota
            his, los = [], []
            for v in comps:
                line = jnp.sum(v, axis=0, keepdims=True)
                hi, lo = halves(jnp.where(hit, jnp.broadcast_to(line, (padded, tile)), 0.0))
                his.append(hi)
                los.append(lo)
            lefts.append(jnp.concatenate(his + los, axis=0).astype(bf16))
        acc_scr[...] += nt(jnp.concatenate(lefts, axis=1), jnp.concatenate(rights, axis=1))
        return carry

    lax.fori_loop(0, tiles // BEHIND, backward, 0)

    half = 3 * padded
    cen = jnp.concatenate(
        [jnp.transpose(cen_scr[c * LANES : (c + 1) * LANES, :])[0:8] for c in range(own_chunks)], axis=1
    )
    for axis in range(3):
        lo = axis * padded
        sums = acc_scr[lo : lo + padded] + acc_scr[half + lo : half + lo + padded]
        for c in range(own_chunks):
            own_ref[axis : axis + 1, c * LANES : (c + 1) * LANES] = (
                sums[c : c + 1] - cen[axis : axis + 1, c * LANES : (c + 1) * LANES]
            )
        for k, back in enumerate((back_left, back_right, back_lower, back_upper)):
            for j in range(ghost):
                c = own_chunks + k * ghost + j
                back[j, axis : axis + 1, :] = sums[c : c + 1]


def core(split, row, idx, own_pos, own_feat, win, wout, mixing, readout, sides, rows):
    atoms = own_pos.shape[2]
    channels = own_feat.shape[1]
    tiles, tile = idx.shape
    ghost = sides[0].shape[0]
    number, hidden = win.shape
    extent = atoms + len(sides) * ghost * LANES
    padded = -(-extent // (LANES * 16)) * 16
    vm = pl.BlockSpec(memory_space=pltpu.VMEM)
    sm = pl.BlockSpec(memory_space=pltpu.SMEM)
    back = jax.ShapeDtypeStruct((ghost, 3, LANES), f32)
    return pl.pallas_call(
        functools.partial(core_kernel, GROUPS, rows),
        out_shape=(
            jax.ShapeDtypeStruct((1, atoms), f32),
            jax.ShapeDtypeStruct((3, atoms), f32),
        ) + (back,) * len(sides),
        in_specs=[sm, sm] + [vm] * (7 + len(sides)),
        out_specs=(vm,) * (2 + len(sides)),
        scratch_shapes=[
            pltpu.VMEM((3, tiles, tile), f32),
            pltpu.VMEM((2 * number, 2 * hidden), f32),
            pltpu.VMEM((2 * channels, extent), bf16),
            pltpu.VMEM((tiles, 2 * channels, tile), bf16),
            pltpu.VMEM((tiles, 2 * channels, tile), bf16),
            pltpu.VMEM((9, atoms, channels), f32),
            pltpu.VMEM((tiles, 18 * GROUPS, channels), f32),
            pltpu.VMEM((6 * padded, LANES), f32),
            pltpu.VMEM((atoms, LANES), f32),
        ],
        compiler_params=pltpu.CompilerParams(vmem_limit_bytes=32 << 20),
        name="core",
    )(split, row, idx, own_pos, own_feat, win, wout, mixing, readout, *sides)


def source_slot(slot, ghost, crossing, split, sign):
    rolled = lax.rem(slot + sign * split + ghost, ghost)
    return jnp.where(crossing, rolled, slot)


def shared_blocks(faces_ref, rows, split, row):
    ghost = faces_ref.shape[0]
    listed = [[faces_ref[j, k] for j in range(ghost)] for k in range(2)]
    listed.append([faces_ref[source_slot(j, ghost, row == rows - 1, split, -1), 2] for j in range(ghost)])
    listed.append([faces_ref[source_slot(j, ghost, row == 0, split, 1), 3] for j in range(ghost)])
    return listed


def pack_kernel(rows, split_ref, row_ref, faces_ref, pos_ref, feat_ref, *out_refs):
    channels = feat_ref.shape[1]
    listed = shared_blocks(faces_ref, rows, split_ref[0], row_ref[0])
    for out, blocks in zip(out_refs, listed):
        for j, block in enumerate(blocks):
            lanes = pl.ds(pl.multiple_of(block * LANES, LANES), LANES)
            out[j, 0:channels, :] = feat_ref[0, :, lanes]
            for axis in range(3):
                out[j, channels + axis : channels + axis + 1, :] = pos_ref[axis, :, lanes]
            out[j, channels + 3 :, :] = jnp.zeros((out.shape[1] - channels - 3, LANES), f32)


def pack(split, row, faces, pos, feat, rows):
    ghost, sides = faces.shape
    vm = pl.BlockSpec(memory_space=pltpu.VMEM)
    sm = pl.BlockSpec(memory_space=pltpu.SMEM)
    side = jax.ShapeDtypeStruct((ghost, feat.shape[1] + 8, LANES), f32)
    return pl.pallas_call(
        functools.partial(pack_kernel, rows),
        out_shape=(side,) * sides,
        in_specs=[sm, sm, sm, vm, vm],
        out_specs=(vm,) * sides,
        name="pack",
    )(split, row, faces, pos, feat)


def finish_kernel(rows, split_ref, row_ref, faces_ref, own_ref, *refs):
    forces_ref = refs[-1]
    listed = shared_blocks(faces_ref, rows, split_ref[0], row_ref[0])
    for number in range(own_ref.shape[1] // LANES):
        lanes = slice(number * LANES, (number + 1) * LANES)
        total = own_ref[:, lanes]
        for back, blocks in zip(refs[:-1], listed):
            for j, block in enumerate(blocks):
                total = total + jnp.where(block == number, back[j], 0.0)
        for axis in range(3):
            forces_ref[axis, :, lanes] = -total[axis : axis + 1]


def finish(split, row, faces, own, backs, rows):
    vm = pl.BlockSpec(memory_space=pltpu.VMEM)
    sm = pl.BlockSpec(memory_space=pltpu.SMEM)
    return pl.pallas_call(
        functools.partial(finish_kernel, rows),
        out_shape=jax.ShapeDtypeStruct((3, 1, own.shape[1]), f32),
        in_specs=[sm, sm, sm] + [vm] * (1 + len(backs)),
        out_specs=vm,
        name="finish",
    )(split, row, faces, own, *backs)


def row_permutation(rows, cols, upward, shift):
    pairs = []
    for g in range(rows):
        for c in range(cols):
            if upward:
                target = (g + 1, c) if g < rows - 1 else (0, (c + shift) % cols)
            else:
                target = (g - 1, c) if g > 0 else (rows - 1, (c - shift) % cols)
            pairs.append((c * rows + g, target[1] * rows + target[0]))
    return pairs


def ring_permutation(rows, cols, by):
    return [(c * rows + g, (c + by) % cols * rows + g) for c in range(cols) for g in range(rows)]


def exchange(sides, branch, rows, cols, back):
    ghost = sides[0].shape[0]

    def send(value, perm):
        pairs = [(b, a) for a, b in perm] if back else perm
        return lax.ppermute(value, ("flow", "grad"), pairs)

    def sheared(value, upward, shift, nearer):
        if nearer in (0, ghost):
            return send(value, row_permutation(rows, cols, upward, shift + (1 if nearer == 0 else 0)))
        first, rest = value[:nearer], value[nearer:]
        early, late = (shift + 1, shift) if upward else (shift, shift + 1)
        return jnp.concatenate(
            [
                send(first, row_permutation(rows, cols, upward, early)),
                send(rest, row_permutation(rows, cols, upward, late)),
            ],
            axis=0,
        )

    def case(number):
        shift, split = divmod(number, ghost)

        def route(values):
            left, right, lower, upper = values
            if split == 0:
                lower = send(lower, row_permutation(rows, cols, True, shift))
                upper = send(upper, row_permutation(rows, cols, False, shift))
            else:
                lower = sheared(lower, True, shift, split)
                upper = sheared(upper, False, shift, ghost - split)
            left = send(left, ring_permutation(rows, cols, 1))
            right = send(right, ring_permutation(rows, cols, -1))
            return (left, right, lower, upper)

        return route

    return lax.switch(branch, [case(number) for number in range(cols * ghost)], tuple(sides))


def body(
    positions,
    features,
    neighbours,
    face_blocks,
    shear_cells,
    split_block,
    radial_in,
    radial_out,
    mixing,
    readout,
):
    faces = jnp.transpose(face_blocks[0])
    entries, atoms = neighbours.shape[1:]
    ghost = faces.shape[0]
    rows = lax.axis_size("grad")
    cols = lax.axis_size("flow")
    row = lax.axis_index("grad").astype(jnp.int32).reshape(1)
    branch = shear_cells[0] * ghost + split_block[0]
    branch = jnp.where(branch == cols * ghost, 0, branch)
    idx = jnp.transpose(neighbours[0]).reshape(atoms // GROUPS, GROUPS * entries)

    sides = pack(split_block, row, faces, positions, features, rows)
    sides = exchange(sides, branch, rows, cols, False)
    energy, own, *backs = core(
        split_block, row, idx, positions, features, radial_in, radial_out, mixing, readout.reshape(1, -1), sides, rows
    )
    backs = exchange(backs, branch, rows, cols, True)
    forces = finish(split_block, row, faces, own, backs, rows)
    return (energy, forces)


def solution(mesh):
    in_specs = (
        P(None, "grad", "flow"),
        P("grad", None, "flow"),
        P("grad", None, "flow"),
        P("grad", None, "flow"),
        P(),
        P(),
        P(),
        P(),
        P(),
        P(),
    )
    out_specs = (P("grad", "flow"), P(None, "grad", "flow"))
    return jax.shard_map(body, mesh=mesh, in_specs=in_specs, out_specs=out_specs, check_vma=False)
```

```python
import functools

import jax
import jax.numpy as jnp
from jax import lax
from jax.experimental import pallas as pl
from jax.experimental.pallas import tpu as pltpu
from jax.sharding import PartitionSpec as P

LANES = 128
GROUPS = 8
AHEAD = 8
BEHIND = 8
highest = lax.Precision.HIGHEST
root_three = 3.0**0.5
root_five = 5.0**0.5
root_fifteen = 15.0**0.5
f32 = jnp.float32
bf16 = jnp.bfloat16


def halves(value):
    upper = value.astype(bf16).astype(f32)
    return upper, value - upper


def nt(left, right, precision=None):
    return lax.dot_general(left, right, (((1,), (1,)), ((), ())), precision=precision, preferred_element_type=f32)


def core_kernel(groups, rows, split_ref, place_ref, idx_ref, own_pos, own_feat, win_ref, wout_ref, mix_ref, read_ref,
                first_ref, second_ref, third_ref, fourth_ref,
                energy_ref, own_ref, first_back, second_back, third_back, fourth_back,
                xyz_scr, d_scr, f_scr, w_scr, dw_scr, mom_scr, g_scr, acc_scr, cen_scr):
    split = split_ref[0]
    row = place_ref[0]
    row_odd = lax.rem(row, 2) == 1
    col_odd = lax.rem(place_ref[1], 2) == 1
    atoms = own_pos.shape[2]
    channels = own_feat.shape[1]
    number, hidden = win_ref.shape
    ghost = first_ref.shape[0]
    tiles, tile = idx_ref.shape
    neighbours = tile // groups
    own_chunks = atoms // LANES
    sides = (
        (col_odd, third_ref, fourth_ref),
        (col_odd, fourth_ref, third_ref),
        (row_odd, second_ref, first_ref),
        (row_odd, first_ref, second_ref),
    )
    chunks = own_chunks + len(sides) * ghost
    factor = neighbours ** (-0.5)

    def side(k, j, part):
        odd, one, other = sides[k]
        return jnp.where(odd, one[j, part, :], other[j, part, :])

    def pos_chunk(c, axis):
        if c < own_chunks:
            return own_pos[axis, :, c * LANES : (c + 1) * LANES]
        k, j = divmod(c - own_chunks, ghost)
        line = side(k, j, slice(channels + axis, channels + axis + 1))
        fraction = split.astype(f32) / ghost
        if axis == 0:
            if k < 2:
                line = line + (2.0 * k - 1.0)
            elif k == 2:
                line = line + jnp.where(row == 0, jnp.where(j < split, fraction - 1.0, fraction), 0.0)
            else:
                line = line + jnp.where(
                    row == rows - 1, jnp.where(j < ghost - split, -fraction, 1.0 - fraction), 0.0
                )
        elif axis == 1 and k >= 2:
            line = line + (2.0 * k - 5.0)
        return line

    blocks = tile // LANES
    for lb in range(blocks):
        lanes = slice(lb * LANES, (lb + 1) * LANES)
        idx = idx_ref[:, lanes]
        low = jnp.bitwise_and(idx, LANES - 1)
        chunk = jnp.right_shift(idx, LANES.bit_length() - 1)
        lines = lax.broadcasted_iota(jnp.int32, idx.shape, 0)
        cols = lax.broadcasted_iota(jnp.int32, idx.shape, 1) + lb * LANES
        centre = lines * groups + cols // neighbours
        clow = jnp.bitwise_and(centre, LANES - 1)
        cchunk = jnp.right_shift(centre, LANES.bit_length() - 1)
        for axis in range(3):
            other = None
            mine = None
            for c in range(chunks):
                src = jnp.broadcast_to(pos_chunk(c, axis), idx.shape)
                got = jnp.take_along_axis(src, low, axis=1)
                other = got if other is None else jnp.where(chunk == c, got, other)
                if c < own_chunks:
                    got = jnp.take_along_axis(src, clow, axis=1)
                    mine = got if mine is None else jnp.where(cchunk == c, got, mine)
            xyz_scr[axis, :, lanes] = other - mine

    d_scr[...] = jnp.zeros(d_scr.shape, f32)
    d_scr[0:number, 0:hidden] = win_ref[...]
    d_scr[number : 2 * number, hidden : 2 * hidden] = win_ref[...]
    dhi, dlo = halves(d_scr[...])
    first = jnp.transpose(jnp.concatenate([dhi, dhi, dlo, dlo], axis=0)).astype(bf16)
    ohi, olo = halves(wout_ref[...])
    second = jnp.transpose(jnp.concatenate([ohi, ohi, olo, olo], axis=0)).astype(bf16)

    for c in range(chunks):
        lanes = slice(c * LANES, (c + 1) * LANES)
        if c < own_chunks:
            feat = own_feat[0, :, lanes]
        else:
            k, j = divmod(c - own_chunks, ghost)
            feat = side(k, j, slice(0, channels))
        hi, lo = halves(feat)
        f_scr[0:channels, lanes] = hi.astype(bf16)
        f_scr[channels : 2 * channels, lanes] = lo.astype(bf16)

    row_iota = lax.broadcasted_iota(jnp.int32, (groups, tile), 0)
    lane_iota = lax.broadcasted_iota(jnp.int32, (groups, tile), 1)
    mine_mask = row_iota == lane_iota // neighbours
    centres = lax.broadcasted_iota(jnp.int32, (number, tile), 0).astype(f32) * (6.0 / (number - 1))
    entry_iota = lax.broadcasted_iota(jnp.int16, (chunks * LANES, tile), 0)

    def spread(axis, t, lines=groups):
        return jnp.broadcast_to(xyz_scr[axis, pl.ds(t, 1), :], (lines, tile))

    def harmonics(x, y, z):
        square = x * x + y * y + z * z
        return [
            jnp.ones_like(x),
            root_three * x,
            root_three * y,
            root_three * z,
            root_fifteen * x * y,
            root_fifteen * y * z,
            0.5 * root_five * (3.0 * z * z - square),
            root_fifteen * x * z,
            0.5 * root_fifteen * (x * x - y * y),
        ]

    def stacked(value):
        hi, lo = halves(value)
        return jnp.concatenate([hi, lo, hi, lo], axis=0).astype(bf16)

    def forward(step, carry):
        numbers = [step * AHEAD + u for u in range(AHEAD)]
        bases = []
        for t in numbers:
            x, y, z = (spread(axis, t, number) for axis in range(3))
            away = x * x + y * y + z * z - centres
            scaled = away / 0.75
            gauss = jnp.exp(-0.5 * (scaled * scaled))
            slope = gauss * (away * (-1.0 / 0.5625))
            bases.append(stacked(jnp.concatenate([gauss, slope], axis=0)))
        boths = [jnp.dot(first, basis, preferred_element_type=f32) for basis in bases]
        gathered = []
        for t in numbers:
            listed = jnp.broadcast_to(idx_ref[pl.ds(t, 1), :], (16, tile)).astype(jnp.int16)
            listed = jnp.concatenate([listed] * (chunks * LANES // 16), axis=0)
            picks = jnp.where(listed == entry_iota, jnp.ones((), bf16), jnp.zeros((), bf16))
            gathered.append(jnp.dot(f_scr[...], picks, preferred_element_type=f32))
        acts, dacts = [], []
        for both in boths:
            h, dh = both[0:hidden], both[hidden : 2 * hidden]
            sig = 0.5 * jnp.tanh(0.5 * h) + 0.5
            act = h * sig
            acts.append(stacked(act))
            dacts.append(stacked(dh * (sig + act * (1.0 - sig))))
        radials = [jnp.dot(second, act, preferred_element_type=f32) for act in acts]
        dradials = [jnp.dot(second, dact, preferred_element_type=f32) for dact in dacts]
        feats = [part[0:channels] + part[channels:] for part in gathered]
        blocks_of = []
        for t in numbers:
            his, los = [], []
            for value in harmonics(*(spread(axis, t) for axis in range(3))):
                hi, lo = halves(jnp.where(mine_mask, value, 0.0))
                his.append(hi)
                los.append(lo)
            blocks_of.append(jnp.concatenate(his + los, axis=0).astype(bf16))
        weights = []
        for t, radial, feat in zip(numbers, radials, feats):
            whi, wlo = halves(radial * feat)
            weight = jnp.concatenate([whi, wlo], axis=0).astype(bf16)
            w_scr[t] = weight
            weights.append(weight)
        for t, dradial, feat in zip(numbers, dradials, feats):
            whi, wlo = halves(dradial * feat)
            dw_scr[t] = jnp.concatenate([whi, wlo], axis=0).astype(bf16)
        n = 9 * groups
        for t, ys, weight in zip(numbers, blocks_of, weights):
            out = nt(ys, weight)
            total = (out[0:n, 0:channels] + out[0:n, channels:]) + out[n : 2 * n, 0:channels]
            base = pl.multiple_of(t * groups, groups)
            for m in range(9):
                mom_scr[m, pl.ds(base, groups), :] = total[m * groups : (m + 1) * groups] * factor
        return carry

    lax.fori_loop(0, tiles // AHEAD, forward, 0)

    degree = [0, 1, 1, 1, 2, 2, 2, 2, 2]
    count = len(degree)
    invariants = []
    for l in range(3):
        total = None
        for m in range(count):
            if degree[m] == l:
                sq = mom_scr[m] * mom_scr[m]
                total = sq if total is None else total + sq
        invariants.append(total)
    mixed = None
    for l in range(3):
        part = jnp.dot(invariants[l], mix_ref[l], precision=highest, preferred_element_type=f32)
        mixed = part if mixed is None else mixed + part
    sig = 0.5 * jnp.tanh(0.5 * mixed) + 0.5
    act = mixed * sig
    reads = read_ref[...]
    energy_ref[...] = nt(jnp.broadcast_to(reads, (8, channels)), act, highest)[0:1]
    dmixed = reads * (sig + act * (1.0 - sig))
    for l in range(3):
        dinv = nt(dmixed, mix_ref[l], highest) * (2.0 * factor)
        for m in range(count):
            if degree[m] == l:
                hi, lo = halves(dinv * mom_scr[m])
                g_scr[:, m * groups : (m + 1) * groups, :] = hi.reshape(tiles, groups, channels)
                g_scr[:, (count + m) * groups : (count + m + 1) * groups, :] = lo.reshape(tiles, groups, channels)

    acc_scr[...] = jnp.zeros(acc_scr.shape, f32)
    padded = acc_scr.shape[0] // 6
    chunk_iota = lax.broadcasted_iota(jnp.int32, (padded, tile), 0)
    lane_rows = lax.broadcasted_iota(jnp.int32, (LANES, tile), 0)
    n = count * groups

    def backward(step, carry):
        numbers = [step * BEHIND + u for u in range(BEHIND)]
        outs = []
        for t in numbers:
            g = g_scr[t]
            gl = jnp.concatenate(
                [g.astype(bf16), jnp.concatenate([g[0:n], jnp.zeros((n, channels), f32)], axis=0).astype(bf16)],
                axis=1,
            )
            outs.append(
                (
                    jnp.dot(gl, w_scr[t], preferred_element_type=f32),
                    jnp.dot(gl, dw_scr[t], preferred_element_type=f32),
                )
            )
        rights = []
        for t in numbers:
            low = jnp.bitwise_and(idx_ref[pl.ds(t, 1), :], LANES - 1)
            rights.append(jnp.where(jnp.broadcast_to(low, (LANES, tile)) == lane_rows, 1.0, 0.0).astype(bf16))
        lefts = []
        for t, (a, b) in zip(numbers, outs):
            x, y, z = spread(0, t), spread(1, t), spread(2, t)
            values = harmonics(x, y, z)
            A = [a[m * groups : (m + 1) * groups] + a[n + m * groups : n + (m + 1) * groups] for m in range(count)]
            rad = None
            for m in range(count):
                B = b[m * groups : (m + 1) * groups] + b[n + m * groups : n + (m + 1) * groups]
                rad = B if m == 0 else rad + values[m] * B
            rad = 2.0 * rad
            dx = root_three * A[1] + root_fifteen * (y * A[4] + z * A[7] + x * A[8]) - root_five * (x * A[6]) + x * rad
            dy = root_three * A[2] + root_fifteen * (x * A[4] + z * A[5] - y * A[8]) - root_five * (y * A[6]) + y * rad
            dz = root_three * A[3] + root_fifteen * (y * A[5] + x * A[7]) + (2.0 * root_five) * (z * A[6]) + z * rad
            comps = [jnp.where(mine_mask, v, 0.0) for v in (dx, dy, dz)]
            base = pl.multiple_of(t * groups, groups)
            lane = lax.broadcasted_iota(jnp.int32, (groups, LANES), 1)
            cen = jnp.zeros((groups, LANES), f32)
            for i, v in enumerate(comps):
                cen = jnp.where(lane == i, jnp.sum(v, axis=1, keepdims=True), cen)
            cen_scr[pl.ds(base, groups), :] = cen
            chunk = jnp.right_shift(idx_ref[pl.ds(t, 1), :], LANES.bit_length() - 1)
            hit = jnp.broadcast_to(chunk, (padded, tile)) == chunk_iota
            his, los = [], []
            for v in comps:
                line = jnp.sum(v, axis=0, keepdims=True)
                hi, lo = halves(jnp.where(hit, jnp.broadcast_to(line, (padded, tile)), 0.0))
                his.append(hi)
                los.append(lo)
            lefts.append(jnp.concatenate(his + los, axis=0).astype(bf16))
        acc_scr[...] += nt(jnp.concatenate(lefts, axis=1), jnp.concatenate(rights, axis=1))
        return carry

    lax.fori_loop(0, tiles // BEHIND, backward, 0)

    half = 3 * padded
    cen = jnp.concatenate(
        [jnp.transpose(cen_scr[c * LANES : (c + 1) * LANES, :])[0:8] for c in range(own_chunks)], axis=1
    )
    for axis in range(3):
        lo = axis * padded
        sums = acc_scr[lo : lo + padded] + acc_scr[half + lo : half + lo + padded]
        for c in range(own_chunks):
            own_ref[axis : axis + 1, c * LANES : (c + 1) * LANES] = (
                sums[c : c + 1] - cen[axis : axis + 1, c * LANES : (c + 1) * LANES]
            )
        left, right, lower, upper = (
            [sums[own_chunks + k * ghost + j : own_chunks + k * ghost + j + 1] for j in range(ghost)] for k in range(4)
        )
        for back, odd, one, other in (
            (first_back, row_odd, upper, lower),
            (second_back, row_odd, lower, upper),
            (third_back, col_odd, left, right),
            (fourth_back, col_odd, right, left),
        ):
            for j in range(ghost):
                back[j, axis : axis + 1, :] = jnp.where(odd, one[j], other[j])


def core(split, place, idx, own_pos, own_feat, win, wout, mixing, readout, sides, rows):
    atoms = own_pos.shape[2]
    channels = own_feat.shape[1]
    tiles, tile = idx.shape
    ghost = sides[0].shape[0]
    number, hidden = win.shape
    extent = atoms + len(sides) * ghost * LANES
    padded = -(-extent // (LANES * 16)) * 16
    vm = pl.BlockSpec(memory_space=pltpu.VMEM)
    sm = pl.BlockSpec(memory_space=pltpu.SMEM)
    back = jax.ShapeDtypeStruct((ghost, 3, LANES), f32)
    return pl.pallas_call(
        functools.partial(core_kernel, GROUPS, rows),
        out_shape=(
            jax.ShapeDtypeStruct((1, atoms), f32),
            jax.ShapeDtypeStruct((3, atoms), f32),
        ) + (back,) * len(sides),
        in_specs=[sm, sm] + [vm] * (7 + len(sides)),
        out_specs=(vm,) * (2 + len(sides)),
        scratch_shapes=[
            pltpu.VMEM((3, tiles, tile), f32),
            pltpu.VMEM((2 * number, 2 * hidden), f32),
            pltpu.VMEM((2 * channels, extent), bf16),
            pltpu.VMEM((tiles, 2 * channels, tile), bf16),
            pltpu.VMEM((tiles, 2 * channels, tile), bf16),
            pltpu.VMEM((9, atoms, channels), f32),
            pltpu.VMEM((tiles, 18 * GROUPS, channels), f32),
            pltpu.VMEM((6 * padded, LANES), f32),
            pltpu.VMEM((atoms, LANES), f32),
        ],
        compiler_params=pltpu.CompilerParams(vmem_limit_bytes=32 << 20),
        name="core",
    )(split, place, idx, own_pos, own_feat, win, wout, mixing, readout, *sides)


def source_slot(slot, ghost, row, rows, split):
    raised = lax.rem(slot + split, ghost)
    lowered = lax.rem(slot - split + ghost, ghost)
    return jnp.where(row == 0, raised, jnp.where(row == rows - 1, lowered, slot))


def shared_blocks(faces_ref, rows, split, row, col):
    ghost = faces_ref.shape[0]
    row_odd = lax.rem(row, 2)
    col_odd = lax.rem(col, 2)
    return [
        [faces_ref[source_slot(j, ghost, row, rows, split), 3 - row_odd] for j in range(ghost)],
        [faces_ref[j, 2 + row_odd] for j in range(ghost)],
        [faces_ref[j, col_odd] for j in range(ghost)],
        [faces_ref[j, 1 - col_odd] for j in range(ghost)],
    ]


def pack_kernel(rows, split_ref, place_ref, faces_ref, pos_ref, feat_ref, *out_refs):
    channels = feat_ref.shape[1]
    listed = shared_blocks(faces_ref, rows, split_ref[0], place_ref[0], place_ref[1])
    for out, blocks in zip(out_refs, listed):
        for j, block in enumerate(blocks):
            lanes = pl.ds(pl.multiple_of(block * LANES, LANES), LANES)
            out[j, 0:channels, :] = feat_ref[0, :, lanes]
            for axis in range(3):
                out[j, channels + axis : channels + axis + 1, :] = pos_ref[axis, :, lanes]
            out[j, channels + 3 :, :] = jnp.zeros((out.shape[1] - channels - 3, LANES), f32)


def pack(split, place, faces, pos, feat, rows):
    ghost, sides = faces.shape
    vm = pl.BlockSpec(memory_space=pltpu.VMEM)
    sm = pl.BlockSpec(memory_space=pltpu.SMEM)
    side = jax.ShapeDtypeStruct((ghost, feat.shape[1] + 8, LANES), f32)
    return pl.pallas_call(
        functools.partial(pack_kernel, rows),
        out_shape=(side,) * sides,
        in_specs=[sm, sm, sm, vm, vm],
        out_specs=(vm,) * sides,
        name="pack",
    )(split, place, faces, pos, feat)


def finish_kernel(rows, split_ref, place_ref, faces_ref, own_ref, *refs):
    forces_ref = refs[-1]
    listed = shared_blocks(faces_ref, rows, split_ref[0], place_ref[0], place_ref[1])
    for number in range(own_ref.shape[1] // LANES):
        lanes = slice(number * LANES, (number + 1) * LANES)
        total = own_ref[:, lanes]
        for back, blocks in zip(refs[:-1], listed):
            for j, block in enumerate(blocks):
                total = total + jnp.where(block == number, back[j], 0.0)
        for axis in range(3):
            forces_ref[axis, :, lanes] = -total[axis : axis + 1]


def finish(split, place, faces, own, backs, rows):
    vm = pl.BlockSpec(memory_space=pltpu.VMEM)
    sm = pl.BlockSpec(memory_space=pltpu.SMEM)
    return pl.pallas_call(
        functools.partial(finish_kernel, rows),
        out_shape=jax.ShapeDtypeStruct((3, 1, own.shape[1]), f32),
        in_specs=[sm, sm, sm] + [vm] * (1 + len(backs)),
        out_specs=vm,
        name="finish",
    )(split, place, faces, own, *backs)


def row_swaps(rows, cols, odd, lower_shift=0, upper_shift=0):
    pairs = []
    for c in range(cols):
        for g in range(rows):
            if g % 2 == odd:
                target = (g + 1, c) if g < rows - 1 else (0, (c + lower_shift) % cols)
            else:
                target = (g - 1, c) if g > 0 else (rows - 1, (c - upper_shift) % cols)
            pairs.append((c * rows + g, target[1] * rows + target[0]))
    return pairs


def column_swaps(rows, cols, odd):
    pairs = []
    for c in range(cols):
        target = (c + 1 if c % 2 == odd else c - 1) % cols
        pairs += [(c * rows + g, target * rows + g) for g in range(rows)]
    return pairs


def exchange(sides, branch, rows, cols, back):
    ghost = sides[0].shape[0]

    def send(value, perm):
        pairs = [(b, a) for a, b in perm] if back else perm
        return lax.ppermute(value, ("flow", "grad"), pairs)

    def case(number):
        shift, split = divmod(number, ghost)

        def crossing(value):
            if split == 0:
                return send(value, row_swaps(rows, cols, 1, shift, shift))
            parts = []
            for j in range(ghost):
                lower_shift = shift + (1 if j < split else 0)
                upper_shift = shift + (1 if j >= ghost - split else 0)
                parts.append(send(value[j : j + 1], row_swaps(rows, cols, 1, lower_shift, upper_shift)))
            return jnp.concatenate(parts, axis=0)

        def route(values):
            first, second, third, fourth = values
            first = crossing(first)
            fourth = send(fourth, column_swaps(rows, cols, 1))
            second = send(second, row_swaps(rows, cols, 0))
            third = send(third, column_swaps(rows, cols, 0))
            return (first, second, third, fourth)

        return route

    return lax.switch(branch, [case(number) for number in range(cols * ghost)], tuple(sides))


def body(
    positions,
    features,
    neighbours,
    face_blocks,
    shear_cells,
    split_block,
    radial_in,
    radial_out,
    mixing,
    readout,
):
    faces = jnp.transpose(face_blocks[0])
    entries, atoms = neighbours.shape[1:]
    ghost = faces.shape[0]
    rows = lax.axis_size("grad")
    cols = lax.axis_size("flow")
    place = jnp.stack([lax.axis_index("grad"), lax.axis_index("flow")]).astype(jnp.int32)
    branch = shear_cells[0] * ghost + split_block[0]
    branch = jnp.where(branch == cols * ghost, 0, branch)
    idx = jnp.transpose(neighbours[0]).reshape(atoms // GROUPS, GROUPS * entries)

    sides = pack(split_block, place, faces, positions, features, rows)
    sides = exchange(sides, branch, rows, cols, False)
    energy, own, *backs = core(
        split_block, place, idx, positions, features, radial_in, radial_out, mixing, readout.reshape(1, -1), sides, rows
    )
    backs = exchange(backs, branch, rows, cols, True)
    forces = finish(split_block, place, faces, own, backs, rows)
    return (energy, forces)


def solution(mesh):
    in_specs = (
        P(None, "grad", "flow"),
        P("grad", None, "flow"),
        P("grad", None, "flow"),
        P("grad", None, "flow"),
        P(),
        P(),
        P(),
        P(),
        P(),
        P(),
    )
    out_specs = (P("grad", "flow"), P(None, "grad", "flow"))
    return jax.shard_map(body, mesh=mesh, in_specs=in_specs, out_specs=out_specs, check_vma=False)
```

```python
import functools

import jax
import jax.numpy as jnp
from jax import lax
from jax.experimental import pallas as pl
from jax.experimental.pallas import tpu as pltpu
from jax.sharding import PartitionSpec as P

LANES = 128
GROUPS = 8
AHEAD = 16
BEHIND = 16
SHUFFLED = 4
SKEW = (2, 3, 4)
BACK_SKEW = 3
highest = lax.Precision.HIGHEST
root_three = 3.0**0.5
root_five = 5.0**0.5
root_fifteen = 15.0**0.5
f32 = jnp.float32
bf16 = jnp.bfloat16


def halves(value):
    upper = value.astype(bf16).astype(f32)
    return upper, value - upper


def nt(left, right, precision=None):
    return lax.dot_general(left, right, (((1,), (1,)), ((), ())), precision=precision, preferred_element_type=f32)


def core_kernel(groups, rows, split_ref, row_ref, col_ref, idx_ref, own_pos, own_feat, win_ref, wout_ref, mix_ref, read_ref,
                first_ref, second_ref, third_ref, fourth_ref,
                energy_ref, own_ref, first_back, second_back, third_back, fourth_back,
                xyz_scr, d_scr, x_scr, f_scr, w_scr, dw_scr, mom_scr, g_scr, acc_scr, cen_scr):
    split = split_ref[0]
    row = row_ref[0]
    row_odd = lax.rem(row, 2) == 1
    col_odd = lax.rem(col_ref[0], 2) == 1
    atoms = own_pos.shape[2]
    channels = own_feat.shape[1]
    number, hidden = win_ref.shape
    ghost = first_ref.shape[0]
    tiles, tile = idx_ref.shape
    neighbours = tile // groups
    own_chunks = atoms // LANES
    sides = (
        (col_odd, third_ref, fourth_ref),
        (col_odd, fourth_ref, third_ref),
        (row_odd, second_ref, first_ref),
        (row_odd, first_ref, second_ref),
    )
    chunks = own_chunks + len(sides) * ghost
    factor = neighbours ** (-0.5)

    def side(k, j, part):
        odd, one, other = sides[k]
        return jnp.where(odd, one[j, part, :], other[j, part, :])

    def pos_chunk(c, axis):
        if c < own_chunks:
            return own_pos[axis, :, c * LANES : (c + 1) * LANES]
        k, j = divmod(c - own_chunks, ghost)
        line = side(k, j, slice(channels + axis, channels + axis + 1))
        fraction = split.astype(f32) / ghost
        if axis == 0:
            if k < 2:
                line = line + (2.0 * k - 1.0)
            elif k == 2:
                line = line + jnp.where(row == 0, jnp.where(j < split, fraction - 1.0, fraction), 0.0)
            else:
                line = line + jnp.where(
                    row == rows - 1, jnp.where(j < ghost - split, -fraction, 1.0 - fraction), 0.0
                )
        elif axis == 1 and k >= 2:
            line = line + (2.0 * k - 5.0)
        return line

    def place_features(c):
        lanes = slice(c * LANES, (c + 1) * LANES)
        if c < own_chunks:
            feat = own_feat[0, :, lanes]
        else:
            k, j = divmod(c - own_chunks, ghost)
            feat = side(k, j, slice(0, channels))
        if c < SHUFFLED:
            x_scr[:, lanes] = feat
        else:
            hi, lo = halves(feat)
            lanes = slice((c - SHUFFLED) * LANES, (c - SHUFFLED + 1) * LANES)
            f_scr[0:channels, lanes] = hi.astype(bf16)
            f_scr[channels : 2 * channels, lanes] = lo.astype(bf16)

    waiting = list(range(chunks))

    blocks = tile // LANES
    for lb in range(blocks):
        lanes = slice(lb * LANES, (lb + 1) * LANES)
        idx = idx_ref[:, lanes]
        low = jnp.bitwise_and(idx, LANES - 1)
        chunk = jnp.right_shift(idx, LANES.bit_length() - 1)
        lines = lax.broadcasted_iota(jnp.int32, idx.shape, 0)
        cols = lax.broadcasted_iota(jnp.int32, idx.shape, 1) + lb * LANES
        centre = lines * groups + cols // neighbours
        clow = jnp.bitwise_and(centre, LANES - 1)
        cchunk = jnp.right_shift(centre, LANES.bit_length() - 1)
        for axis in range(3):
            other = None
            mine = None
            for c in range(chunks):
                src = jnp.broadcast_to(pos_chunk(c, axis), idx.shape)
                got = jnp.take_along_axis(src, low, axis=1)
                other = got if other is None else jnp.where(chunk == c, got, other)
                if c < own_chunks:
                    got = jnp.take_along_axis(src, clow, axis=1)
                    mine = got if mine is None else jnp.where(cchunk == c, got, mine)
            xyz_scr[axis, :, lanes] = other - mine
            for c in waiting[:2]:
                place_features(c)
            del waiting[:2]

    for c in waiting:
        place_features(c)

    d_scr[...] = jnp.zeros(d_scr.shape, f32)
    d_scr[0:number, 0:hidden] = win_ref[...]
    d_scr[number : 2 * number, hidden : 2 * hidden] = win_ref[...]
    dhi, dlo = halves(d_scr[...])
    first = jnp.transpose(jnp.concatenate([dhi, dhi, dlo, dlo], axis=0)).astype(bf16)
    ohi, olo = halves(wout_ref[...])
    second = jnp.transpose(jnp.concatenate([ohi, ohi, olo, olo], axis=0)).astype(bf16)

    row_iota = lax.broadcasted_iota(jnp.int32, (groups, tile), 0)
    lane_iota = lax.broadcasted_iota(jnp.int32, (groups, tile), 1)
    mine_mask = row_iota == lane_iota // neighbours
    centres = lax.broadcasted_iota(jnp.int32, (number, tile), 0).astype(f32) * (6.0 / (number - 1))
    entry_iota = lax.broadcasted_iota(jnp.int16, ((chunks - SHUFFLED) * LANES, tile), 0)

    def spread(axis, t, lines=groups):
        return jnp.broadcast_to(xyz_scr[axis, pl.ds(t, 1), :], (lines, tile))

    def harmonics(x, y, z):
        square = x * x + y * y + z * z
        return [
            jnp.ones_like(x),
            root_three * x,
            root_three * y,
            root_three * z,
            root_fifteen * x * y,
            root_fifteen * y * z,
            0.5 * root_five * (3.0 * z * z - square),
            root_fifteen * x * z,
            0.5 * root_fifteen * (x * x - y * y),
        ]

    def stacked(value):
        hi, lo = halves(value)
        return jnp.concatenate([hi, lo, hi, lo], axis=0).astype(bf16)

    def spread_idx(t, lines):
        return jnp.broadcast_to(idx_ref[pl.ds(t, 1), :], (lines, tile))

    def basis_stage(t):
        x, y, z = (spread(axis, t, number) for axis in range(3))
        away = x * x + y * y + z * z - centres
        scaled = away / 0.75
        gauss = jnp.exp(-0.5 * (scaled * scaled))
        slope = gauss * (away * (-1.0 / 0.5625))
        basis = stacked(jnp.concatenate([gauss, slope], axis=0))
        return jnp.dot(first, basis, preferred_element_type=f32)

    def gather_stage(t):
        listed = spread_idx(t, 16).astype(jnp.int16)
        listed = jnp.concatenate([listed - SHUFFLED * LANES] * ((chunks - SHUFFLED) * LANES // 16), axis=0)
        picks = jnp.where(listed == entry_iota, jnp.ones((), bf16), jnp.zeros((), bf16))
        return jnp.dot(f_scr[...], picks, preferred_element_type=f32)

    def hidden_stage(both):
        h, dh = both[0:hidden], both[hidden : 2 * hidden]
        sig = 0.5 * jnp.tanh(0.5 * h) + 0.5
        act = h * sig
        dact = dh * (sig + act * (1.0 - sig))
        radial = jnp.dot(second, stacked(act), preferred_element_type=f32)
        dradial = jnp.dot(second, stacked(dact), preferred_element_type=f32)
        return radial, dradial

    def feature_stage(t, part):
        feat = part[0:channels] + part[channels:]
        listed = spread_idx(t, channels)
        low = jnp.bitwise_and(listed, LANES - 1)
        chunk = jnp.right_shift(listed, LANES.bit_length() - 1)
        lines = []
        for lb in range(tile // LANES):
            lanes = slice(lb * LANES, (lb + 1) * LANES)
            line = feat[:, lanes]
            for c in range(SHUFFLED):
                moved = jnp.take_along_axis(x_scr[:, c * LANES : (c + 1) * LANES], low[:, lanes], axis=1)
                line = jnp.where(chunk[:, lanes] == c, moved, line)
            lines.append(line)
        return jnp.concatenate(lines, axis=1)

    def weight_stage(t, radial, dradial, feat):
        whi, wlo = halves(radial * feat)
        weight = jnp.concatenate([whi, wlo], axis=0).astype(bf16)
        w_scr[t] = weight
        whi, wlo = halves(dradial * feat)
        dw_scr[t] = jnp.concatenate([whi, wlo], axis=0).astype(bf16)
        return weight

    def moment_stage(t, weight):
        his, los = [], []
        for value in harmonics(*(spread(axis, t) for axis in range(3))):
            hi, lo = halves(jnp.where(mine_mask, value, 0.0))
            his.append(hi)
            los.append(lo)
        out = nt(jnp.concatenate(his + los, axis=0).astype(bf16), weight)
        n = 9 * groups
        total = (out[0:n, 0:channels] + out[0:n, channels:]) + out[n : 2 * n, 0:channels]
        base = pl.multiple_of(t * groups, groups)
        for m in range(9):
            mom_scr[m, pl.ds(base, groups), :] = total[m * groups : (m + 1) * groups] * factor

    def forward(step, carry):
        numbers = [step * AHEAD + u for u in range(AHEAD)]
        boths, parts, nets, weights = {}, {}, {}, {}
        for u in range(AHEAD + SKEW[-1]):
            if u < AHEAD:
                boths[u] = basis_stage(numbers[u])
                parts[u] = gather_stage(numbers[u])
            v = u - SKEW[0]
            if 0 <= v < AHEAD:
                nets[v] = hidden_stage(boths.pop(v))
            v = u - SKEW[1]
            if 0 <= v < AHEAD:
                feat = feature_stage(numbers[v], parts.pop(v))
                weights[v] = weight_stage(numbers[v], *nets.pop(v), feat)
            v = u - SKEW[2]
            if 0 <= v < AHEAD:
                moment_stage(numbers[v], weights.pop(v))
        return carry

    lax.fori_loop(0, tiles // AHEAD, forward, 0)

    degree = [0, 1, 1, 1, 2, 2, 2, 2, 2]
    count = len(degree)
    invariants = []
    for l in range(3):
        total = None
        for m in range(count):
            if degree[m] == l:
                sq = mom_scr[m] * mom_scr[m]
                total = sq if total is None else total + sq
        invariants.append(total)
    upper, lower, back_upper, back_lower = [], [], [], []
    blank = jnp.zeros((channels, channels), f32)
    for l in range(3):
        hi, lo = halves(mix_ref[l])
        upper.append(jnp.concatenate([hi, lo], axis=1))
        back_upper.append(jnp.concatenate([hi, hi], axis=1))
        back_lower.append(jnp.concatenate([lo, blank], axis=1))
    pieces = [halves(value) for value in invariants]
    left = jnp.concatenate([hi for hi, _ in pieces] + [lo for _, lo in pieces], axis=1).astype(bf16)
    mixed = jnp.dot(left, jnp.concatenate(upper + upper, axis=0).astype(bf16), preferred_element_type=f32)
    mixed = mixed[:, 0:channels] + mixed[:, channels:]
    sig = 0.5 * jnp.tanh(0.5 * mixed) + 0.5
    act = mixed * sig
    reads = read_ref[...]
    rhi, rlo = (jnp.broadcast_to(value, (8, channels)) for value in halves(reads))
    rows_of = jnp.concatenate([jnp.concatenate([rhi, rhi], axis=1), jnp.concatenate([rlo, rlo], axis=1)], axis=0)
    sums = nt(rows_of.astype(bf16), jnp.concatenate(halves(act), axis=1).astype(bf16))
    energy_ref[...] = sums[0:1] + sums[8:9]
    dmixed = reads * (sig + act * (1.0 - sig))
    dleft = jnp.concatenate(halves(dmixed), axis=1).astype(bf16)
    dinvs = nt(dleft, jnp.concatenate(back_upper + back_lower, axis=0).astype(bf16))
    for l in range(3):
        upto = (3 + l) * channels
        dinv = (dinvs[:, l * channels : (l + 1) * channels] + dinvs[:, upto : upto + channels]) * (2.0 * factor)
        for m in range(count):
            if degree[m] == l:
                hi, lo = halves(dinv * mom_scr[m])
                g_scr[:, m * groups : (m + 1) * groups, :] = hi.reshape(tiles, groups, channels)
                g_scr[:, (count + m) * groups : (count + m + 1) * groups, :] = lo.reshape(tiles, groups, channels)

    acc_scr[...] = jnp.zeros(acc_scr.shape, f32)
    padded = acc_scr.shape[0] // 6
    chunk_iota = lax.broadcasted_iota(jnp.int32, (padded, tile), 0)
    lane_rows = lax.broadcasted_iota(jnp.int16, (LANES, tile), 0)
    n = count * groups

    def pull_stage(t):
        g = g_scr[t]
        gl = jnp.concatenate(
            [g.astype(bf16), jnp.concatenate([g[0:n], jnp.zeros((n, channels), f32)], axis=0).astype(bf16)], axis=1
        )
        a = jnp.dot(gl, w_scr[t], preferred_element_type=f32)
        b = jnp.dot(gl, dw_scr[t], preferred_element_type=f32)
        return a, b

    def force_stage(t, a, b):
        x, y, z = spread(0, t), spread(1, t), spread(2, t)
        values = harmonics(x, y, z)
        A = [a[m * groups : (m + 1) * groups] + a[n + m * groups : n + (m + 1) * groups] for m in range(count)]
        rad = None
        for m in range(count):
            B = b[m * groups : (m + 1) * groups] + b[n + m * groups : n + (m + 1) * groups]
            rad = B if m == 0 else rad + values[m] * B
        rad = 2.0 * rad
        dx = root_three * A[1] + root_fifteen * (y * A[4] + z * A[7] + x * A[8]) - root_five * (x * A[6]) + x * rad
        dy = root_three * A[2] + root_fifteen * (x * A[4] + z * A[5] - y * A[8]) - root_five * (y * A[6]) + y * rad
        dz = root_three * A[3] + root_fifteen * (y * A[5] + x * A[7]) + (2.0 * root_five) * (z * A[6]) + z * rad
        comps = [jnp.where(mine_mask, v, 0.0) for v in (dx, dy, dz)]
        base = pl.multiple_of(t * groups, groups)
        lane = lax.broadcasted_iota(jnp.int32, (groups, LANES), 1)
        cen = jnp.zeros((groups, LANES), f32)
        for i, v in enumerate(comps):
            cen = jnp.where(lane == i, jnp.sum(v, axis=1, keepdims=True), cen)
        cen_scr[pl.ds(base, groups), :] = cen
        chunk = jnp.right_shift(idx_ref[pl.ds(t, 1), :], LANES.bit_length() - 1)
        hit = jnp.broadcast_to(chunk, (padded, tile)) == chunk_iota
        his, los = [], []
        for v in comps:
            hi, lo = halves(jnp.sum(v, axis=0, keepdims=True))
            his.append(jnp.where(hit, jnp.broadcast_to(hi, (padded, tile)), 0.0))
            los.append(jnp.where(hit, jnp.broadcast_to(lo, (padded, tile)), 0.0))
        left = jnp.concatenate(his + los, axis=0).astype(bf16)
        low = spread_idx(t, 16).astype(jnp.int16) & jnp.int16(LANES - 1)
        low = jnp.concatenate([low] * (LANES // 16), axis=0)
        right = jnp.where(low == lane_rows, jnp.ones((), bf16), jnp.zeros((), bf16))
        return left, right

    def backward(step, carry):
        numbers = [step * BEHIND + u for u in range(BEHIND)]
        pulls, total = {}, None
        for u in range(BEHIND + BACK_SKEW):
            if u < BEHIND:
                pulls[u] = pull_stage(numbers[u])
            v = u - BACK_SKEW
            if 0 <= v < BEHIND:
                left, right = force_stage(numbers[v], *pulls.pop(v))
                part = nt(left, right)
                total = part if total is None else total + part
        acc_scr[...] += total
        return carry

    lax.fori_loop(0, tiles // BEHIND, backward, 0)

    half = 3 * padded
    cen = jnp.concatenate(
        [jnp.transpose(cen_scr[c * LANES : (c + 1) * LANES, :])[0:8] for c in range(own_chunks)], axis=1
    )
    for axis in range(3):
        lo = axis * padded
        sums = acc_scr[lo : lo + padded] + acc_scr[half + lo : half + lo + padded]
        for c in range(own_chunks):
            own_ref[axis : axis + 1, c * LANES : (c + 1) * LANES] = (
                sums[c : c + 1] - cen[axis : axis + 1, c * LANES : (c + 1) * LANES]
            )
        left, right, lower, upper = (
            [sums[own_chunks + k * ghost + j : own_chunks + k * ghost + j + 1] for j in range(ghost)] for k in range(4)
        )
        for back, odd, one, other in (
            (first_back, row_odd, upper, lower),
            (second_back, row_odd, lower, upper),
            (third_back, col_odd, left, right),
            (fourth_back, col_odd, right, left),
        ):
            for j in range(ghost):
                back[j, axis : axis + 1, :] = jnp.where(odd, one[j], other[j])


def core(split, place, idx, own_pos, own_feat, win, wout, mixing, readout, sides, rows):
    atoms = own_pos.shape[2]
    channels = own_feat.shape[1]
    tiles, tile = idx.shape
    ghost = sides[0].shape[0]
    number, hidden = win.shape
    extent = atoms + len(sides) * ghost * LANES
    padded = -(-extent // (LANES * 16)) * 16
    vm = pl.BlockSpec(memory_space=pltpu.VMEM)
    sm = pl.BlockSpec(memory_space=pltpu.SMEM)
    back = jax.ShapeDtypeStruct((ghost, 3, LANES), f32)
    return pl.pallas_call(
        functools.partial(core_kernel, GROUPS, rows),
        out_shape=(
            jax.ShapeDtypeStruct((1, atoms), f32),
            jax.ShapeDtypeStruct((3, atoms), f32),
        ) + (back,) * len(sides),
        in_specs=[sm, sm, sm] + [vm] * (7 + len(sides)),
        out_specs=(vm,) * (2 + len(sides)),
        scratch_shapes=[
            pltpu.VMEM((3, tiles, tile), f32),
            pltpu.VMEM((2 * number, 2 * hidden), f32),
            pltpu.VMEM((channels, SHUFFLED * LANES), f32),
            pltpu.VMEM((2 * channels, extent - SHUFFLED * LANES), bf16),
            pltpu.VMEM((tiles, 2 * channels, tile), bf16),
            pltpu.VMEM((tiles, 2 * channels, tile), bf16),
            pltpu.VMEM((9, atoms, channels), f32),
            pltpu.VMEM((tiles, 18 * GROUPS, channels), f32),
            pltpu.VMEM((6 * padded, LANES), f32),
            pltpu.VMEM((atoms, LANES), f32),
        ],
        compiler_params=pltpu.CompilerParams(vmem_limit_bytes=32 << 20),
        name="core",
    )(split, *place, idx, own_pos, own_feat, win, wout, mixing, readout, *sides)


def source_slot(slot, ghost, row, rows, split):
    raised = lax.rem(slot + split, ghost)
    lowered = lax.rem(slot - split + ghost, ghost)
    return jnp.where(row == 0, raised, jnp.where(row == rows - 1, lowered, slot))


def shared_blocks(faces_ref, rows, split, row, col):
    ghost = faces_ref.shape[0]
    row_odd = lax.rem(row, 2)
    col_odd = lax.rem(col, 2)
    return [
        [faces_ref[source_slot(j, ghost, row, rows, split), 3 - row_odd] for j in range(ghost)],
        [faces_ref[j, 2 + row_odd] for j in range(ghost)],
        [faces_ref[j, col_odd] for j in range(ghost)],
        [faces_ref[j, 1 - col_odd] for j in range(ghost)],
    ]


def pack_kernel(rows, split_ref, row_ref, col_ref, faces_ref, pos_ref, feat_ref, *out_refs):
    channels = feat_ref.shape[1]
    listed = shared_blocks(faces_ref, rows, split_ref[0], row_ref[0], col_ref[0])
    for out, blocks in zip(out_refs, listed):
        for j, block in enumerate(blocks):
            lanes = pl.ds(pl.multiple_of(block * LANES, LANES), LANES)
            out[j, 0:channels, :] = feat_ref[0, :, lanes]
            for axis in range(3):
                out[j, channels + axis : channels + axis + 1, :] = pos_ref[axis, :, lanes]
            out[j, channels + 3 :, :] = jnp.zeros((out.shape[1] - channels - 3, LANES), f32)


def pack(split, place, faces, pos, feat, rows):
    ghost, sides = faces.shape
    vm = pl.BlockSpec(memory_space=pltpu.VMEM)
    sm = pl.BlockSpec(memory_space=pltpu.SMEM)
    side = jax.ShapeDtypeStruct((ghost, feat.shape[1] + 8, LANES), f32)
    return pl.pallas_call(
        functools.partial(pack_kernel, rows),
        out_shape=(side,) * sides,
        in_specs=[sm, sm, sm, sm, vm, vm],
        out_specs=(vm,) * sides,
        name="pack",
    )(split, *place, faces, pos, feat)


def finish_kernel(rows, split_ref, row_ref, col_ref, faces_ref, own_ref, *refs):
    forces_ref = refs[-1]
    listed = shared_blocks(faces_ref, rows, split_ref[0], row_ref[0], col_ref[0])
    for number in range(own_ref.shape[1] // LANES):
        lanes = slice(number * LANES, (number + 1) * LANES)
        total = own_ref[:, lanes]
        for back, blocks in zip(refs[:-1], listed):
            for j, block in enumerate(blocks):
                total = total + jnp.where(block == number, back[j], 0.0)
        for axis in range(3):
            forces_ref[axis, :, lanes] = -total[axis : axis + 1]


def finish(split, place, faces, own, backs, rows):
    vm = pl.BlockSpec(memory_space=pltpu.VMEM)
    sm = pl.BlockSpec(memory_space=pltpu.SMEM)
    return pl.pallas_call(
        functools.partial(finish_kernel, rows),
        out_shape=jax.ShapeDtypeStruct((3, 1, own.shape[1]), f32),
        in_specs=[sm, sm, sm, sm] + [vm] * (1 + len(backs)),
        out_specs=vm,
        name="finish",
    )(split, *place, faces, own, *backs)


def row_swaps(rows, cols, odd, lower_shift=0, upper_shift=0):
    pairs = []
    for c in range(cols):
        for g in range(rows):
            if g % 2 == odd:
                target = (g + 1, c) if g < rows - 1 else (0, (c + lower_shift) % cols)
            else:
                target = (g - 1, c) if g > 0 else (rows - 1, (c - upper_shift) % cols)
            pairs.append((c * rows + g, target[1] * rows + target[0]))
    return pairs


def column_swaps(rows, cols, odd):
    pairs = []
    for c in range(cols):
        target = (c + 1 if c % 2 == odd else c - 1) % cols
        pairs += [(c * rows + g, target * rows + g) for g in range(rows)]
    return pairs


def exchange(sides, branch, rows, cols, back):
    ghost = sides[0].shape[0]

    def send(value, perm):
        pairs = [(b, a) for a, b in perm] if back else perm
        return lax.ppermute(value, ("flow", "grad"), pairs)

    def case(number):
        shift, split = divmod(number, ghost)

        def crossing(value):
            if split == 0:
                return send(value, row_swaps(rows, cols, 1, shift, shift))
            parts = []
            for j in range(ghost):
                lower_shift = shift + (1 if j < split else 0)
                upper_shift = shift + (1 if j >= ghost - split else 0)
                parts.append(send(value[j : j + 1], row_swaps(rows, cols, 1, lower_shift, upper_shift)))
            return jnp.concatenate(parts, axis=0)

        def route(values):
            first, second, third, fourth = values
            first = crossing(first)
            fourth = send(fourth, column_swaps(rows, cols, 1))
            second = send(second, row_swaps(rows, cols, 0))
            third = send(third, column_swaps(rows, cols, 0))
            return (first, second, third, fourth)

        return route

    return lax.switch(branch, [case(number) for number in range(cols * ghost)], tuple(sides))


def body(
    positions,
    features,
    neighbours,
    face_blocks,
    shear_cells,
    split_block,
    radial_in,
    radial_out,
    mixing,
    readout,
):
    faces = jnp.transpose(face_blocks[0])
    entries, atoms = neighbours.shape[1:]
    ghost = faces.shape[0]
    rows = lax.axis_size("grad")
    cols = lax.axis_size("flow")
    place = tuple(lax.axis_index(axis).astype(jnp.int32).reshape(1) for axis in ("grad", "flow"))
    branch = shear_cells[0] * ghost + split_block[0]
    branch = jnp.where(branch == cols * ghost, 0, branch)
    idx = jnp.transpose(neighbours[0]).reshape(atoms // GROUPS, GROUPS * entries)

    sides = pack(split_block, place, faces, positions, features, rows)
    sides = exchange(sides, branch, rows, cols, False)
    energy, own, *backs = core(
        split_block, place, idx, positions, features, radial_in, radial_out, mixing, readout.reshape(1, -1), sides, rows
    )
    backs = exchange(backs, branch, rows, cols, True)
    forces = finish(split_block, place, faces, own, backs, rows)
    return (energy, forces)


def solution(mesh):
    in_specs = (
        P(None, "grad", "flow"),
        P("grad", None, "flow"),
        P("grad", None, "flow"),
        P("grad", None, "flow"),
        P(),
        P(),
        P(),
        P(),
        P(),
        P(),
    )
    out_specs = (P("grad", "flow"), P(None, "grad", "flow"))
    return jax.shard_map(body, mesh=mesh, in_specs=in_specs, out_specs=out_specs, check_vma=False)
```

```python
import functools

import jax
import jax.numpy as jnp
from jax import lax
from jax.experimental import pallas as pl
from jax.experimental.pallas import tpu as pltpu
from jax.sharding import PartitionSpec as P

LANES = 128
GROUPS = 8
AHEAD = 16
BEHIND = 16
SHUFFLED = 4
SKEW = (2, 3, 4)
BACK_SKEW = 3
highest = lax.Precision.HIGHEST
root_three = 3.0**0.5
root_five = 5.0**0.5
root_fifteen = 15.0**0.5
f32 = jnp.float32
bf16 = jnp.bfloat16


def halves(value):
    upper = value.astype(bf16).astype(f32)
    return upper, value - upper


def nt(left, right, precision=None):
    return lax.dot_general(left, right, (((1,), (1,)), ((), ())), precision=precision, preferred_element_type=f32)


def core_kernel(groups, rows, split_ref, row_ref, col_ref, listed_ref, own_pos, own_feat, win_ref, wout_ref, mix_ref, read_ref,
                first_ref, second_ref, third_ref, fourth_ref,
                energy_ref, own_ref, first_back, second_back, third_back, fourth_back,
                turn_scr, idx_ref, xyz_scr, d_scr, x_scr, f_scr, w_scr, dw_scr, mom_scr, g_scr, acc_scr, cen_scr):
    split = split_ref[0]
    row = row_ref[0]
    row_odd = lax.rem(row, 2) == 1
    col_odd = lax.rem(col_ref[0], 2) == 1
    atoms = own_pos.shape[2]
    channels = own_feat.shape[1]
    number, hidden = win_ref.shape
    ghost = first_ref.shape[0]
    tiles, tile = idx_ref.shape
    neighbours = listed_ref.shape[1]
    own_chunks = atoms // LANES
    sides = (
        (col_odd, third_ref, fourth_ref),
        (col_odd, fourth_ref, third_ref),
        (row_odd, second_ref, first_ref),
        (row_odd, first_ref, second_ref),
    )
    chunks = own_chunks + len(sides) * ghost
    factor = neighbours ** (-0.5)

    def side(k, j, part):
        odd, one, other = sides[k]
        return jnp.where(odd, one[j, part, :], other[j, part, :])

    def pos_chunk(c, axis):
        if c < own_chunks:
            return own_pos[axis, :, c * LANES : (c + 1) * LANES]
        k, j = divmod(c - own_chunks, ghost)
        line = side(k, j, slice(channels + axis, channels + axis + 1))
        fraction = split.astype(f32) / ghost
        if axis == 0:
            if k < 2:
                line = line + (2.0 * k - 1.0)
            elif k == 2:
                line = line + jnp.where(row == 0, jnp.where(j < split, fraction - 1.0, fraction), 0.0)
            else:
                line = line + jnp.where(
                    row == rows - 1, jnp.where(j < ghost - split, -fraction, 1.0 - fraction), 0.0
                )
        elif axis == 1 and k >= 2:
            line = line + (2.0 * k - 5.0)
        return line

    for c in range(own_chunks):
        rows_of = slice(c * LANES, (c + 1) * LANES)
        turn_scr[rows_of, :] = jnp.transpose(listed_ref[0, :, rows_of])
    for a in range(groups):
        idx_ref[:, a * neighbours : (a + 1) * neighbours] = turn_scr[pl.ds(a, tiles, stride=groups), :]

    def place_features(c):
        lanes = slice(c * LANES, (c + 1) * LANES)
        if c < own_chunks:
            feat = own_feat[0, :, lanes]
        else:
            k, j = divmod(c - own_chunks, ghost)
            feat = side(k, j, slice(0, channels))
        if c < SHUFFLED:
            x_scr[:, lanes] = feat
        else:
            hi, lo = halves(feat)
            lanes = slice((c - SHUFFLED) * LANES, (c - SHUFFLED + 1) * LANES)
            f_scr[0:channels, lanes] = hi.astype(bf16)
            f_scr[channels : 2 * channels, lanes] = lo.astype(bf16)

    waiting = list(range(chunks))

    blocks = tile // LANES
    for lb in range(blocks):
        lanes = slice(lb * LANES, (lb + 1) * LANES)
        idx = idx_ref[:, lanes]
        low = jnp.bitwise_and(idx, LANES - 1)
        chunk = jnp.right_shift(idx, LANES.bit_length() - 1)
        lines = lax.broadcasted_iota(jnp.int32, idx.shape, 0)
        cols = lax.broadcasted_iota(jnp.int32, idx.shape, 1) + lb * LANES
        centre = lines * groups + cols // neighbours
        clow = jnp.bitwise_and(centre, LANES - 1)
        cchunk = jnp.right_shift(centre, LANES.bit_length() - 1)
        for axis in range(3):
            other = None
            mine = None
            for c in range(chunks):
                src = jnp.broadcast_to(pos_chunk(c, axis), idx.shape)
                got = jnp.take_along_axis(src, low, axis=1)
                other = got if other is None else jnp.where(chunk == c, got, other)
                if c < own_chunks:
                    got = jnp.take_along_axis(src, clow, axis=1)
                    mine = got if mine is None else jnp.where(cchunk == c, got, mine)
            xyz_scr[axis, :, lanes] = other - mine
            for c in waiting[:2]:
                place_features(c)
            del waiting[:2]

    for c in waiting:
        place_features(c)

    d_scr[...] = jnp.zeros(d_scr.shape, f32)
    d_scr[0:number, 0:hidden] = win_ref[...]
    d_scr[number : 2 * number, hidden : 2 * hidden] = win_ref[...]
    dhi, dlo = halves(d_scr[...])
    first = jnp.transpose(jnp.concatenate([dhi, dhi, dlo, dlo], axis=0)).astype(bf16)
    ohi, olo = halves(wout_ref[...])
    second = jnp.transpose(jnp.concatenate([ohi, ohi, olo, olo], axis=0)).astype(bf16)

    row_iota = lax.broadcasted_iota(jnp.int32, (groups, tile), 0)
    lane_iota = lax.broadcasted_iota(jnp.int32, (groups, tile), 1)
    mine_mask = row_iota == lane_iota // neighbours
    centres = lax.broadcasted_iota(jnp.int32, (number, tile), 0).astype(f32) * (6.0 / (number - 1))
    entry_iota = lax.broadcasted_iota(jnp.int16, ((chunks - SHUFFLED) * LANES, tile), 0)

    def spread(axis, t, lines=groups):
        return jnp.broadcast_to(xyz_scr[axis, pl.ds(t, 1), :], (lines, tile))

    def harmonics(x, y, z):
        square = x * x + y * y + z * z
        return [
            jnp.ones_like(x),
            root_three * x,
            root_three * y,
            root_three * z,
            root_fifteen * x * y,
            root_fifteen * y * z,
            0.5 * root_five * (3.0 * z * z - square),
            root_fifteen * x * z,
            0.5 * root_fifteen * (x * x - y * y),
        ]

    def stacked(value):
        hi, lo = halves(value)
        return jnp.concatenate([hi, lo, hi, lo], axis=0).astype(bf16)

    def spread_idx(t, lines):
        return jnp.broadcast_to(idx_ref[pl.ds(t, 1), :], (lines, tile))

    def basis_stage(t):
        x, y, z = (spread(axis, t, number) for axis in range(3))
        away = x * x + y * y + z * z - centres
        scaled = away / 0.75
        gauss = jnp.exp(-0.5 * (scaled * scaled))
        slope = gauss * (away * (-1.0 / 0.5625))
        basis = stacked(jnp.concatenate([gauss, slope], axis=0))
        return jnp.dot(first, basis, preferred_element_type=f32)

    def gather_stage(t):
        listed = spread_idx(t, 16).astype(jnp.int16)
        listed = jnp.concatenate([listed - SHUFFLED * LANES] * ((chunks - SHUFFLED) * LANES // 16), axis=0)
        picks = jnp.where(listed == entry_iota, jnp.ones((), bf16), jnp.zeros((), bf16))
        return jnp.dot(f_scr[...], picks, preferred_element_type=f32)

    def hidden_stage(both):
        h, dh = both[0:hidden], both[hidden : 2 * hidden]
        sig = 0.5 * jnp.tanh(0.5 * h) + 0.5
        act = h * sig
        dact = dh * (sig + act * (1.0 - sig))
        radial = jnp.dot(second, stacked(act), preferred_element_type=f32)
        dradial = jnp.dot(second, stacked(dact), preferred_element_type=f32)
        return radial, dradial

    def feature_stage(t, part):
        feat = part[0:channels] + part[channels:]
        listed = spread_idx(t, channels)
        low = jnp.bitwise_and(listed, LANES - 1)
        chunk = jnp.right_shift(listed, LANES.bit_length() - 1)
        lines = []
        for lb in range(tile // LANES):
            lanes = slice(lb * LANES, (lb + 1) * LANES)
            line = feat[:, lanes]
            for c in range(SHUFFLED):
                moved = jnp.take_along_axis(x_scr[:, c * LANES : (c + 1) * LANES], low[:, lanes], axis=1)
                line = jnp.where(chunk[:, lanes] == c, moved, line)
            lines.append(line)
        return jnp.concatenate(lines, axis=1)

    def weight_stage(t, radial, dradial, feat):
        whi, wlo = halves(radial * feat)
        weight = jnp.concatenate([whi, wlo], axis=0).astype(bf16)
        w_scr[t] = weight
        whi, wlo = halves(dradial * feat)
        dw_scr[t] = jnp.concatenate([whi, wlo], axis=0).astype(bf16)
        return weight

    def moment_stage(t, weight):
        his, los = [], []
        for value in harmonics(*(spread(axis, t) for axis in range(3))):
            hi, lo = halves(jnp.where(mine_mask, value, 0.0))
            his.append(hi)
            los.append(lo)
        out = nt(jnp.concatenate(his + los, axis=0).astype(bf16), weight)
        n = 9 * groups
        total = (out[0:n, 0:channels] + out[0:n, channels:]) + out[n : 2 * n, 0:channels]
        base = pl.multiple_of(t * groups, groups)
        for m in range(9):
            mom_scr[m, pl.ds(base, groups), :] = total[m * groups : (m + 1) * groups] * factor

    def forward(step, carry):
        numbers = [step * AHEAD + u for u in range(AHEAD)]
        boths, parts, nets, weights = {}, {}, {}, {}
        for u in range(AHEAD + SKEW[-1]):
            if u < AHEAD:
                boths[u] = basis_stage(numbers[u])
                parts[u] = gather_stage(numbers[u])
            v = u - SKEW[0]
            if 0 <= v < AHEAD:
                nets[v] = hidden_stage(boths.pop(v))
            v = u - SKEW[1]
            if 0 <= v < AHEAD:
                feat = feature_stage(numbers[v], parts.pop(v))
                weights[v] = weight_stage(numbers[v], *nets.pop(v), feat)
            v = u - SKEW[2]
            if 0 <= v < AHEAD:
                moment_stage(numbers[v], weights.pop(v))
        return carry

    lax.fori_loop(0, tiles // AHEAD, forward, 0)

    degree = [0, 1, 1, 1, 2, 2, 2, 2, 2]
    count = len(degree)
    invariants = []
    for l in range(3):
        total = None
        for m in range(count):
            if degree[m] == l:
                sq = mom_scr[m] * mom_scr[m]
                total = sq if total is None else total + sq
        invariants.append(total)
    upper, lower, back_upper, back_lower = [], [], [], []
    blank = jnp.zeros((channels, channels), f32)
    for l in range(3):
        hi, lo = halves(mix_ref[l])
        upper.append(jnp.concatenate([hi, lo], axis=1))
        back_upper.append(jnp.concatenate([hi, hi], axis=1))
        back_lower.append(jnp.concatenate([lo, blank], axis=1))
    pieces = [halves(value) for value in invariants]
    left = jnp.concatenate([hi for hi, _ in pieces] + [lo for _, lo in pieces], axis=1).astype(bf16)
    mixed = jnp.dot(left, jnp.concatenate(upper + upper, axis=0).astype(bf16), preferred_element_type=f32)
    mixed = mixed[:, 0:channels] + mixed[:, channels:]
    sig = 0.5 * jnp.tanh(0.5 * mixed) + 0.5
    act = mixed * sig
    reads = read_ref[...]
    rhi, rlo = (jnp.broadcast_to(value, (8, channels)) for value in halves(reads))
    rows_of = jnp.concatenate([jnp.concatenate([rhi, rhi], axis=1), jnp.concatenate([rlo, rlo], axis=1)], axis=0)
    sums = nt(rows_of.astype(bf16), jnp.concatenate(halves(act), axis=1).astype(bf16))
    energy_ref[...] = sums[0:1] + sums[8:9]
    dmixed = reads * (sig + act * (1.0 - sig))
    dleft = jnp.concatenate(halves(dmixed), axis=1).astype(bf16)
    dinvs = nt(dleft, jnp.concatenate(back_upper + back_lower, axis=0).astype(bf16))
    for l in range(3):
        upto = (3 + l) * channels
        dinv = (dinvs[:, l * channels : (l + 1) * channels] + dinvs[:, upto : upto + channels]) * (2.0 * factor)
        for m in range(count):
            if degree[m] == l:
                hi, lo = halves(dinv * mom_scr[m])
                g_scr[:, m * groups : (m + 1) * groups, :] = hi.reshape(tiles, groups, channels)
                g_scr[:, (count + m) * groups : (count + m + 1) * groups, :] = lo.reshape(tiles, groups, channels)

    acc_scr[...] = jnp.zeros(acc_scr.shape, f32)
    padded = acc_scr.shape[0] // 6
    chunk_iota = lax.broadcasted_iota(jnp.int32, (padded, tile), 0)
    lane_rows = lax.broadcasted_iota(jnp.int16, (LANES, tile), 0)
    n = count * groups

    def pull_stage(t):
        g = g_scr[t]
        gl = jnp.concatenate(
            [g.astype(bf16), jnp.concatenate([g[0:n], jnp.zeros((n, channels), f32)], axis=0).astype(bf16)], axis=1
        )
        a = jnp.dot(gl, w_scr[t], preferred_element_type=f32)
        b = jnp.dot(gl, dw_scr[t], preferred_element_type=f32)
        return a, b

    def force_stage(t, a, b):
        x, y, z = spread(0, t), spread(1, t), spread(2, t)
        values = harmonics(x, y, z)
        A = [a[m * groups : (m + 1) * groups] + a[n + m * groups : n + (m + 1) * groups] for m in range(count)]
        rad = None
        for m in range(count):
            B = b[m * groups : (m + 1) * groups] + b[n + m * groups : n + (m + 1) * groups]
            rad = B if m == 0 else rad + values[m] * B
        rad = 2.0 * rad
        dx = root_three * A[1] + root_fifteen * (y * A[4] + z * A[7] + x * A[8]) - root_five * (x * A[6]) + x * rad
        dy = root_three * A[2] + root_fifteen * (x * A[4] + z * A[5] - y * A[8]) - root_five * (y * A[6]) + y * rad
        dz = root_three * A[3] + root_fifteen * (y * A[5] + x * A[7]) + (2.0 * root_five) * (z * A[6]) + z * rad
        comps = [jnp.where(mine_mask, v, 0.0) for v in (dx, dy, dz)]
        base = pl.multiple_of(t * groups, groups)
        lane = lax.broadcasted_iota(jnp.int32, (groups, LANES), 1)
        cen = jnp.zeros((groups, LANES), f32)
        for i, v in enumerate(comps):
            cen = jnp.where(lane == i, jnp.sum(v, axis=1, keepdims=True), cen)
        cen_scr[pl.ds(base, groups), :] = cen
        chunk = jnp.right_shift(idx_ref[pl.ds(t, 1), :], LANES.bit_length() - 1)
        hit = jnp.broadcast_to(chunk, (padded, tile)) == chunk_iota
        his, los = [], []
        for v in comps:
            hi, lo = halves(jnp.sum(v, axis=0, keepdims=True))
            his.append(jnp.where(hit, jnp.broadcast_to(hi, (padded, tile)), 0.0))
            los.append(jnp.where(hit, jnp.broadcast_to(lo, (padded, tile)), 0.0))
        left = jnp.concatenate(his + los, axis=0).astype(bf16)
        low = spread_idx(t, 16).astype(jnp.int16) & jnp.int16(LANES - 1)
        low = jnp.concatenate([low] * (LANES // 16), axis=0)
        right = jnp.where(low == lane_rows, jnp.ones((), bf16), jnp.zeros((), bf16))
        return left, right

    def backward(step, carry):
        numbers = [step * BEHIND + u for u in range(BEHIND)]
        pulls, total = {}, None
        for u in range(BEHIND + BACK_SKEW):
            if u < BEHIND:
                pulls[u] = pull_stage(numbers[u])
            v = u - BACK_SKEW
            if 0 <= v < BEHIND:
                left, right = force_stage(numbers[v], *pulls.pop(v))
                part = nt(left, right)
                total = part if total is None else total + part
        acc_scr[...] += total
        return carry

    lax.fori_loop(0, tiles // BEHIND, backward, 0)

    half = 3 * padded
    cen = jnp.concatenate(
        [jnp.transpose(cen_scr[c * LANES : (c + 1) * LANES, :])[0:8] for c in range(own_chunks)], axis=1
    )
    for axis in range(3):
        lo = axis * padded
        sums = acc_scr[lo : lo + padded] + acc_scr[half + lo : half + lo + padded]
        for c in range(own_chunks):
            own_ref[axis : axis + 1, c * LANES : (c + 1) * LANES] = (
                sums[c : c + 1] - cen[axis : axis + 1, c * LANES : (c + 1) * LANES]
            )
        left, right, lower, upper = (
            [sums[own_chunks + k * ghost + j : own_chunks + k * ghost + j + 1] for j in range(ghost)] for k in range(4)
        )
        for back, odd, one, other in (
            (first_back, row_odd, upper, lower),
            (second_back, row_odd, lower, upper),
            (third_back, col_odd, left, right),
            (fourth_back, col_odd, right, left),
        ):
            for j in range(ghost):
                back[j, axis : axis + 1, :] = jnp.where(odd, one[j], other[j])


def core(split, place, listed, own_pos, own_feat, win, wout, mixing, readout, sides, rows):
    atoms = own_pos.shape[2]
    channels = own_feat.shape[1]
    entries = listed.shape[1]
    tiles, tile = atoms // GROUPS, GROUPS * entries
    ghost = sides[0].shape[0]
    number, hidden = win.shape
    extent = atoms + len(sides) * ghost * LANES
    padded = -(-extent // (LANES * 16)) * 16
    vm = pl.BlockSpec(memory_space=pltpu.VMEM)
    sm = pl.BlockSpec(memory_space=pltpu.SMEM)
    back = jax.ShapeDtypeStruct((ghost, 3, LANES), f32)
    return pl.pallas_call(
        functools.partial(core_kernel, GROUPS, rows),
        out_shape=(
            jax.ShapeDtypeStruct((1, atoms), f32),
            jax.ShapeDtypeStruct((3, atoms), f32),
        ) + (back,) * len(sides),
        in_specs=[sm, sm, sm] + [vm] * (7 + len(sides)),
        out_specs=(vm,) * (2 + len(sides)),
        scratch_shapes=[
            pltpu.VMEM((atoms, entries), jnp.int32),
            pltpu.VMEM((tiles, tile), jnp.int32),
            pltpu.VMEM((3, tiles, tile), f32),
            pltpu.VMEM((2 * number, 2 * hidden), f32),
            pltpu.VMEM((channels, SHUFFLED * LANES), f32),
            pltpu.VMEM((2 * channels, extent - SHUFFLED * LANES), bf16),
            pltpu.VMEM((tiles, 2 * channels, tile), bf16),
            pltpu.VMEM((tiles, 2 * channels, tile), bf16),
            pltpu.VMEM((9, atoms, channels), f32),
            pltpu.VMEM((tiles, 18 * GROUPS, channels), f32),
            pltpu.VMEM((6 * padded, LANES), f32),
            pltpu.VMEM((atoms, LANES), f32),
        ],
        name="core",
    )(split, *place, listed, own_pos, own_feat, win, wout, mixing, readout, *sides)


def source_slot(slot, ghost, row, rows, split):
    raised = lax.rem(slot + split, ghost)
    lowered = lax.rem(slot - split + ghost, ghost)
    return jnp.where(row == 0, raised, jnp.where(row == rows - 1, lowered, slot))


def shared_blocks(faces_ref, rows, split, row, col):
    ghost = faces_ref.shape[0]
    row_odd = lax.rem(row, 2)
    col_odd = lax.rem(col, 2)
    return [
        [faces_ref[source_slot(j, ghost, row, rows, split), 3 - row_odd] for j in range(ghost)],
        [faces_ref[j, 2 + row_odd] for j in range(ghost)],
        [faces_ref[j, col_odd] for j in range(ghost)],
        [faces_ref[j, 1 - col_odd] for j in range(ghost)],
    ]


def pack_kernel(rows, split_ref, row_ref, col_ref, faces_ref, pos_ref, feat_ref, *out_refs):
    channels = feat_ref.shape[1]
    listed = shared_blocks(faces_ref, rows, split_ref[0], row_ref[0], col_ref[0])
    for out, blocks in zip(out_refs, listed):
        for j, block in enumerate(blocks):
            lanes = pl.ds(pl.multiple_of(block * LANES, LANES), LANES)
            out[j, 0:channels, :] = feat_ref[0, :, lanes]
            for axis in range(3):
                out[j, channels + axis : channels + axis + 1, :] = pos_ref[axis, :, lanes]
            out[j, channels + 3 :, :] = jnp.zeros((out.shape[1] - channels - 3, LANES), f32)


def pack(split, place, faces, pos, feat, rows):
    ghost, sides = faces.shape
    vm = pl.BlockSpec(memory_space=pltpu.VMEM)
    sm = pl.BlockSpec(memory_space=pltpu.SMEM)
    side = jax.ShapeDtypeStruct((ghost, feat.shape[1] + 8, LANES), f32)
    return pl.pallas_call(
        functools.partial(pack_kernel, rows),
        out_shape=(side,) * sides,
        in_specs=[sm, sm, sm, sm, vm, vm],
        out_specs=(vm,) * sides,
        name="pack",
    )(split, *place, faces, pos, feat)


def finish_kernel(rows, split_ref, row_ref, col_ref, faces_ref, own_ref, *refs):
    forces_ref = refs[-1]
    listed = shared_blocks(faces_ref, rows, split_ref[0], row_ref[0], col_ref[0])
    for number in range(own_ref.shape[1] // LANES):
        lanes = slice(number * LANES, (number + 1) * LANES)
        total = own_ref[:, lanes]
        for back, blocks in zip(refs[:-1], listed):
            for j, block in enumerate(blocks):
                total = total + jnp.where(block == number, back[j], 0.0)
        for axis in range(3):
            forces_ref[axis, :, lanes] = -total[axis : axis + 1]


def finish(split, place, faces, own, backs, rows):
    vm = pl.BlockSpec(memory_space=pltpu.VMEM)
    sm = pl.BlockSpec(memory_space=pltpu.SMEM)
    return pl.pallas_call(
        functools.partial(finish_kernel, rows),
        out_shape=jax.ShapeDtypeStruct((3, 1, own.shape[1]), f32),
        in_specs=[sm, sm, sm, sm] + [vm] * (1 + len(backs)),
        out_specs=vm,
        name="finish",
    )(split, *place, faces, own, *backs)


def row_swaps(rows, cols, odd, lower_shift=0, upper_shift=0):
    pairs = []
    for c in range(cols):
        for g in range(rows):
            if g % 2 == odd:
                target = (g + 1, c) if g < rows - 1 else (0, (c + lower_shift) % cols)
            else:
                target = (g - 1, c) if g > 0 else (rows - 1, (c - upper_shift) % cols)
            pairs.append((c * rows + g, target[1] * rows + target[0]))
    return pairs


def column_swaps(rows, cols, odd):
    pairs = []
    for c in range(cols):
        target = (c + 1 if c % 2 == odd else c - 1) % cols
        pairs += [(c * rows + g, target * rows + g) for g in range(rows)]
    return pairs


def exchange(sides, branch, rows, cols, back):
    ghost = sides[0].shape[0]

    def send(value, perm):
        pairs = [(b, a) for a, b in perm] if back else perm
        return lax.ppermute(value, ("flow", "grad"), pairs)

    def case(number):
        shift, split = divmod(number, ghost)

        def crossing(value):
            if split == 0:
                return send(value, row_swaps(rows, cols, 1, shift, shift))
            parts = []
            for j in range(ghost):
                lower_shift = shift + (1 if j < split else 0)
                upper_shift = shift + (1 if j >= ghost - split else 0)
                parts.append(send(value[j : j + 1], row_swaps(rows, cols, 1, lower_shift, upper_shift)))
            return jnp.concatenate(parts, axis=0)

        def route(values):
            first, second, third, fourth = values
            first = crossing(first)
            fourth = send(fourth, column_swaps(rows, cols, 1))
            second = send(second, row_swaps(rows, cols, 0))
            third = send(third, column_swaps(rows, cols, 0))
            return (first, second, third, fourth)

        return route

    return lax.switch(branch, [case(number) for number in range(cols * ghost)], tuple(sides))


def body(
    positions,
    features,
    neighbours,
    face_blocks,
    shear_cells,
    split_block,
    radial_in,
    radial_out,
    mixing,
    readout,
):
    faces = jnp.transpose(face_blocks[0])
    ghost = faces.shape[0]
    rows = lax.axis_size("grad")
    cols = lax.axis_size("flow")
    place = tuple(lax.axis_index(axis).astype(jnp.int32).reshape(1) for axis in ("grad", "flow"))
    branch = shear_cells[0] * ghost + split_block[0]
    branch = jnp.where(branch == cols * ghost, 0, branch)

    sides = pack(split_block, place, faces, positions, features, rows)
    sides = exchange(sides, branch, rows, cols, False)
    energy, own, *backs = core(
        split_block, place, neighbours, positions, features, radial_in, radial_out, mixing, readout.reshape(1, -1), sides, rows
    )
    backs = exchange(backs, branch, rows, cols, True)
    forces = finish(split_block, place, faces, own, backs, rows)
    return (energy, forces)


def solution(mesh):
    in_specs = (
        P(None, "grad", "flow"),
        P("grad", None, "flow"),
        P("grad", None, "flow"),
        P("grad", None, "flow"),
        P(),
        P(),
        P(),
        P(),
        P(),
        P(),
    )
    out_specs = (P("grad", "flow"), P(None, "grad", "flow"))
    return jax.shard_map(body, mesh=mesh, in_specs=in_specs, out_specs=out_specs, check_vma=False)
```

```python
import functools

import jax
import jax.numpy as jnp
from jax import lax
from jax.experimental import pallas as pl
from jax.experimental.pallas import tpu as pltpu
from jax.sharding import PartitionSpec as P

LANES = 128
GROUPS = 8
AHEAD = 16
BEHIND = 16
SHUFFLED = 4
SKEW = (2, 3, 4)
BACK_SKEW = 3
highest = lax.Precision.HIGHEST
root_three = 3.0**0.5
root_five = 5.0**0.5
root_fifteen = 15.0**0.5
f32 = jnp.float32
bf16 = jnp.bfloat16


def halves(value):
    upper = value.astype(bf16).astype(f32)
    return upper, value - upper


def nt(left, right, precision=None):
    return lax.dot_general(left, right, (((1,), (1,)), ((), ())), precision=precision, preferred_element_type=f32)


def core_kernel(groups, rows, split_ref, row_ref, col_ref, listed_ref, own_pos, own_feat, win_ref, wout_ref, mix_ref, read_ref,
                first_ref, second_ref, third_ref, fourth_ref,
                energy_ref, own_ref, first_back, second_back, third_back, fourth_back,
                turn_scr, idx_ref, xyz_scr, d_scr, x_scr, f_scr, w_scr, dw_scr, mom_scr, g_scr, acc_scr, cen_scr):
    split = split_ref[0]
    row = row_ref[0]
    row_odd = lax.rem(row, 2) == 1
    col_odd = lax.rem(col_ref[0], 2) == 1
    atoms = own_pos.shape[2]
    channels = own_feat.shape[1]
    number, hidden = win_ref.shape
    ghost = first_ref.shape[0]
    tiles, tile = idx_ref.shape
    neighbours = listed_ref.shape[1]
    own_chunks = atoms // LANES
    sides = (
        (col_odd, third_ref, fourth_ref),
        (col_odd, fourth_ref, third_ref),
        (row_odd, second_ref, first_ref),
        (row_odd, first_ref, second_ref),
    )
    chunks = own_chunks + len(sides) * ghost
    places = [landing_place(j, ghost, row, split) for j in range(ghost)]
    factor = neighbours ** (-0.5)

    def side(k, j, part):
        odd, one, other = sides[k]
        lines = [ref[places[j] if ref is first_ref else j, part, :] for ref in (one, other)]
        return jnp.where(odd, *lines)

    def pos_chunk(c, axis):
        if c < own_chunks:
            return own_pos[axis, :, c * LANES : (c + 1) * LANES]
        k, j = divmod(c - own_chunks, ghost)
        line = side(k, j, slice(channels + axis, channels + axis + 1))
        fraction = split.astype(f32) / ghost
        if axis == 0:
            if k < 2:
                line = line + (2.0 * k - 1.0)
            elif k == 2:
                line = line + jnp.where(row == 0, jnp.where(j < split, fraction - 1.0, fraction), 0.0)
            else:
                line = line + jnp.where(
                    row == rows - 1, jnp.where(j < ghost - split, -fraction, 1.0 - fraction), 0.0
                )
        elif axis == 1 and k >= 2:
            line = line + (2.0 * k - 5.0)
        return line

    for c in range(own_chunks):
        rows_of = slice(c * LANES, (c + 1) * LANES)
        turn_scr[rows_of, :] = jnp.transpose(listed_ref[0, :, rows_of])
    for a in range(groups):
        idx_ref[:, a * neighbours : (a + 1) * neighbours] = turn_scr[pl.ds(a, tiles, stride=groups), :]

    def place_features(c):
        lanes = slice(c * LANES, (c + 1) * LANES)
        if c < own_chunks:
            feat = own_feat[0, :, lanes]
        else:
            k, j = divmod(c - own_chunks, ghost)
            feat = side(k, j, slice(0, channels))
        if c < SHUFFLED:
            x_scr[:, lanes] = feat
        else:
            hi, lo = halves(feat)
            lanes = slice((c - SHUFFLED) * LANES, (c - SHUFFLED + 1) * LANES)
            f_scr[0:channels, lanes] = hi.astype(bf16)
            f_scr[channels : 2 * channels, lanes] = lo.astype(bf16)

    waiting = list(range(chunks))

    blocks = tile // LANES
    for lb in range(blocks):
        lanes = slice(lb * LANES, (lb + 1) * LANES)
        idx = idx_ref[:, lanes]
        low = jnp.bitwise_and(idx, LANES - 1)
        chunk = jnp.right_shift(idx, LANES.bit_length() - 1)
        lines = lax.broadcasted_iota(jnp.int32, idx.shape, 0)
        cols = lax.broadcasted_iota(jnp.int32, idx.shape, 1) + lb * LANES
        centre = lines * groups + cols // neighbours
        clow = jnp.bitwise_and(centre, LANES - 1)
        cchunk = jnp.right_shift(centre, LANES.bit_length() - 1)
        for axis in range(3):
            other = None
            mine = None
            for c in range(chunks):
                src = jnp.broadcast_to(pos_chunk(c, axis), idx.shape)
                got = jnp.take_along_axis(src, low, axis=1)
                other = got if other is None else jnp.where(chunk == c, got, other)
                if c < own_chunks:
                    got = jnp.take_along_axis(src, clow, axis=1)
                    mine = got if mine is None else jnp.where(cchunk == c, got, mine)
            xyz_scr[axis, :, lanes] = other - mine
            for c in waiting[:2]:
                place_features(c)
            del waiting[:2]

    for c in waiting:
        place_features(c)

    d_scr[...] = jnp.zeros(d_scr.shape, f32)
    d_scr[0:number, 0:hidden] = win_ref[...]
    d_scr[number : 2 * number, hidden : 2 * hidden] = win_ref[...]
    dhi, dlo = halves(d_scr[...])
    first = jnp.transpose(jnp.concatenate([dhi, dhi, dlo, dlo], axis=0)).astype(bf16)
    ohi, olo = halves(wout_ref[...])
    second = jnp.transpose(jnp.concatenate([ohi, ohi, olo, olo], axis=0)).astype(bf16)

    row_iota = lax.broadcasted_iota(jnp.int32, (groups, tile), 0)
    lane_iota = lax.broadcasted_iota(jnp.int32, (groups, tile), 1)
    mine_mask = row_iota == lane_iota // neighbours
    centres = lax.broadcasted_iota(jnp.int32, (number, tile), 0).astype(f32) * (6.0 / (number - 1))
    entry_iota = lax.broadcasted_iota(jnp.int16, ((chunks - SHUFFLED) * LANES, tile), 0)

    def spread(axis, t, lines=groups):
        return jnp.broadcast_to(xyz_scr[axis, pl.ds(t, 1), :], (lines, tile))

    def harmonics(x, y, z):
        square = x * x + y * y + z * z
        return [
            jnp.ones_like(x),
            root_three * x,
            root_three * y,
            root_three * z,
            root_fifteen * x * y,
            root_fifteen * y * z,
            0.5 * root_five * (3.0 * z * z - square),
            root_fifteen * x * z,
            0.5 * root_fifteen * (x * x - y * y),
        ]

    def stacked(value):
        hi, lo = halves(value)
        return jnp.concatenate([hi, lo, hi, lo], axis=0).astype(bf16)

    def spread_idx(t, lines):
        return jnp.broadcast_to(idx_ref[pl.ds(t, 1), :], (lines, tile))

    def basis_stage(t):
        x, y, z = (spread(axis, t, number) for axis in range(3))
        away = x * x + y * y + z * z - centres
        scaled = away / 0.75
        gauss = jnp.exp(-0.5 * (scaled * scaled))
        slope = gauss * (away * (-1.0 / 0.5625))
        basis = stacked(jnp.concatenate([gauss, slope], axis=0))
        return jnp.dot(first, basis, preferred_element_type=f32)

    def gather_stage(t):
        listed = spread_idx(t, 16).astype(jnp.int16)
        listed = jnp.concatenate([listed - SHUFFLED * LANES] * ((chunks - SHUFFLED) * LANES // 16), axis=0)
        picks = jnp.where(listed == entry_iota, jnp.ones((), bf16), jnp.zeros((), bf16))
        return jnp.dot(f_scr[...], picks, preferred_element_type=f32)

    def hidden_stage(both):
        h, dh = both[0:hidden], both[hidden : 2 * hidden]
        sig = 0.5 * jnp.tanh(0.5 * h) + 0.5
        act = h * sig
        dact = dh * (sig + act * (1.0 - sig))
        radial = jnp.dot(second, stacked(act), preferred_element_type=f32)
        dradial = jnp.dot(second, stacked(dact), preferred_element_type=f32)
        return radial, dradial

    def feature_stage(t, part):
        feat = part[0:channels] + part[channels:]
        listed = spread_idx(t, channels)
        low = jnp.bitwise_and(listed, LANES - 1)
        chunk = jnp.right_shift(listed, LANES.bit_length() - 1)
        lines = []
        for lb in range(tile // LANES):
            lanes = slice(lb * LANES, (lb + 1) * LANES)
            line = feat[:, lanes]
            for c in range(SHUFFLED):
                moved = jnp.take_along_axis(x_scr[:, c * LANES : (c + 1) * LANES], low[:, lanes], axis=1)
                line = jnp.where(chunk[:, lanes] == c, moved, line)
            lines.append(line)
        return jnp.concatenate(lines, axis=1)

    def weight_stage(t, radial, dradial, feat):
        whi, wlo = halves(radial * feat)
        weight = jnp.concatenate([whi, wlo], axis=0).astype(bf16)
        w_scr[t] = weight
        whi, wlo = halves(dradial * feat)
        dw_scr[t] = jnp.concatenate([whi, wlo], axis=0).astype(bf16)
        return weight

    def moment_stage(t, weight):
        his, los = [], []
        for value in harmonics(*(spread(axis, t) for axis in range(3))):
            hi, lo = halves(jnp.where(mine_mask, value, 0.0))
            his.append(hi)
            los.append(lo)
        out = nt(jnp.concatenate(his + los, axis=0).astype(bf16), weight)
        n = 9 * groups
        total = (out[0:n, 0:channels] + out[0:n, channels:]) + out[n : 2 * n, 0:channels]
        base = pl.multiple_of(t * groups, groups)
        for m in range(9):
            mom_scr[m, pl.ds(base, groups), :] = total[m * groups : (m + 1) * groups] * factor

    def forward(step, carry):
        numbers = [step * AHEAD + u for u in range(AHEAD)]
        boths, parts, nets, weights = {}, {}, {}, {}
        for u in range(AHEAD + SKEW[-1]):
            if u < AHEAD:
                boths[u] = basis_stage(numbers[u])
                parts[u] = gather_stage(numbers[u])
            v = u - SKEW[0]
            if 0 <= v < AHEAD:
                nets[v] = hidden_stage(boths.pop(v))
            v = u - SKEW[1]
            if 0 <= v < AHEAD:
                feat = feature_stage(numbers[v], parts.pop(v))
                weights[v] = weight_stage(numbers[v], *nets.pop(v), feat)
            v = u - SKEW[2]
            if 0 <= v < AHEAD:
                moment_stage(numbers[v], weights.pop(v))
        return carry

    lax.fori_loop(0, tiles // AHEAD, forward, 0)

    degree = [0, 1, 1, 1, 2, 2, 2, 2, 2]
    count = len(degree)
    invariants = []
    for l in range(3):
        total = None
        for m in range(count):
            if degree[m] == l:
                sq = mom_scr[m] * mom_scr[m]
                total = sq if total is None else total + sq
        invariants.append(total)
    upper, lower, back_upper, back_lower = [], [], [], []
    blank = jnp.zeros((channels, channels), f32)
    for l in range(3):
        hi, lo = halves(mix_ref[l])
        upper.append(jnp.concatenate([hi, lo], axis=1))
        back_upper.append(jnp.concatenate([hi, hi], axis=1))
        back_lower.append(jnp.concatenate([lo, blank], axis=1))
    pieces = [halves(value) for value in invariants]
    left = jnp.concatenate([hi for hi, _ in pieces] + [lo for _, lo in pieces], axis=1).astype(bf16)
    mixed = jnp.dot(left, jnp.concatenate(upper + upper, axis=0).astype(bf16), preferred_element_type=f32)
    mixed = mixed[:, 0:channels] + mixed[:, channels:]
    sig = 0.5 * jnp.tanh(0.5 * mixed) + 0.5
    act = mixed * sig
    reads = read_ref[...]
    rhi, rlo = (jnp.broadcast_to(value, (8, channels)) for value in halves(reads))
    rows_of = jnp.concatenate([jnp.concatenate([rhi, rhi], axis=1), jnp.concatenate([rlo, rlo], axis=1)], axis=0)
    sums = nt(rows_of.astype(bf16), jnp.concatenate(halves(act), axis=1).astype(bf16))
    energy_ref[...] = sums[0:1] + sums[8:9]
    dmixed = reads * (sig + act * (1.0 - sig))
    dleft = jnp.concatenate(halves(dmixed), axis=1).astype(bf16)
    dinvs = nt(dleft, jnp.concatenate(back_upper + back_lower, axis=0).astype(bf16))
    for l in range(3):
        upto = (3 + l) * channels
        dinv = (dinvs[:, l * channels : (l + 1) * channels] + dinvs[:, upto : upto + channels]) * (2.0 * factor)
        for m in range(count):
            if degree[m] == l:
                hi, lo = halves(dinv * mom_scr[m])
                g_scr[:, m * groups : (m + 1) * groups, :] = hi.reshape(tiles, groups, channels)
                g_scr[:, (count + m) * groups : (count + m + 1) * groups, :] = lo.reshape(tiles, groups, channels)

    acc_scr[...] = jnp.zeros(acc_scr.shape, f32)
    padded = acc_scr.shape[0] // 6
    chunk_iota = lax.broadcasted_iota(jnp.int32, (padded, tile), 0)
    lane_rows = lax.broadcasted_iota(jnp.int16, (LANES, tile), 0)
    n = count * groups

    def pull_stage(t):
        g = g_scr[t]
        gl = jnp.concatenate(
            [g.astype(bf16), jnp.concatenate([g[0:n], jnp.zeros((n, channels), f32)], axis=0).astype(bf16)], axis=1
        )
        a = jnp.dot(gl, w_scr[t], preferred_element_type=f32)
        b = jnp.dot(gl, dw_scr[t], preferred_element_type=f32)
        return a, b

    def force_stage(t, a, b):
        x, y, z = spread(0, t), spread(1, t), spread(2, t)
        values = harmonics(x, y, z)
        A = [a[m * groups : (m + 1) * groups] + a[n + m * groups : n + (m + 1) * groups] for m in range(count)]
        rad = None
        for m in range(count):
            B = b[m * groups : (m + 1) * groups] + b[n + m * groups : n + (m + 1) * groups]
            rad = B if m == 0 else rad + values[m] * B
        rad = 2.0 * rad
        dx = root_three * A[1] + root_fifteen * (y * A[4] + z * A[7] + x * A[8]) - root_five * (x * A[6]) + x * rad
        dy = root_three * A[2] + root_fifteen * (x * A[4] + z * A[5] - y * A[8]) - root_five * (y * A[6]) + y * rad
        dz = root_three * A[3] + root_fifteen * (y * A[5] + x * A[7]) + (2.0 * root_five) * (z * A[6]) + z * rad
        comps = [jnp.where(mine_mask, v, 0.0) for v in (dx, dy, dz)]
        base = pl.multiple_of(t * groups, groups)
        lane = lax.broadcasted_iota(jnp.int32, (groups, LANES), 1)
        cen = jnp.zeros((groups, LANES), f32)
        for i, v in enumerate(comps):
            cen = jnp.where(lane == i, jnp.sum(v, axis=1, keepdims=True), cen)
        cen_scr[pl.ds(base, groups), :] = cen
        chunk = jnp.right_shift(idx_ref[pl.ds(t, 1), :], LANES.bit_length() - 1)
        hit = jnp.broadcast_to(chunk, (padded, tile)) == chunk_iota
        his, los = [], []
        for v in comps:
            hi, lo = halves(jnp.sum(v, axis=0, keepdims=True))
            his.append(jnp.where(hit, jnp.broadcast_to(hi, (padded, tile)), 0.0))
            los.append(jnp.where(hit, jnp.broadcast_to(lo, (padded, tile)), 0.0))
        left = jnp.concatenate(his + los, axis=0).astype(bf16)
        low = spread_idx(t, 16).astype(jnp.int16) & jnp.int16(LANES - 1)
        low = jnp.concatenate([low] * (LANES // 16), axis=0)
        right = jnp.where(low == lane_rows, jnp.ones((), bf16), jnp.zeros((), bf16))
        return left, right

    def backward(step, carry):
        numbers = [step * BEHIND + u for u in range(BEHIND)]
        pulls, total = {}, None
        for u in range(BEHIND + BACK_SKEW):
            if u < BEHIND:
                pulls[u] = pull_stage(numbers[u])
            v = u - BACK_SKEW
            if 0 <= v < BEHIND:
                left, right = force_stage(numbers[v], *pulls.pop(v))
                part = nt(left, right)
                total = part if total is None else total + part
        acc_scr[...] += total
        return carry

    lax.fori_loop(0, tiles // BEHIND, backward, 0)

    half = 3 * padded
    cen = jnp.concatenate(
        [jnp.transpose(cen_scr[c * LANES : (c + 1) * LANES, :])[0:8] for c in range(own_chunks)], axis=1
    )
    for axis in range(3):
        lo = axis * padded
        sums = acc_scr[lo : lo + padded] + acc_scr[half + lo : half + lo + padded]
        for c in range(own_chunks):
            own_ref[axis : axis + 1, c * LANES : (c + 1) * LANES] = (
                sums[c : c + 1] - cen[axis : axis + 1, c * LANES : (c + 1) * LANES]
            )
        left, right, lower, upper = (
            [sums[own_chunks + k * ghost + j : own_chunks + k * ghost + j + 1] for j in range(ghost)] for k in range(4)
        )
        for back, odd, one, other in (
            (first_back, row_odd, upper, lower),
            (second_back, row_odd, lower, upper),
            (third_back, col_odd, left, right),
            (fourth_back, col_odd, right, left),
        ):
            for j in range(ghost):
                place = places[j] if back is first_back else j
                back[place, axis : axis + 1, :] = jnp.where(odd, one[j], other[j])


def core(split, place, listed, own_pos, own_feat, win, wout, mixing, readout, sides, rows):
    atoms = own_pos.shape[2]
    channels = own_feat.shape[1]
    entries = listed.shape[1]
    tiles, tile = atoms // GROUPS, GROUPS * entries
    ghost = sides[0].shape[0]
    number, hidden = win.shape
    extent = atoms + len(sides) * ghost * LANES
    padded = -(-extent // (LANES * 16)) * 16
    vm = pl.BlockSpec(memory_space=pltpu.VMEM)
    sm = pl.BlockSpec(memory_space=pltpu.SMEM)
    back = jax.ShapeDtypeStruct((ghost, 3, LANES), f32)
    return pl.pallas_call(
        functools.partial(core_kernel, GROUPS, rows),
        out_shape=(
            jax.ShapeDtypeStruct((1, atoms), f32),
            jax.ShapeDtypeStruct((3, atoms), f32),
        ) + (back,) * len(sides),
        in_specs=[sm, sm, sm] + [vm] * (7 + len(sides)),
        out_specs=(vm,) * (2 + len(sides)),
        scratch_shapes=[
            pltpu.VMEM((atoms, entries), jnp.int32),
            pltpu.VMEM((tiles, tile), jnp.int32),
            pltpu.VMEM((3, tiles, tile), f32),
            pltpu.VMEM((2 * number, 2 * hidden), f32),
            pltpu.VMEM((channels, SHUFFLED * LANES), f32),
            pltpu.VMEM((2 * channels, extent - SHUFFLED * LANES), bf16),
            pltpu.VMEM((tiles, 2 * channels, tile), bf16),
            pltpu.VMEM((tiles, 2 * channels, tile), bf16),
            pltpu.VMEM((9, atoms, channels), f32),
            pltpu.VMEM((tiles, 18 * GROUPS, channels), f32),
            pltpu.VMEM((6 * padded, LANES), f32),
            pltpu.VMEM((atoms, LANES), f32),
        ],
        name="core",
    )(split, *place, listed, own_pos, own_feat, win, wout, mixing, readout, *sides)


def source_slot(place, ghost, row, split):
    return jnp.where(row == 0, lax.rem(place + split, ghost), place)


def landing_place(slot, ghost, row, split):
    return jnp.where(row == 0, lax.rem(slot - split + ghost, ghost), slot)


def shared_blocks(faces_ref, split, row, col):
    ghost = faces_ref.shape[0]
    row_odd = lax.rem(row, 2)
    col_odd = lax.rem(col, 2)
    return [
        [faces_ref[source_slot(j, ghost, row, split), 3 - row_odd] for j in range(ghost)],
        [faces_ref[j, 2 + row_odd] for j in range(ghost)],
        [faces_ref[j, col_odd] for j in range(ghost)],
        [faces_ref[j, 1 - col_odd] for j in range(ghost)],
    ]


def pack_kernel(split_ref, row_ref, col_ref, faces_ref, pos_ref, feat_ref, *out_refs):
    channels = feat_ref.shape[1]
    listed = shared_blocks(faces_ref, split_ref[0], row_ref[0], col_ref[0])
    for out, blocks in zip(out_refs, listed):
        for j, block in enumerate(blocks):
            lanes = pl.ds(pl.multiple_of(block * LANES, LANES), LANES)
            out[j, 0:channels, :] = feat_ref[0, :, lanes]
            for axis in range(3):
                out[j, channels + axis : channels + axis + 1, :] = pos_ref[axis, :, lanes]
            out[j, channels + 3 :, :] = jnp.zeros((out.shape[1] - channels - 3, LANES), f32)


def pack(split, place, faces, pos, feat):
    ghost, sides = faces.shape
    vm = pl.BlockSpec(memory_space=pltpu.VMEM)
    sm = pl.BlockSpec(memory_space=pltpu.SMEM)
    side = jax.ShapeDtypeStruct((ghost, feat.shape[1] + 8, LANES), f32)
    return pl.pallas_call(
        pack_kernel,
        out_shape=(side,) * sides,
        in_specs=[sm, sm, sm, sm, vm, vm],
        out_specs=(vm,) * sides,
        name="pack",
    )(split, *place, faces, pos, feat)


def finish_kernel(split_ref, row_ref, col_ref, faces_ref, own_ref, *refs):
    forces_ref = refs[-1]
    listed = shared_blocks(faces_ref, split_ref[0], row_ref[0], col_ref[0])
    for number in range(own_ref.shape[1] // LANES):
        lanes = slice(number * LANES, (number + 1) * LANES)
        total = own_ref[:, lanes]
        for back, blocks in zip(refs[:-1], listed):
            for j, block in enumerate(blocks):
                total = total + jnp.where(block == number, back[j], 0.0)
        for axis in range(3):
            forces_ref[axis, :, lanes] = -total[axis : axis + 1]


def finish(split, place, faces, own, backs):
    vm = pl.BlockSpec(memory_space=pltpu.VMEM)
    sm = pl.BlockSpec(memory_space=pltpu.SMEM)
    return pl.pallas_call(
        finish_kernel,
        out_shape=jax.ShapeDtypeStruct((3, 1, own.shape[1]), f32),
        in_specs=[sm, sm, sm, sm] + [vm] * (1 + len(backs)),
        out_specs=vm,
        name="finish",
    )(split, *place, faces, own, *backs)


def row_swaps(rows, cols, odd, shift=0):
    pairs = []
    for c in range(cols):
        for g in range(rows):
            if g % 2 == odd:
                target = (g + 1, c) if g < rows - 1 else (0, (c + shift) % cols)
            else:
                target = (g - 1, c) if g > 0 else (rows - 1, (c - shift) % cols)
            pairs.append((c * rows + g, target[1] * rows + target[0]))
    return pairs


def column_swaps(rows, cols, odd):
    pairs = []
    for c in range(cols):
        target = (c + 1 if c % 2 == odd else c - 1) % cols
        pairs += [(c * rows + g, target * rows + g) for g in range(rows)]
    return pairs


def exchange(sides, branch, rows, cols, back):
    ghost = sides[0].shape[0]

    def send(value, perm):
        pairs = [(b, a) for a, b in perm] if back else perm
        return lax.ppermute(value, ("flow", "grad"), pairs)

    def case(number):
        shift, split = divmod(number, ghost)

        def crossing(value):
            if split == 0:
                return send(value, row_swaps(rows, cols, 1, shift))
            parts = []
            for part, by in ((value[: ghost - split], shift), (value[ghost - split :], shift + 1)):
                parts.append(send(part, row_swaps(rows, cols, 1, by)))
            return jnp.concatenate(parts, axis=0)

        def route(values):
            first, second, third, fourth = values
            first = crossing(first)
            fourth = send(fourth, column_swaps(rows, cols, 1))
            second = send(second, row_swaps(rows, cols, 0))
            third = send(third, column_swaps(rows, cols, 0))
            return (first, second, third, fourth)

        return route

    return lax.switch(branch, [case(number) for number in range(cols * ghost)], tuple(sides))


def body(
    positions,
    features,
    neighbours,
    face_blocks,
    shear_cells,
    split_block,
    radial_in,
    radial_out,
    mixing,
    readout,
):
    faces = jnp.transpose(face_blocks[0])
    ghost = faces.shape[0]
    rows = lax.axis_size("grad")
    cols = lax.axis_size("flow")
    place = tuple(lax.axis_index(axis).astype(jnp.int32).reshape(1) for axis in ("grad", "flow"))
    branch = shear_cells[0] * ghost + split_block[0]
    branch = jnp.where(branch == cols * ghost, 0, branch)

    sides = pack(split_block, place, faces, positions, features)
    sides = exchange(sides, branch, rows, cols, False)
    energy, own, *backs = core(
        split_block, place, neighbours, positions, features, radial_in, radial_out, mixing, readout.reshape(1, -1), sides, rows
    )
    backs = exchange(backs, branch, rows, cols, True)
    forces = finish(split_block, place, faces, own, backs)
    return (energy, forces)


def solution(mesh):
    in_specs = (
        P(None, "grad", "flow"),
        P("grad", None, "flow"),
        P("grad", None, "flow"),
        P("grad", None, "flow"),
        P(),
        P(),
        P(),
        P(),
        P(),
        P(),
    )
    out_specs = (P("grad", "flow"), P(None, "grad", "flow"))
    return jax.shard_map(body, mesh=mesh, in_specs=in_specs, out_specs=out_specs, check_vma=False)
```

```python
import functools

import jax
import jax.numpy as jnp
from jax import lax
from jax.experimental import pallas as pl
from jax.experimental.pallas import tpu as pltpu
from jax.sharding import PartitionSpec as P

LANES = 128
GROUPS = 8
AHEAD = 16
BEHIND = 16
SHUFFLED = 4
SKEW = (2, 3, 4)
BACK_SKEW = 3
highest = lax.Precision.HIGHEST
root_three = 3.0**0.5
root_five = 5.0**0.5
root_fifteen = 15.0**0.5
f32 = jnp.float32
bf16 = jnp.bfloat16


def halves(value):
    upper = value.astype(bf16).astype(f32)
    return upper, value - upper


def nt(left, right, precision=None):
    return lax.dot_general(left, right, (((1,), (1,)), ((), ())), precision=precision, preferred_element_type=f32)


def core_kernel(groups, rows, split_ref, place_ref, listed_ref, own_pos, own_feat, win_ref, wout_ref, mix_ref, read_ref,
                first_ref, second_ref, third_ref, fourth_ref,
                energy_ref, own_ref, first_back, second_back, third_back, fourth_back,
                turn_scr, idx_ref, xyz_scr, d_scr, x_scr, f_scr, w_scr, dw_scr, mom_scr, g_scr, acc_scr, cen_scr):
    split = split_ref[0]
    row = lax.rem(place_ref[0], rows)
    row_odd = lax.rem(row, 2) == 1
    col_odd = lax.rem(lax.div(place_ref[0], rows), 2) == 1
    atoms = own_pos.shape[2]
    channels = own_feat.shape[1]
    number, hidden = win_ref.shape
    ghost = first_ref.shape[0]
    tiles, tile = idx_ref.shape
    neighbours = listed_ref.shape[1]
    own_chunks = atoms // LANES
    sides = (
        (col_odd, third_ref, fourth_ref),
        (col_odd, fourth_ref, third_ref),
        (row_odd, second_ref, first_ref),
        (row_odd, first_ref, second_ref),
    )
    chunks = own_chunks + len(sides) * ghost
    places = [landing_place(j, ghost, row, split) for j in range(ghost)]
    factor = neighbours ** (-0.5)

    def side(k, j, part):
        odd, one, other = sides[k]
        lines = [ref[places[j] if ref is first_ref else j, part, :] for ref in (one, other)]
        return jnp.where(odd, *lines)

    def pos_chunk(c, axis):
        if c < own_chunks:
            return own_pos[axis, :, c * LANES : (c + 1) * LANES]
        k, j = divmod(c - own_chunks, ghost)
        line = side(k, j, slice(channels + axis, channels + axis + 1))
        fraction = split.astype(f32) / ghost
        if axis == 0:
            if k < 2:
                line = line + (2.0 * k - 1.0)
            elif k == 2:
                line = line + jnp.where(row == 0, jnp.where(j < split, fraction - 1.0, fraction), 0.0)
            else:
                line = line + jnp.where(
                    row == rows - 1, jnp.where(j < ghost - split, -fraction, 1.0 - fraction), 0.0
                )
        elif axis == 1 and k >= 2:
            line = line + (2.0 * k - 5.0)
        return line

    for c in range(own_chunks):
        rows_of = slice(c * LANES, (c + 1) * LANES)
        turn_scr[rows_of, :] = jnp.transpose(listed_ref[0, :, rows_of])
    for a in range(groups):
        idx_ref[:, a * neighbours : (a + 1) * neighbours] = turn_scr[pl.ds(a, tiles, stride=groups), :]

    def place_features(c):
        lanes = slice(c * LANES, (c + 1) * LANES)
        if c < own_chunks:
            feat = own_feat[0, :, lanes]
        else:
            k, j = divmod(c - own_chunks, ghost)
            feat = side(k, j, slice(0, channels))
        if c < SHUFFLED:
            x_scr[:, lanes] = feat
        else:
            hi, lo = halves(feat)
            lanes = slice((c - SHUFFLED) * LANES, (c - SHUFFLED + 1) * LANES)
            f_scr[0:channels, lanes] = hi.astype(bf16)
            f_scr[channels : 2 * channels, lanes] = lo.astype(bf16)

    waiting = list(range(chunks))

    blocks = tile // LANES
    for lb in range(blocks):
        lanes = slice(lb * LANES, (lb + 1) * LANES)
        idx = idx_ref[:, lanes]
        low = jnp.bitwise_and(idx, LANES - 1)
        chunk = jnp.right_shift(idx, LANES.bit_length() - 1)
        lines = lax.broadcasted_iota(jnp.int32, idx.shape, 0)
        cols = lax.broadcasted_iota(jnp.int32, idx.shape, 1) + lb * LANES
        centre = lines * groups + cols // neighbours
        clow = jnp.bitwise_and(centre, LANES - 1)
        cchunk = jnp.right_shift(centre, LANES.bit_length() - 1)
        for axis in range(3):
            other = None
            mine = None
            for c in range(chunks):
                src = jnp.broadcast_to(pos_chunk(c, axis), idx.shape)
                got = jnp.take_along_axis(src, low, axis=1)
                other = got if other is None else jnp.where(chunk == c, got, other)
                if c < own_chunks:
                    got = jnp.take_along_axis(src, clow, axis=1)
                    mine = got if mine is None else jnp.where(cchunk == c, got, mine)
            xyz_scr[axis, :, lanes] = other - mine
            for c in waiting[:2]:
                place_features(c)
            del waiting[:2]

    for c in waiting:
        place_features(c)

    d_scr[...] = jnp.zeros(d_scr.shape, f32)
    d_scr[0:number, 0:hidden] = win_ref[...]
    d_scr[number : 2 * number, hidden : 2 * hidden] = win_ref[...]
    dhi, dlo = halves(d_scr[...])
    first = jnp.transpose(jnp.concatenate([dhi, dhi, dlo, dlo], axis=0)).astype(bf16)
    ohi, olo = halves(wout_ref[...])
    second = jnp.transpose(jnp.concatenate([ohi, ohi, olo, olo], axis=0)).astype(bf16)

    row_iota = lax.broadcasted_iota(jnp.int32, (groups, tile), 0)
    lane_iota = lax.broadcasted_iota(jnp.int32, (groups, tile), 1)
    mine_mask = row_iota == lane_iota // neighbours
    centres = lax.broadcasted_iota(jnp.int32, (number, tile), 0).astype(f32) * (6.0 / (number - 1))
    entry_iota = lax.broadcasted_iota(jnp.int16, ((chunks - SHUFFLED) * LANES, tile), 0)

    def spread(axis, t, lines=groups):
        return jnp.broadcast_to(xyz_scr[axis, pl.ds(t, 1), :], (lines, tile))

    def harmonics(x, y, z):
        square = x * x + y * y + z * z
        return [
            jnp.ones_like(x),
            root_three * x,
            root_three * y,
            root_three * z,
            root_fifteen * x * y,
            root_fifteen * y * z,
            0.5 * root_five * (3.0 * z * z - square),
            root_fifteen * x * z,
            0.5 * root_fifteen * (x * x - y * y),
        ]

    def stacked(value):
        hi, lo = halves(value)
        return jnp.concatenate([hi, lo, hi, lo], axis=0).astype(bf16)

    def spread_idx(t, lines):
        return jnp.broadcast_to(idx_ref[pl.ds(t, 1), :], (lines, tile))

    def basis_stage(t):
        x, y, z = (spread(axis, t, number) for axis in range(3))
        away = x * x + y * y + z * z - centres
        scaled = away / 0.75
        gauss = jnp.exp(-0.5 * (scaled * scaled))
        slope = gauss * (away * (-1.0 / 0.5625))
        basis = stacked(jnp.concatenate([gauss, slope], axis=0))
        return jnp.dot(first, basis, preferred_element_type=f32)

    def gather_stage(t):
        listed = spread_idx(t, 16).astype(jnp.int16)
        listed = jnp.concatenate([listed - SHUFFLED * LANES] * ((chunks - SHUFFLED) * LANES // 16), axis=0)
        picks = jnp.where(listed == entry_iota, jnp.ones((), bf16), jnp.zeros((), bf16))
        return jnp.dot(f_scr[...], picks, preferred_element_type=f32)

    def hidden_stage(both):
        h, dh = both[0:hidden], both[hidden : 2 * hidden]
        sig = 0.5 * jnp.tanh(0.5 * h) + 0.5
        act = h * sig
        dact = dh * (sig + act * (1.0 - sig))
        radial = jnp.dot(second, stacked(act), preferred_element_type=f32)
        dradial = jnp.dot(second, stacked(dact), preferred_element_type=f32)
        return radial, dradial

    def feature_stage(t, part):
        feat = part[0:channels] + part[channels:]
        listed = spread_idx(t, channels)
        low = jnp.bitwise_and(listed, LANES - 1)
        chunk = jnp.right_shift(listed, LANES.bit_length() - 1)
        lines = []
        for lb in range(tile // LANES):
            lanes = slice(lb * LANES, (lb + 1) * LANES)
            line = feat[:, lanes]
            for c in range(SHUFFLED):
                moved = jnp.take_along_axis(x_scr[:, c * LANES : (c + 1) * LANES], low[:, lanes], axis=1)
                line = jnp.where(chunk[:, lanes] == c, moved, line)
            lines.append(line)
        return jnp.concatenate(lines, axis=1)

    def weight_stage(t, radial, dradial, feat):
        whi, wlo = halves(radial * feat)
        weight = jnp.concatenate([whi, wlo], axis=0).astype(bf16)
        w_scr[t] = weight
        whi, wlo = halves(dradial * feat)
        dw_scr[t] = jnp.concatenate([whi, wlo], axis=0).astype(bf16)
        return weight

    def moment_stage(t, weight):
        his, los = [], []
        for value in harmonics(*(spread(axis, t) for axis in range(3))):
            hi, lo = halves(jnp.where(mine_mask, value, 0.0))
            his.append(hi)
            los.append(lo)
        out = nt(jnp.concatenate(his + los, axis=0).astype(bf16), weight)
        n = 9 * groups
        total = (out[0:n, 0:channels] + out[0:n, channels:]) + out[n : 2 * n, 0:channels]
        base = pl.multiple_of(t * groups, groups)
        for m in range(9):
            mom_scr[m, pl.ds(base, groups), :] = total[m * groups : (m + 1) * groups] * factor

    def forward(step, carry):
        numbers = [step * AHEAD + u for u in range(AHEAD)]
        boths, parts, nets, weights = {}, {}, {}, {}
        for u in range(AHEAD + SKEW[-1]):
            if u < AHEAD:
                boths[u] = basis_stage(numbers[u])
                parts[u] = gather_stage(numbers[u])
            v = u - SKEW[0]
            if 0 <= v < AHEAD:
                nets[v] = hidden_stage(boths.pop(v))
            v = u - SKEW[1]
            if 0 <= v < AHEAD:
                feat = feature_stage(numbers[v], parts.pop(v))
                weights[v] = weight_stage(numbers[v], *nets.pop(v), feat)
            v = u - SKEW[2]
            if 0 <= v < AHEAD:
                moment_stage(numbers[v], weights.pop(v))
        return carry

    lax.fori_loop(0, tiles // AHEAD, forward, 0)

    degree = [0, 1, 1, 1, 2, 2, 2, 2, 2]
    count = len(degree)
    invariants = []
    for l in range(3):
        total = None
        for m in range(count):
            if degree[m] == l:
                sq = mom_scr[m] * mom_scr[m]
                total = sq if total is None else total + sq
        invariants.append(total)
    upper, lower, back_upper, back_lower = [], [], [], []
    blank = jnp.zeros((channels, channels), f32)
    for l in range(3):
        hi, lo = halves(mix_ref[l])
        upper.append(jnp.concatenate([hi, lo], axis=1))
        back_upper.append(jnp.concatenate([hi, hi], axis=1))
        back_lower.append(jnp.concatenate([lo, blank], axis=1))
    pieces = [halves(value) for value in invariants]
    left = jnp.concatenate([hi for hi, _ in pieces] + [lo for _, lo in pieces], axis=1).astype(bf16)
    mixed = jnp.dot(left, jnp.concatenate(upper + upper, axis=0).astype(bf16), preferred_element_type=f32)
    mixed = mixed[:, 0:channels] + mixed[:, channels:]
    sig = 0.5 * jnp.tanh(0.5 * mixed) + 0.5
    act = mixed * sig
    reads = read_ref[...]
    rhi, rlo = (jnp.broadcast_to(value, (8, channels)) for value in halves(reads))
    rows_of = jnp.concatenate([jnp.concatenate([rhi, rhi], axis=1), jnp.concatenate([rlo, rlo], axis=1)], axis=0)
    sums = nt(rows_of.astype(bf16), jnp.concatenate(halves(act), axis=1).astype(bf16))
    energy_ref[...] = sums[0:1] + sums[8:9]
    dmixed = reads * (sig + act * (1.0 - sig))
    dleft = jnp.concatenate(halves(dmixed), axis=1).astype(bf16)
    dinvs = nt(dleft, jnp.concatenate(back_upper + back_lower, axis=0).astype(bf16))
    for l in range(3):
        upto = (3 + l) * channels
        dinv = (dinvs[:, l * channels : (l + 1) * channels] + dinvs[:, upto : upto + channels]) * (2.0 * factor)
        for m in range(count):
            if degree[m] == l:
                hi, lo = halves(dinv * mom_scr[m])
                g_scr[:, m * groups : (m + 1) * groups, :] = hi.reshape(tiles, groups, channels)
                g_scr[:, (count + m) * groups : (count + m + 1) * groups, :] = lo.reshape(tiles, groups, channels)

    acc_scr[...] = jnp.zeros(acc_scr.shape, f32)
    padded = acc_scr.shape[0] // 6
    chunk_iota = lax.broadcasted_iota(jnp.int32, (padded, tile), 0)
    lane_rows = lax.broadcasted_iota(jnp.int16, (LANES, tile), 0)
    n = count * groups

    def pull_stage(t):
        g = g_scr[t]
        gl = jnp.concatenate(
            [g.astype(bf16), jnp.concatenate([g[0:n], jnp.zeros((n, channels), f32)], axis=0).astype(bf16)], axis=1
        )
        a = jnp.dot(gl, w_scr[t], preferred_element_type=f32)
        b = jnp.dot(gl, dw_scr[t], preferred_element_type=f32)
        return a, b

    def force_stage(t, a, b):
        x, y, z = spread(0, t), spread(1, t), spread(2, t)
        values = harmonics(x, y, z)
        A = [a[m * groups : (m + 1) * groups] + a[n + m * groups : n + (m + 1) * groups] for m in range(count)]
        rad = None
        for m in range(count):
            B = b[m * groups : (m + 1) * groups] + b[n + m * groups : n + (m + 1) * groups]
            rad = B if m == 0 else rad + values[m] * B
        rad = 2.0 * rad
        dx = root_three * A[1] + root_fifteen * (y * A[4] + z * A[7] + x * A[8]) - root_five * (x * A[6]) + x * rad
        dy = root_three * A[2] + root_fifteen * (x * A[4] + z * A[5] - y * A[8]) - root_five * (y * A[6]) + y * rad
        dz = root_three * A[3] + root_fifteen * (y * A[5] + x * A[7]) + (2.0 * root_five) * (z * A[6]) + z * rad
        comps = [jnp.where(mine_mask, v, 0.0) for v in (dx, dy, dz)]
        base = pl.multiple_of(t * groups, groups)
        lane = lax.broadcasted_iota(jnp.int32, (groups, LANES), 1)
        cen = jnp.zeros((groups, LANES), f32)
        for i, v in enumerate(comps):
            cen = jnp.where(lane == i, jnp.sum(v, axis=1, keepdims=True), cen)
        cen_scr[pl.ds(base, groups), :] = cen
        chunk = jnp.right_shift(idx_ref[pl.ds(t, 1), :], LANES.bit_length() - 1)
        hit = jnp.broadcast_to(chunk, (padded, tile)) == chunk_iota
        his, los = [], []
        for v in comps:
            hi, lo = halves(jnp.sum(v, axis=0, keepdims=True))
            his.append(jnp.where(hit, jnp.broadcast_to(hi, (padded, tile)), 0.0))
            los.append(jnp.where(hit, jnp.broadcast_to(lo, (padded, tile)), 0.0))
        left = jnp.concatenate(his + los, axis=0).astype(bf16)
        low = spread_idx(t, 16).astype(jnp.int16) & jnp.int16(LANES - 1)
        low = jnp.concatenate([low] * (LANES // 16), axis=0)
        right = jnp.where(low == lane_rows, jnp.ones((), bf16), jnp.zeros((), bf16))
        return left, right

    def backward(step, carry):
        numbers = [step * BEHIND + u for u in range(BEHIND)]
        pulls, total = {}, None
        for u in range(BEHIND + BACK_SKEW):
            if u < BEHIND:
                pulls[u] = pull_stage(numbers[u])
            v = u - BACK_SKEW
            if 0 <= v < BEHIND:
                left, right = force_stage(numbers[v], *pulls.pop(v))
                part = nt(left, right)
                total = part if total is None else total + part
        acc_scr[...] += total
        return carry

    lax.fori_loop(0, tiles // BEHIND, backward, 0)

    half = 3 * padded
    cen = jnp.concatenate(
        [jnp.transpose(cen_scr[c * LANES : (c + 1) * LANES, :])[0:8] for c in range(own_chunks)], axis=1
    )
    for axis in range(3):
        lo = axis * padded
        sums = acc_scr[lo : lo + padded] + acc_scr[half + lo : half + lo + padded]
        for c in range(own_chunks):
            own_ref[axis : axis + 1, c * LANES : (c + 1) * LANES] = (
                sums[c : c + 1] - cen[axis : axis + 1, c * LANES : (c + 1) * LANES]
            )
        left, right, lower, upper = (
            [sums[own_chunks + k * ghost + j : own_chunks + k * ghost + j + 1] for j in range(ghost)] for k in range(4)
        )
        for back, odd, one, other in (
            (first_back, row_odd, upper, lower),
            (second_back, row_odd, lower, upper),
            (third_back, col_odd, left, right),
            (fourth_back, col_odd, right, left),
        ):
            for j in range(ghost):
                place = places[j] if back is first_back else j
                back[place, axis : axis + 1, :] = jnp.where(odd, one[j], other[j])


def core(split, place, listed, own_pos, own_feat, win, wout, mixing, readout, sides, rows):
    atoms = own_pos.shape[2]
    channels = own_feat.shape[1]
    entries = listed.shape[1]
    tiles, tile = atoms // GROUPS, GROUPS * entries
    ghost = sides[0].shape[0]
    number, hidden = win.shape
    extent = atoms + len(sides) * ghost * LANES
    padded = -(-extent // (LANES * 16)) * 16
    vm = pl.BlockSpec(memory_space=pltpu.VMEM)
    sm = pl.BlockSpec(memory_space=pltpu.SMEM)
    back = jax.ShapeDtypeStruct((ghost, 3, LANES), f32)
    return pl.pallas_call(
        functools.partial(core_kernel, GROUPS, rows),
        out_shape=(
            jax.ShapeDtypeStruct((1, atoms), f32),
            jax.ShapeDtypeStruct((3, atoms), f32),
        ) + (back,) * len(sides),
        in_specs=[sm, sm] + [vm] * (7 + len(sides)),
        out_specs=(vm,) * (2 + len(sides)),
        scratch_shapes=[
            pltpu.VMEM((atoms, entries), jnp.int32),
            pltpu.VMEM((tiles, tile), jnp.int32),
            pltpu.VMEM((3, tiles, tile), f32),
            pltpu.VMEM((2 * number, 2 * hidden), f32),
            pltpu.VMEM((channels, SHUFFLED * LANES), f32),
            pltpu.VMEM((2 * channels, extent - SHUFFLED * LANES), bf16),
            pltpu.VMEM((tiles, 2 * channels, tile), bf16),
            pltpu.VMEM((tiles, 2 * channels, tile), bf16),
            pltpu.VMEM((9, atoms, channels), f32),
            pltpu.VMEM((tiles, 18 * GROUPS, channels), f32),
            pltpu.VMEM((6 * padded, LANES), f32),
            pltpu.VMEM((atoms, LANES), f32),
        ],
        name="core",
    )(split, place, listed, own_pos, own_feat, win, wout, mixing, readout, *sides)


def source_slot(place, ghost, row, split):
    return jnp.where(row == 0, lax.rem(place + split, ghost), place)


def landing_place(slot, ghost, row, split):
    return jnp.where(row == 0, lax.rem(slot - split + ghost, ghost), slot)


def shared_blocks(faces_ref, split, row, col):
    ghost = faces_ref.shape[0]
    row_odd = lax.rem(row, 2)
    col_odd = lax.rem(col, 2)
    return [
        [faces_ref[source_slot(j, ghost, row, split), 3 - row_odd] for j in range(ghost)],
        [faces_ref[j, 2 + row_odd] for j in range(ghost)],
        [faces_ref[j, col_odd] for j in range(ghost)],
        [faces_ref[j, 1 - col_odd] for j in range(ghost)],
    ]


def pack_kernel(rows, split_ref, place_ref, faces_ref, pos_ref, feat_ref, *out_refs):
    channels = feat_ref.shape[1]
    listed = shared_blocks(faces_ref, split_ref[0], lax.rem(place_ref[0], rows), lax.div(place_ref[0], rows))
    for out, blocks in zip(out_refs, listed):
        for j, block in enumerate(blocks):
            lanes = pl.ds(pl.multiple_of(block * LANES, LANES), LANES)
            out[j, 0:channels, :] = feat_ref[0, :, lanes]
            for axis in range(3):
                out[j, channels + axis : channels + axis + 1, :] = pos_ref[axis, :, lanes]
            out[j, channels + 3 :, :] = jnp.zeros((out.shape[1] - channels - 3, LANES), f32)


def pack(split, place, faces, pos, feat, rows):
    ghost, sides = faces.shape
    vm = pl.BlockSpec(memory_space=pltpu.VMEM)
    sm = pl.BlockSpec(memory_space=pltpu.SMEM)
    side = jax.ShapeDtypeStruct((ghost, feat.shape[1] + 8, LANES), f32)
    return pl.pallas_call(
        functools.partial(pack_kernel, rows),
        out_shape=(side,) * sides,
        in_specs=[sm, sm, sm, vm, vm],
        out_specs=(vm,) * sides,
        name="pack",
    )(split, place, faces, pos, feat)


def finish_kernel(rows, split_ref, place_ref, faces_ref, own_ref, *refs):
    forces_ref = refs[-1]
    listed = shared_blocks(faces_ref, split_ref[0], lax.rem(place_ref[0], rows), lax.div(place_ref[0], rows))
    for number in range(own_ref.shape[1] // LANES):
        lanes = slice(number * LANES, (number + 1) * LANES)
        total = own_ref[:, lanes]
        for back, blocks in zip(refs[:-1], listed):
            for j, block in enumerate(blocks):
                total = total + jnp.where(block == number, back[j], 0.0)
        for axis in range(3):
            forces_ref[axis, :, lanes] = -total[axis : axis + 1]


def finish(split, place, faces, own, backs, rows):
    vm = pl.BlockSpec(memory_space=pltpu.VMEM)
    sm = pl.BlockSpec(memory_space=pltpu.SMEM)
    return pl.pallas_call(
        functools.partial(finish_kernel, rows),
        out_shape=jax.ShapeDtypeStruct((3, 1, own.shape[1]), f32),
        in_specs=[sm, sm, sm] + [vm] * (1 + len(backs)),
        out_specs=vm,
        name="finish",
    )(split, place, faces, own, *backs)


def row_swaps(rows, cols, odd, shift=0):
    pairs = []
    for c in range(cols):
        for g in range(rows):
            if g % 2 == odd:
                target = (g + 1, c) if g < rows - 1 else (0, (c + shift) % cols)
            else:
                target = (g - 1, c) if g > 0 else (rows - 1, (c - shift) % cols)
            pairs.append((c * rows + g, target[1] * rows + target[0]))
    return pairs


def column_swaps(rows, cols, odd):
    pairs = []
    for c in range(cols):
        target = (c + 1 if c % 2 == odd else c - 1) % cols
        pairs += [(c * rows + g, target * rows + g) for g in range(rows)]
    return pairs


def exchange(sides, branch, rows, cols, back):
    ghost = sides[0].shape[0]

    def send(value, perm):
        pairs = [(b, a) for a, b in perm] if back else perm
        return lax.ppermute(value, ("flow", "grad"), pairs)

    def case(number):
        shift, split = divmod(number, ghost)

        def crossing(value):
            if split == 0:
                return send(value, row_swaps(rows, cols, 1, shift))
            parts = []
            for part, by in ((value[: ghost - split], shift), (value[ghost - split :], shift + 1)):
                parts.append(send(part, row_swaps(rows, cols, 1, by)))
            return jnp.concatenate(parts, axis=0)

        def route(values):
            first, second, third, fourth = values
            first = crossing(first)
            fourth = send(fourth, column_swaps(rows, cols, 1))
            second = send(second, row_swaps(rows, cols, 0))
            third = send(third, column_swaps(rows, cols, 0))
            return (first, second, third, fourth)

        return route

    return lax.switch(branch, [case(number) for number in range(cols * ghost)], tuple(sides))


def body(
    positions,
    features,
    neighbours,
    face_blocks,
    shear_cells,
    split_block,
    radial_in,
    radial_out,
    mixing,
    readout,
):
    faces = jnp.transpose(face_blocks[0])
    ghost = faces.shape[0]
    rows = lax.axis_size("grad")
    cols = lax.axis_size("flow")
    place = lax.axis_index(("flow", "grad")).astype(jnp.int32).reshape(1)
    branch = shear_cells[0] * ghost + split_block[0]
    branch = jnp.where(branch == cols * ghost, 0, branch)

    sides = pack(split_block, place, faces, positions, features, rows)
    sides = exchange(sides, branch, rows, cols, False)
    energy, own, *backs = core(
        split_block, place, neighbours, positions, features, radial_in, radial_out, mixing, readout.reshape(1, -1), sides, rows
    )
    backs = exchange(backs, branch, rows, cols, True)
    forces = finish(split_block, place, faces, own, backs, rows)
    return (energy, forces)


def solution(mesh):
    in_specs = (
        P(None, "grad", "flow"),
        P("grad", None, "flow"),
        P("grad", None, "flow"),
        P("grad", None, "flow"),
        P(),
        P(),
        P(),
        P(),
        P(),
        P(),
    )
    out_specs = (P("grad", "flow"), P(None, "grad", "flow"))
    return jax.shard_map(body, mesh=mesh, in_specs=in_specs, out_specs=out_specs, check_vma=False)
```
